32 devices in a mesh: dp: 16 (over z, x, core), seq: 2 (over y).
Axes of the slice: x: 2, y: 2, z: 4, core: 2. Of those that a mesh axis runs over, the one named last changes fastest.
Arguments:
- inputs: bfloat16 [32, 1024, 768], P('dp', 'seq'), may hold values from -6 to 6
- cluster_ids: int32 [32, 12, 1024], P('dp', None, 'seq'), may hold values from 0 to 99, as said below
- masked: int32 [32, 1024], P('dp', 'seq'), may hold values from 0 to 1, as said below
- cotangent: bfloat16 [32, 1024, 768], P('dp', 'seq'), may hold values from -6 to 6
- w_query: bfloat16 [768, 768], replicated, may hold values from -1.5 to 1.5
- w_key: bfloat16 [768, 768], replicated, may hold values from -0.21875 to 0.21875
- w_value: bfloat16 [768, 768], replicated, may hold values from -0.21875 to 0.21875
- w_out: bfloat16 [768, 768], replicated, may hold values from -1 to 1
- w_up: bfloat16 [768, 3072], replicated, may hold values from -0.21875 to 0.21875
- w_down: bfloat16 [3072, 768], replicated, may hold values from -0.109375 to 0.109375
- bias_query: bfloat16 [768], replicated, may hold values from -6 to 6
- bias_value: bfloat16 [768], replicated, may hold values from -4 to 4
- bias_out: bfloat16 [768], replicated, may hold values from -4 to 4
- bias_up: bfloat16 [3072], replicated, may hold values from -4 to 4
- bias_down: bfloat16 [768], replicated, may hold values from -4 to 4
- gain_attn: bfloat16 [768], replicated, may hold values from 0.5 to 1.5
- shift_attn: bfloat16 [768], replicated, may hold values from -1.5 to 1.5
- gain_ffn: bfloat16 [768], replicated, may hold values from 0.5 to 1.5
- shift_ffn: bfloat16 [768], replicated, may hold values from -1.5 to 1.5
Outputs:
- block_out: bfloat16 [32, 1024, 768], P('dp', 'seq')
- grad_input: bfloat16 [32, 1024, 768], P('dp', 'seq')
- grad_w_query: float32 [768, 768], replicated
- grad_w_key: float32 [768, 768], replicated
- grad_w_value: float32 [768, 768], replicated
- grad_w_out: float32 [768, 768], replicated
- grad_w_up: float32 [768, 3072], replicated
- grad_w_down: float32 [3072, 768], replicated
- grad_bias_query: float32 [768], replicated
- grad_bias_value: float32 [768], replicated
- grad_bias_out: float32 [768], replicated
- grad_bias_up: float32 [3072], replicated
- grad_bias_down: float32 [768], replicated
- grad_gain_attn: float32 [768], replicated
- grad_shift_attn: float32 [768], replicated
- grad_gain_ffn: float32 [768], replicated
- grad_shift_ffn: float32 [768], replicated
The draws below stay inside these ranges and needn't reach their ends.
Inputs may be any that keep to these rules, and one draw needn't show every extreme that they name: `cluster_ids`: every cluster of every head has at least one token in every sequence. In every sequence, each aligned block of 512 tokens (the tokens that one device holds) has 25 to 128 masked positions, and some block of every sequence has exactly 128.
All inputs are finite; a program needn't handle non-finite values.
Results may differ from the reference program's by a relative error of at most 0.015.
The reference program's roundings to bfloat16 on the way count: a program that leaves them out, or rounds other values in their place, can miss the bound.
Values may be sent and summed in bfloat16 or wider, within the bound.
No kernel may reach another device: no remote copies, remote signals or barrier semaphores. Data moves between devices by JAX's collectives and lax.ppermute only.
A program may use at most 256 MiB of HBM per device.

```python
import jax
import jax.numpy as jnp
from jax import lax

D = 768
HEADS = 12
HDIM = 64
FF = 3072
CLUSTERS = 100
LENGTH = 1024
TOK_SEQ = 512
SEQUENCES = 32
MASK_MOST = 128
MASK_LEAST = 25


def draw_cluster_ids(key, part):
    base_key, order_key = jax.random.split(key)
    base_ids = jax.random.randint(base_key, (SEQUENCES, HEADS, LENGTH), 0, CLUSTERS)
    subkeys = jax.random.split(order_key, SEQUENCES * HEADS)
    shuffled = jax.vmap(lambda subkey: jax.random.permutation(subkey, LENGTH))(subkeys).reshape(SEQUENCES, HEADS, LENGTH)
    return jnp.where(shuffled < CLUSTERS, shuffled, base_ids).astype(jnp.int32)


def draw_masked(key, part):
    blocks = LENGTH // TOK_SEQ
    count_key, forced_key, order_key = jax.random.split(key, 3)
    counts = jax.random.randint(count_key, (SEQUENCES, blocks), MASK_LEAST, MASK_MOST + 1)
    forced = jax.random.randint(forced_key, (SEQUENCES, 1), 0, blocks)
    counts = jnp.where(jnp.arange(blocks)[None, :] == forced, MASK_MOST, counts)
    subkeys = jax.random.split(order_key, SEQUENCES * blocks)
    shuffled = jax.vmap(lambda subkey: jax.random.permutation(subkey, TOK_SEQ))(subkeys).reshape(SEQUENCES, blocks, TOK_SEQ)
    return (shuffled < counts[:, :, None]).astype(jnp.int32).reshape(SEQUENCES, LENGTH)


def levels(own_key, dims, cuts, low, largest):
    level = 1.0
    for position, parts in cuts:
        draws = jax.random.uniform(jax.random.fold_in(jax.random.fold_in(own_key, 6), position), (parts,), jnp.float32, low / len(cuts), largest / len(cuts))
        level = level * jnp.repeat(jnp.exp(draws), dims[position] // parts).reshape((-1,) + (1,) * (len(dims) - 1 - position))
    return level


def gaussian(own_key, extent, width, limit, cuts=(), kind=jnp.bfloat16):
    values = jax.random.normal(own_key, extent, jnp.float32) * width
    if len(cuts) > 0:
        values = levels(own_key, extent, cuts, -0.22, 0.18) * values
    return jnp.clip(values, min=-limit, max=limit).astype(kind)


def setup_inputs(seed: int = 0) -> dict:
    arg_keys = jax.random.split(jax.random.key(seed), 20)
    return {
        "inputs": gaussian(arg_keys[0], (SEQUENCES, LENGTH, D), 1.0, 6.0, ((0, 16), (1, 2))),
        "cluster_ids": draw_cluster_ids(jax.random.fold_in(arg_keys[19], 71), 0),
        "masked": draw_masked(jax.random.fold_in(arg_keys[19], 71), 0),
        "cotangent": gaussian(arg_keys[3], (SEQUENCES, LENGTH, D), 1.0, 6.0, ((0, 16), (1, 2))),
        "w_query": gaussian(arg_keys[4], (D, D), (max(1, D * CLUSTERS // (4 * LENGTH))) ** -0.5, 1.5),
        "w_key": gaussian(arg_keys[5], (D, D), D ** -0.5, 0.21875),
        "w_value": gaussian(arg_keys[6], (D, D), D ** -0.5, 0.21875),
        "w_out": gaussian(arg_keys[7], (D, D), (max(1, D * 50 // LENGTH)) ** -0.5, 1.0),
        "w_up": gaussian(arg_keys[8], (D, FF), D ** -0.5, 0.21875),
        "w_down": gaussian(arg_keys[9], (FF, D), FF ** -0.5, 0.109375),
        "bias_query": gaussian(arg_keys[10], (D,), 1.0, 6.0),
        "bias_value": gaussian(arg_keys[11], (D,), 0.3, 4.0),
        "bias_out": gaussian(arg_keys[12], (D,), 0.3, 4.0),
        "bias_up": gaussian(arg_keys[13], (FF,), 0.3, 4.0),
        "bias_down": gaussian(arg_keys[14], (D,), 0.3, 4.0),
        "gain_attn": jnp.clip(1.0 + 0.1 * jax.random.normal(arg_keys[15], (D,), jnp.float32), 0.5, 1.5).astype(jnp.bfloat16),
        "shift_attn": gaussian(arg_keys[16], (D,), 0.1, 1.5),
        "gain_ffn": jnp.clip(1.0 + 0.1 * jax.random.normal(arg_keys[17], (D,), jnp.float32), 0.5, 1.5).astype(jnp.bfloat16),
        "shift_ffn": gaussian(arg_keys[18], (D,), 0.1, 1.5),
    }


@jax.custom_vjp
def low(v):
    return lax.optimization_barrier(v.astype(jnp.bfloat16)).astype(jnp.float32)

@jax.custom_vjp
def low_back(v):
    return v

def lower_retained(v):
    return (low(v), None)

def low_pass(kept, grad):
    return (grad,)

def back_keep(v):
    return (v, None)

def back_low(kept, grad):
    return (low(grad),)
low.defvjp(lower_retained, low_pass)
low_back.defvjp(back_keep, back_low)
epsilon = 1e-05
exact_mode = lax.Precision.HIGHEST

def layer_norm(tensor_in, gain_in, shift_in):
    center = tensor_in - lax.optimization_barrier(jnp.mean(tensor_in, axis=-1, keepdims=True))
    spread = lax.optimization_barrier(jnp.mean(center * center, axis=-1, keepdims=True))
    return center * lax.rsqrt(spread + epsilon) * gain_in + shift_in

def matmul(left_operand, right_operand):
    return jnp.dot(left_operand, right_operand, precision=exact_mode)

def block_forward(params, tokens_in, sequence_index):
    w_query, w_key, w_value, w_out, w_up, w_down, bias_query, bias_value, bias_out, bias_up, bias_down, gain_attn, shift_attn, gain_ffn, shift_ffn = params
    length = tokens_in.shape[0]
    normed = low(layer_norm(tokens_in, gain_attn, shift_attn))
    queries = low(low_back(matmul(normed, w_query) + bias_query)).reshape(length, HEADS, HDIM)
    key_rows = low(low_back(matmul(normed, w_key))).reshape(length, HEADS, HDIM)
    value_rows = low(low_back(matmul(normed, w_value) + bias_value)).reshape(length, HEADS, HDIM)
    member = (sequence_index[:, None, :] == jnp.arange(CLUSTERS, dtype=jnp.int32)[None, :, None]).astype(jnp.float32)
    counts = lax.optimization_barrier(jnp.sum(member, axis=2))
    query_sums = jnp.einsum('hcl,lhd->hcd', member, queries, precision=exact_mode)
    centroid = low(low_back(query_sums / counts[:, :, None]))
    attention_scores = low_back(jnp.einsum('hcd,lhd->hcl', centroid, key_rows, precision=exact_mode) * HDIM ** (-0.5))
    row_peak = lax.optimization_barrier(jnp.max(attention_scores, axis=2, keepdims=True))
    norm_log = row_peak + jnp.log(lax.optimization_barrier(jnp.sum(jnp.exp(attention_scores - row_peak), axis=2, keepdims=True)))
    weights = low(jnp.exp(attention_scores - norm_log))
    cent_out = low(low_back(jnp.einsum('hcl,lhd->hcd', weights, value_rows, precision=exact_mode)))
    context = jnp.einsum('hcl,hcd->lhd', member, cent_out, precision=exact_mode).reshape(length, HEADS * HDIM)
    middle = tokens_in + low_back(matmul(context, w_out) + bias_out)
    normed_ffn = low(layer_norm(middle, gain_ffn, shift_ffn))
    upper = low_back(matmul(normed_ffn, w_up) + bias_up)
    hidden = low(jax.nn.gelu(upper, approximate=False))
    return middle + (matmul(hidden, w_down) + bias_down)

def reference(inputs, cluster_ids, masked, cotangent, w_query, w_key, w_value, w_out, w_up, w_down, bias_query, bias_value, bias_out, bias_up, bias_down, gain_attn, shift_attn, gain_ffn, shift_ffn):
    params = tuple((tensor.astype(jnp.float32) for tensor in (w_query, w_key, w_value, w_out, w_up, w_down, bias_query, bias_value, bias_out, bias_up, bias_down, gain_attn, shift_attn, gain_ffn, shift_ffn)))

    def one_sequence(totals, sequence_in):
        seq_tokens, sequence_index, seq_mask, seq_cot = sequence_in

        def forward_fn(weights_in, tokens):
            return block_forward(weights_in, tokens, sequence_index)
        result, pullback = jax.vjp(forward_fn, params, seq_tokens.astype(jnp.float32))
        grad_params, grad_tokens = pullback(seq_cot.astype(jnp.float32) * seq_mask.astype(jnp.float32)[:, None])
        totals = jax.tree.map(lambda former, latter: former + latter, totals, grad_params)
        return (totals, (result.astype(jnp.bfloat16), grad_tokens.astype(jnp.bfloat16)))
    zero_grads = jax.tree.map(jnp.zeros_like, params)
    totals, (outputs, grad_inputs) = lax.scan(one_sequence, zero_grads, (inputs, cluster_ids, masked, cotangent))
    return (outputs, grad_inputs, totals[0], totals[1], totals[2], totals[3], totals[4], totals[5], totals[6], totals[7], totals[8], totals[9], totals[10], totals[11], totals[12], totals[13], totals[14])
```

```python
import functools

import jax
import jax.numpy as jnp
from jax import lax
from jax.experimental import pallas as pl
from jax.experimental.pallas import tpu as pltpu
from jax.sharding import PartitionSpec as P

HEADS = 12
HDIM = 64
CLUSTERS = 100
MASK_MOST = 128
PAIRS = HEADS // 2
LANES = 2 * HDIM
ROWS = 112
SCALE = HDIM**-0.5
EPS = 1e-05
BF = jnp.bfloat16
F32 = jnp.float32

V_BQ, V_BV, V_BO, V_BU, V_BD, V_GA, V_SA, V_GF, V_SF = 0, 1, 2, 3, 7, 8, 9, 10, 11
VEC_ROWS = 16


def dot(a, b):
    return lax.dot_general(a, b, (((1,), (0,)), ((), ())), preferred_element_type=F32)


def dot_nt(a, b):
    return lax.dot_general(a, b, (((1,), (1,)), ((), ())), preferred_element_type=F32)


def dot_tn(a, b):
    return lax.dot_general(a, b, (((0,), (0,)), ((), ())), preferred_element_type=F32)


def norm_parts(rows):
    center = rows - jnp.mean(rows, axis=-1, keepdims=True)
    inverse = lax.rsqrt(jnp.mean(center * center, axis=-1, keepdims=True) + EPS)
    return center * inverse, inverse


def norm_back(incoming, unit, inverse, gain):
    scaled = incoming * gain
    return inverse * (
        scaled
        - jnp.mean(scaled, axis=-1, keepdims=True)
        - unit * jnp.mean(scaled * unit, axis=-1, keepdims=True)
    )


def normal_cdf(upper):
    return 0.5 * (1.0 + lax.erf(upper * (0.5**0.5)))


def lane_of(rows):
    return lax.broadcasted_iota(jnp.int32, (rows, LANES), 1)


def column(slab, index):
    picked = jnp.where(lane_of(slab.shape[0]) == index, slab, 0.0)
    return jnp.sum(picked, axis=1, keepdims=True)


def member_pair(ids, pair):
    tokens = ids.shape[-1]
    rows = lax.broadcasted_iota(jnp.int32, (ROWS, tokens), 0)
    one = [
        jnp.where(rows == ids[0, pl.ds(2 * pair + side, 1), :], 1.0, 0.0).astype(BF)
        for side in range(2)
    ]
    return jnp.concatenate(one, axis=0)


def stack_pair(both):
    left = lane_of(both.shape[0]) < HDIM
    return jnp.concatenate(
        [jnp.where(left, both, 0.0).astype(BF), jnp.where(left, 0.0, both).astype(BF)], axis=0
    )


def unstack_pair(stacked):
    left = lane_of(ROWS) < HDIM
    return jnp.where(left, stacked[:ROWS], stacked[ROWS:])


def pair_lanes(pair):
    return pl.ds(pl.multiple_of(pair * LANES, LANES), LANES)


def whole(shape):
    return pl.BlockSpec(shape, lambda *_: (0,) * len(shape))


def params(mib=56):
    return pltpu.CompilerParams(vmem_limit_bytes=mib * 2**20)


def cost(flops, moved, exps=0):
    return pl.CostEstimate(flops=int(flops), bytes_accessed=int(moved), transcendentals=int(exps))


def project_kernel(
    x_ref, ids_ref, wq_ref, wk_ref, wv_ref, bq_ref, bv_ref, gain_ref, shift_ref,
    normed_ref, key_ref, value_ref, own_ref, message_ref, query_s,
):
    unit, _ = norm_parts(x_ref[0].astype(F32))
    normed = (unit * gain_ref[...].astype(F32) + shift_ref[...].astype(F32)).astype(BF)
    normed_ref[0] = normed
    query_s[...] = (dot(normed, wq_ref[...]) + bq_ref[...].astype(F32)).astype(BF)
    key_ref[0] = dot(normed, wk_ref[...]).astype(BF)
    value_ref[0] = (dot(normed, wv_ref[...]) + bv_ref[...].astype(F32)).astype(BF)
    lane = lane_of(ROWS)
    ones = jnp.ones((normed.shape[0], LANES), BF)

    def step(pair, slab):
        right = jnp.concatenate([query_s[:, pair_lanes(pair)], ones], axis=1)
        sums = dot(member_pair(ids_ref, pair), right)
        own = unstack_pair(sums[:, :LANES])
        own_ref[0, pair] = own
        message_ref[0, pair] = own.astype(BF)
        for side in range(2):
            count = sums[side * ROWS : (side + 1) * ROWS, LANES:]
            low = jnp.minimum(count, 256.0)
            slab = slab + jnp.where(lane == 2 * pair + side, low, 0.0)
            slab = slab + jnp.where(lane == 16 + 2 * pair + side, count - low, 0.0)
        return slab

    slab = lax.fori_loop(0, PAIRS, step, jnp.zeros((ROWS, LANES), F32))
    message_ref[0, PAIRS] = slab.astype(BF)


def project_call(x, ids, wq, wk, wv, bq, bv, gain, shift):
    seqs, tokens, width = x.shape
    rows = pl.BlockSpec((1, tokens, width), lambda s: (s, 0, 0))
    slab = pl.BlockSpec((1, PAIRS, ROWS, LANES), lambda s: (s, 0, 0, 0))
    slab_more = pl.BlockSpec((1, PAIRS + 1, ROWS, LANES), lambda s: (s, 0, 0, 0))
    row_shape = jax.ShapeDtypeStruct(x.shape, BF)
    return pl.pallas_call(
        project_kernel,
        grid=(seqs,),
        in_specs=[rows, pl.BlockSpec((1, HEADS, tokens), lambda s: (s, 0, 0))]
        + [whole((width, width))] * 3
        + [whole((1, width))] * 4,
        out_specs=[rows, rows, rows, slab, slab_more],
        out_shape=[
            row_shape, row_shape, row_shape,
            jax.ShapeDtypeStruct((seqs, PAIRS, ROWS, LANES), F32),
            jax.ShapeDtypeStruct((seqs, PAIRS + 1, ROWS, LANES), BF),
        ],
        scratch_shapes=[pltpu.VMEM((tokens, width), BF)],
        compiler_params=params(),
        cost_estimate=cost(6 * seqs * tokens * width * width, 6 * width * width + 8 * x.size),
        name="project",
    )(x, ids, wq, wk, wv, bq, bv, gain, shift)


def attend_kernel(
    own_ref, message_ref, got_ref, key_ref, value_ref,
    cent_ref, count_ref, out_ref, lse_ref, send_ref,
):
    peers = got_ref.shape[0]
    lane = lane_of(ROWS)
    slab = message_ref[0, PAIRS].astype(F32)
    for peer in range(peers):
        slab = slab + got_ref[peer, 0, PAIRS].astype(F32)
    count = jnp.maximum(slab + pltpu.roll(slab, LANES - 16, 1), 1.0)
    count_ref[0] = count

    def step(pair, lses):
        total = own_ref[0, pair]
        for peer in range(peers):
            total = total + got_ref[peer, 0, pair].astype(F32)
        divisor = jnp.where(lane < HDIM, column(count, 2 * pair), column(count, 2 * pair + 1))
        cent = (total / divisor).astype(BF)
        cent_ref[0, pair] = cent
        scores = dot_nt(stack_pair(cent.astype(F32)), key_ref[0, :, pair_lanes(pair)]) * SCALE
        peak = jnp.max(scores, axis=1, keepdims=True)
        raised = jnp.exp(scores - peak)
        mass = jnp.sum(raised, axis=1, keepdims=True)
        mixed = unstack_pair(dot(raised.astype(BF), value_ref[0, :, pair_lanes(pair)]) / mass)
        out_ref[0, pair] = mixed
        send_ref[0, pair] = mixed.astype(BF)
        lse = peak + jnp.log(mass)
        lses = lses + jnp.where(lane == 2 * pair, lse[:ROWS], 0.0)
        return lses + jnp.where(lane == 2 * pair + 1, lse[ROWS:], 0.0)

    lses = lax.fori_loop(0, PAIRS, step, jnp.zeros((ROWS, LANES), F32))
    lse_ref[0] = lses
    high = lses.astype(BF).astype(F32)
    rest = lses - high
    middle = rest.astype(BF).astype(F32)
    low = (rest - middle).astype(BF).astype(F32)
    send_ref[0, PAIRS] = (high + pltpu.roll(middle, 16, 1) + pltpu.roll(low, 32, 1)).astype(BF)


def attend_call(own, message, got, keys, values):
    seqs, tokens, width = keys.shape
    peers = got.shape[0]
    rows = pl.BlockSpec((1, tokens, width), lambda s: (s, 0, 0))
    slab = pl.BlockSpec((1, PAIRS, ROWS, LANES), lambda s: (s, 0, 0, 0))
    slab_more = pl.BlockSpec((1, PAIRS + 1, ROWS, LANES), lambda s: (s, 0, 0, 0))
    one = pl.BlockSpec((1, ROWS, LANES), lambda s: (s, 0, 0))
    full = (seqs, PAIRS, ROWS, LANES)
    return pl.pallas_call(
        attend_kernel,
        grid=(seqs,),
        in_specs=[
            slab, slab_more,
            pl.BlockSpec((peers, 1, PAIRS + 1, ROWS, LANES), lambda s: (0, s, 0, 0, 0)),
            rows, rows,
        ],
        out_specs=[slab, one, slab, one, slab_more],
        out_shape=[
            jax.ShapeDtypeStruct(full, BF),
            jax.ShapeDtypeStruct((seqs, ROWS, LANES), F32),
            jax.ShapeDtypeStruct(full, F32),
            jax.ShapeDtypeStruct((seqs, ROWS, LANES), F32),
            jax.ShapeDtypeStruct((seqs, PAIRS + 1, ROWS, LANES), BF),
        ],
        compiler_params=params(),
        cost_estimate=cost(8 * seqs * tokens * width * ROWS, 8 * keys.size, keys.size * 3),
        name="attend",
    )(own, message, got, keys, values)


def masked_kernel(
    core_ref, x_ref, cot_ref, sel_ref, ids_ref, out_ref, lse_ref, got_ref,
    wo_ref, wu_ref, wd_ref, bo_ref, bu_ref, gain_ref, shift_ref,
    ctx_ref, merged_ref, lse_all_ref, keep_ref, send_ref, ctx_m_ref, attn_m_ref, mid_m_ref,
    own_ref, message_ref, vec_ref,
    x_s, low_s, back_s,
):
    seqs, tokens, width = x_ref.shape
    peers = got_ref.shape[0]
    ff_block = width
    ff_blocks = wu_ref.shape[1] // ff_block
    half_blocks = ff_blocks // 2
    tail = 2 * half_blocks * ff_block
    lane = lane_of(ROWS)
    core = core_ref[0]
    vec_ref[...] = jnp.zeros_like(vec_ref)

    for s in range(seqs):
        rows = pl.ds(s * MASK_MOST, MASK_MOST)
        lses = [lse_ref[s]]
        for peer in range(peers):
            slab = got_ref[peer, s, PAIRS].astype(F32)
            lses.append(
                slab + pltpu.roll(slab, LANES - 16, 1) + pltpu.roll(slab, LANES - 32, 1)
            )
        peak = functools.reduce(jnp.maximum, lses)
        merged = peak + jnp.log(sum(jnp.exp(item - peak) for item in lses))
        lse_all_ref[s] = merged
        shares = [jnp.exp(item - merged) for item in lses]

        def gather(pair, carry, s=s, shares=shares):
            total = jnp.zeros((ROWS, LANES), F32)
            for index, share in enumerate(shares):
                part = out_ref[s, pair] if index == 0 else got_ref[index - 1, s, pair].astype(F32)
                weight = jnp.where(
                    lane < HDIM, column(share, 2 * pair), column(share, 2 * pair + 1)
                )
                total = total + weight * part
            merged_ref[s, pair] = total
            member = member_pair(ids_ref.at[pl.ds(s, 1)], pair)
            ctx_ref[s, :, pair_lanes(pair)] = dot_tn(member, stack_pair(total)).astype(BF)
            return carry

        lax.fori_loop(0, PAIRS, gather, 0)
        slots = lax.broadcasted_iota(jnp.int32, (MASK_MOST, tokens), 0)
        pick = jnp.where(slots == sel_ref[s], 1.0, 0.0).astype(BF)
        ctx_m_ref[rows, :] = dot(pick, ctx_ref[s]).astype(BF)
        x_s[rows, :] = dot(pick, x_ref[s])
        low_cot = dot(pick, cot_ref[s]).astype(BF)
        keep_ref[rows, tail : tail + width] = low_cot
        send_ref[rows, tail : tail + width] = low_cot

    middle = x_s[...] + (dot(ctx_m_ref[...], wo_ref[...]) + bo_ref[...].astype(F32))
    unit, inverse = norm_parts(middle)
    gain = gain_ref[...].astype(F32)
    low = (unit * gain + shift_ref[...].astype(F32)).astype(BF)
    low_s[...] = low
    keep_ref[:, tail + width :] = low
    send_ref[:, tail + width :] = low
    back_s[...] = jnp.zeros_like(back_s)

    def feed(block, carry):
        lanes = pl.ds(pl.multiple_of(block * ff_block, ff_block), ff_block)
        upper = dot(low_s[...], wu_ref[:, lanes]) + bu_ref[:, lanes].astype(F32)
        cdf = normal_cdf(upper)
        hidden = (upper * cdf).astype(BF)
        slope = cdf + upper * (jnp.exp(-0.5 * upper * upper) * 0.3989422804014327)
        grad_y = keep_ref[:, tail : tail + width]
        grad_upper = (dot_nt(grad_y, wd_ref[lanes, :]) * slope).astype(BF)
        back_s[...] += dot_nt(grad_upper, wu_ref[:, lanes])
        vec_ref[pl.ds(V_BU + block, 1), :] = jnp.sum(
            grad_upper.astype(F32), axis=0, keepdims=True
        )
        half = block // half_blocks
        inner = block - half * half_blocks
        first = pl.ds(pl.multiple_of(inner * ff_block, ff_block), ff_block)
        second = pl.ds(
            pl.multiple_of(inner * ff_block + half_blocks * ff_block, ff_block), ff_block
        )

        @pl.when(half == core)
        def _():
            keep_ref[:, first] = hidden
            keep_ref[:, second] = grad_upper

        @pl.when(half != core)
        def _():
            send_ref[:, first] = hidden
            send_ref[:, second] = grad_upper

        return carry

    lax.fori_loop(0, ff_blocks, feed, 0)
    middle = x_s[...] + (dot(ctx_m_ref[...], wo_ref[...]) + bo_ref[...].astype(F32))
    unit, inverse = norm_parts(middle)
    incoming = back_s[...]
    grad_y = keep_ref[:, tail : tail + width].astype(F32)
    grad_middle = grad_y + norm_back(incoming, unit, inverse, gain)
    mid_m_ref[...] = grad_middle
    grad_attn = grad_middle.astype(BF)
    attn_m_ref[...] = grad_attn
    vec_ref[V_BD : V_BD + 1, :] = jnp.sum(grad_y, axis=0, keepdims=True)
    vec_ref[V_BO : V_BO + 1, :] = jnp.sum(grad_attn.astype(F32), axis=0, keepdims=True)
    vec_ref[V_GF : V_GF + 1, :] = jnp.sum(incoming * unit, axis=0, keepdims=True)
    vec_ref[V_SF : V_SF + 1, :] = jnp.sum(incoming, axis=0, keepdims=True)
    back_s[...] = dot_nt(grad_attn, wo_ref[...])
    for s in range(seqs):
        slots = lax.broadcasted_iota(jnp.int32, (MASK_MOST, tokens), 0)
        pick = jnp.where(slots == sel_ref[s], 1.0, 0.0).astype(BF)

        def scatter(pair, carry, s=s, pick=pick):
            member = dot_nt(member_pair(ids_ref.at[pl.ds(s, 1)], pair), pick).astype(BF)
            rows = back_s[s * MASK_MOST : (s + 1) * MASK_MOST, pair_lanes(pair)]
            high = rows.astype(BF)
            rest = (rows - high.astype(F32)).astype(BF)
            own = unstack_pair(dot(member, high) + dot(member, rest))
            own_ref[s, pair] = own
            message_ref[s, pair] = own.astype(BF)
            return carry

        lax.fori_loop(0, PAIRS, scatter, 0)


def masked_call(core, x, cot, sel, ids, out, lse, got, wo, wu, wd, bo, bu, gain, shift):
    seqs, tokens, width = x.shape
    picked = seqs * MASK_MOST
    ff = wu.shape[1]
    wide = ff + 2 * width
    slab = (seqs, PAIRS, ROWS, LANES)
    vmem = pl.BlockSpec(memory_space=pltpu.VMEM)
    return pl.pallas_call(
        masked_kernel,
        in_specs=[pl.BlockSpec(memory_space=pltpu.SMEM)] + [vmem] * 14,
        out_specs=[vmem] * 11,
        out_shape=[
            jax.ShapeDtypeStruct(x.shape, BF),
            jax.ShapeDtypeStruct(slab, F32),
            jax.ShapeDtypeStruct((seqs, ROWS, LANES), F32),
            jax.ShapeDtypeStruct((picked, wide), BF),
            jax.ShapeDtypeStruct((picked, wide), BF),
            jax.ShapeDtypeStruct((picked, width), BF),
            jax.ShapeDtypeStruct((picked, width), BF),
            jax.ShapeDtypeStruct((picked, width), F32),
            jax.ShapeDtypeStruct(slab, F32),
            jax.ShapeDtypeStruct(slab, BF),
            jax.ShapeDtypeStruct((VEC_ROWS, width), F32),
        ],
        scratch_shapes=[
            pltpu.VMEM((picked, width), F32),
            pltpu.VMEM((picked, width), BF),
            pltpu.VMEM((picked, width), F32),
        ],
        compiler_params=params(),
        cost_estimate=cost(
            6 * picked * width * ff + 6 * picked * width * width, 4 * width * ff + 12 * x.size
        ),
        name="masked_rows",
    )(core, x, cot, sel, ids, out, lse, got, wo, wu, wd, bo, bu, gain, shift)


def forward_kernel(
    x_ref, ctx_ref, wo_ref, wu_ref, wd_ref, bo_ref, bu_ref, bd_ref, gain_ref, shift_ref, y_ref,
    low_s, total_s,
):
    middle = x_ref[...].astype(F32) + (dot(ctx_ref[...], wo_ref[...]) + bo_ref[...].astype(F32))
    unit, _ = norm_parts(middle)
    low_s[...] = (unit * gain_ref[...].astype(F32) + shift_ref[...].astype(F32)).astype(BF)
    total_s[...] = middle + bd_ref[...].astype(F32)
    block = x_ref.shape[1]

    def feed(index, carry):
        lanes = pl.ds(pl.multiple_of(index * block, block), block)
        upper = dot(low_s[...], wu_ref[:, lanes]) + bu_ref[:, lanes].astype(F32)
        hidden = (upper * normal_cdf(upper)).astype(BF)
        total_s[...] += dot(hidden, wd_ref[lanes, :])
        return carry

    lax.fori_loop(0, wu_ref.shape[1] // block, feed, 0)
    y_ref[...] = total_s[...].astype(BF)


def forward_call(x, ctx, wo, wu, wd, bo, bu, bd, gain, shift, block=256):
    seqs, tokens, width = x.shape
    ff = wu.shape[1]
    total = seqs * tokens
    rows = pl.BlockSpec((block, width), lambda i: (i, 0))
    y = pl.pallas_call(
        forward_kernel,
        grid=(total // block,),
        in_specs=[rows, rows, whole((width, width)), whole((width, ff)), whole((ff, width))]
        + [whole((1, width)), whole((1, ff))]
        + [whole((1, width))] * 3,
        out_specs=rows,
        out_shape=jax.ShapeDtypeStruct((total, width), BF),
        scratch_shapes=[pltpu.VMEM((block, width), BF), pltpu.VMEM((block, width), F32)],
        compiler_params=params(),
        cost_estimate=cost(4 * total * width * ff, 4 * width * ff + 6 * x.size),
        name="forward_rows",
    )(x.reshape(total, width), ctx.reshape(total, width), wo, wu, wd, bo, bu, bd, gain, shift)
    return y.reshape(x.shape)


def attend_back_kernel(
    cent_ref, lse_ref, merged_ref, own_ref, got_ref, key_ref, value_ref,
    grad_key_ref, grad_value_ref, part_ref, send_ref,
):
    peers = got_ref.shape[0]
    lane = lane_of(ROWS)
    lses = lse_ref[0]

    def step(pair, carry):
        total = own_ref[0, pair]
        for peer in range(peers):
            total = total + got_ref[peer, 0, pair].astype(F32)
        grad_cent = total.astype(BF).astype(F32)
        product = grad_cent * merged_ref[0, pair]
        delta = jnp.concatenate(
            [
                jnp.sum(jnp.where(lane < HDIM, product, 0.0), axis=1, keepdims=True),
                jnp.sum(jnp.where(lane < HDIM, 0.0, product), axis=1, keepdims=True),
            ],
            axis=0,
        )
        lse = jnp.concatenate([column(lses, 2 * pair), column(lses, 2 * pair + 1)], axis=0)
        cents = stack_pair(cent_ref[0, pair].astype(F32))
        grads = stack_pair(grad_cent)
        keys = key_ref[0, :, pair_lanes(pair)]
        weights = jnp.exp(dot_nt(cents, keys) * SCALE - lse)
        grad_weights = dot_nt(grads, value_ref[0, :, pair_lanes(pair)])
        grad_scores = (weights * (grad_weights - delta)).astype(BF)
        grad_key_ref[0, :, pair_lanes(pair)] = (dot_tn(grad_scores, cents) * SCALE).astype(BF)
        grad_value_ref[0, :, pair_lanes(pair)] = dot_tn(weights.astype(BF), grads).astype(BF)
        part = unstack_pair(dot(grad_scores, keys))
        part_ref[0, pair] = part
        send_ref[0, pair] = part.astype(BF)
        return carry

    lax.fori_loop(0, PAIRS, step, 0)


def attend_back_call(cent, lse, merged, own, got, keys, values):
    seqs, tokens, width = keys.shape
    peers = got.shape[0]
    rows = pl.BlockSpec((1, tokens, width), lambda s: (s, 0, 0))
    slab = pl.BlockSpec((1, PAIRS, ROWS, LANES), lambda s: (s, 0, 0, 0))
    one = pl.BlockSpec((1, ROWS, LANES), lambda s: (s, 0, 0))
    full = (seqs, PAIRS, ROWS, LANES)
    return pl.pallas_call(
        attend_back_kernel,
        grid=(seqs,),
        in_specs=[
            slab, one, slab, slab,
            pl.BlockSpec((peers, 1, PAIRS, ROWS, LANES), lambda s: (0, s, 0, 0, 0)),
            rows, rows,
        ],
        out_specs=[rows, rows, slab, slab],
        out_shape=[
            jax.ShapeDtypeStruct(keys.shape, BF),
            jax.ShapeDtypeStruct(keys.shape, BF),
            jax.ShapeDtypeStruct(full, F32),
            jax.ShapeDtypeStruct(full, BF),
        ],
        compiler_params=params(),
        cost_estimate=cost(20 * seqs * tokens * width * ROWS, 8 * keys.size, keys.size * 2),
        name="attend_back",
    )(cent, lse, merged, own, got, keys, values)


def back_kv_kernel(gk_ref, gv_ref, wk_ref, wv_ref, g_ref):
    g_ref[0] = dot_nt(gk_ref[0], wk_ref[...]) + dot_nt(gv_ref[0], wv_ref[...])


def back_kv_call(gk, gv, wk, wv):
    seqs, tokens, width = gk.shape
    rows = pl.BlockSpec((1, tokens, width), lambda s: (s, 0, 0))
    return pl.pallas_call(
        back_kv_kernel,
        grid=(seqs,),
        in_specs=[rows, rows] + [whole((width, width))] * 2,
        out_specs=rows,
        out_shape=jax.ShapeDtypeStruct(gk.shape, F32),
        compiler_params=params(),
        cost_estimate=cost(4 * gk.size * width, 8 * gk.size),
        name="back_kv",
    )(gk, gv, wk, wv)


def back_input_kernel(
    part_ref, got_ref, count_ref, ids_ref, g_ref, gv_ref, x_ref, wq_ref, gain_ref, mid_ref, sel_ref,
    vec_in_ref, gq_ref, gx_ref, vec_ref,
):
    peers = got_ref.shape[0]
    lane = lane_of(ROWS)
    count = count_ref[0]

    @pl.when(pl.program_id(0) == 0)
    def _():
        vec_ref[...] = vec_in_ref[...]

    def step(pair, carry):
        total = part_ref[0, pair]
        for peer in range(peers):
            total = total + got_ref[peer, 0, pair].astype(F32)
        grad_cent = (total * SCALE).astype(BF).astype(F32)
        divisor = jnp.where(lane < HDIM, column(count, 2 * pair), column(count, 2 * pair + 1))
        shared = stack_pair(grad_cent / divisor)
        gq_ref[0, :, pair_lanes(pair)] = dot_tn(member_pair(ids_ref, pair), shared).astype(BF)
        return carry

    lax.fori_loop(0, PAIRS, step, 0)
    grad_query = gq_ref[0]
    incoming = g_ref[0] + dot_nt(grad_query, wq_ref[...])
    unit, inverse = norm_parts(x_ref[0].astype(F32))
    grad = norm_back(incoming, unit, inverse, gain_ref[...].astype(F32))
    slots = lax.broadcasted_iota(jnp.int32, (MASK_MOST, x_ref.shape[1]), 0)
    pick = jnp.where(slots == sel_ref[0], 1.0, 0.0).astype(BF)
    middle = mid_ref[...]
    high = middle.astype(BF)
    rest = (middle - high.astype(F32)).astype(BF)
    grad = grad + (dot_tn(pick, high) + dot_tn(pick, rest))
    gx_ref[0] = grad.astype(BF)
    vec_ref[V_BQ : V_BQ + 1, :] += jnp.sum(grad_query.astype(F32), axis=0, keepdims=True)
    vec_ref[V_BV : V_BV + 1, :] += jnp.sum(gv_ref[0].astype(F32), axis=0, keepdims=True)
    vec_ref[V_GA : V_GA + 1, :] += jnp.sum(incoming * unit, axis=0, keepdims=True)
    vec_ref[V_SA : V_SA + 1, :] += jnp.sum(incoming, axis=0, keepdims=True)


def back_input_call(part, got, count, ids, g, gv, x, wq, gain, mid, sel, vec):
    seqs, tokens, width = x.shape
    peers = got.shape[0]
    rows = pl.BlockSpec((1, tokens, width), lambda s: (s, 0, 0))
    slab = pl.BlockSpec((1, PAIRS, ROWS, LANES), lambda s: (s, 0, 0, 0))
    return pl.pallas_call(
        back_input_kernel,
        grid=(seqs,),
        in_specs=[
            slab,
            pl.BlockSpec((peers, 1, PAIRS, ROWS, LANES), lambda s: (0, s, 0, 0, 0)),
            pl.BlockSpec((1, ROWS, LANES), lambda s: (s, 0, 0)),
            pl.BlockSpec((1, HEADS, tokens), lambda s: (s, 0, 0)),
            rows, rows, rows,
            whole((width, width)),
            whole((1, width)),
            pl.BlockSpec((MASK_MOST, width), lambda s: (s, 0)),
            pl.BlockSpec((1, 1, tokens), lambda s: (s, 0, 0)),
            whole((VEC_ROWS, width)),
        ],
        out_specs=[rows, rows, whole((VEC_ROWS, width))],
        out_shape=[
            jax.ShapeDtypeStruct(x.shape, BF),
            jax.ShapeDtypeStruct(x.shape, BF),
            jax.ShapeDtypeStruct((VEC_ROWS, width), F32),
        ],
        compiler_params=params(),
        cost_estimate=cost(4 * x.size * width, 14 * x.size),
        name="back_input",
    )(part, got, count, ids, g, gv, x, wq, gain, mid, sel, vec)


def store_chunks(out_ref, product, rank, per_group):
    size = product.shape[0] // per_group
    for index in range(per_group):
        out_ref[index ^ (rank & (per_group - 1))] = product[
            index * size : (index + 1) * size
        ].astype(BF)


def ffn_grad_kernel(rank_ref, left_ref, left_got_ref, right_ref, right_got_ref, out_ref):
    product = dot_tn(left_ref[...], right_ref[...]) + dot_tn(left_got_ref[...], right_got_ref[...])
    store_chunks(out_ref, product, rank_ref[0], 4)


def ffn_grad_call(rank, keep, got, ff, width, down):
    picked = keep.shape[0]
    half = ff // 2
    rows = half // 4
    if down:
        left = pl.BlockSpec((picked, rows), lambda g, r: (0, g))
        right = pl.BlockSpec((picked, width), lambda g, r: (0, ff // width))
    else:
        left = pl.BlockSpec((picked, rows), lambda g, r: (0, (ff + width) // rows + (g & 1)))
        right = pl.BlockSpec((picked, width), lambda g, r: (0, half // width + g // 2))
    return pl.pallas_call(
        ffn_grad_kernel,
        grid_spec=pltpu.PrefetchScalarGridSpec(
            num_scalar_prefetch=1,
            grid=(4,),
            in_specs=[left, left, right, right],
            out_specs=pl.BlockSpec((4, rows // 4, width), lambda g, r: (g ^ (r[0] // 4), 0, 0)),
        ),
        out_shape=jax.ShapeDtypeStruct((16, rows // 4, width), BF),
        compiler_params=params(),
        cost_estimate=cost(4 * picked * half * width, 4 * picked * half + 2 * half * width),
        name="grad_down" if down else "grad_up",
    )(rank, keep, got, keep, got)


def pair_grad_kernel(rank_ref, a_ref, ga_ref, b_ref, gb_ref, out_ref):
    group = pl.program_id(0)

    @pl.when(group < 2)
    def _():
        store_chunks(out_ref, dot_tn(a_ref[...], ga_ref[...]), rank_ref[0], 8)

    @pl.when(group >= 2)
    def _():
        store_chunks(out_ref, dot_tn(b_ref[...], gb_ref[...]), rank_ref[0], 8)


def pair_grad_call(rank, a, ga, b, gb, name):
    width = ga.shape[1]
    rows = width // 2
    return pl.pallas_call(
        pair_grad_kernel,
        grid_spec=pltpu.PrefetchScalarGridSpec(
            num_scalar_prefetch=1,
            grid=(4,),
            in_specs=[
                pl.BlockSpec((a.shape[0], rows), lambda g, r: (0, jnp.minimum(g, 1))),
                whole(ga.shape),
                pl.BlockSpec((b.shape[0], rows), lambda g, r: (0, jnp.maximum(g - 2, 0))),
                whole(gb.shape),
            ],
            out_specs=pl.BlockSpec((8, rows // 8, width), lambda g, r: (g ^ (r[0] // 8), 0, 0)),
        ),
        out_shape=jax.ShapeDtypeStruct((32, rows // 8, width), BF),
        compiler_params=params(),
        cost_estimate=cost(2 * (a.size + b.size) * width, 2 * (a.size + b.size + ga.size + gb.size)),
        name=name,
    )(rank, a, ga, b, gb)


def place_ffn_kernel(rank_ref, own_ref, got_ref, out_ref):
    group = pl.program_id(0)
    rank = rank_ref[0]
    size = own_ref.shape[1]
    from_own = group // 4 == rank // 16

    def write(source):
        for index in range(4):
            out_ref[index * size : (index + 1) * size, :] = source[index ^ (rank & 3)].astype(F32)

    @pl.when(from_own)
    def _():
        write(own_ref)

    @pl.when(jnp.logical_not(from_own))
    def _():
        write(got_ref)


def place_ffn_call(rank, own, got, down):
    _, size, width = own.shape
    rows = 4 * size
    source = pl.BlockSpec((4, size, width), lambda g, r: ((g ^ (r[0] // 4)) & 3, 0, 0))
    if down:
        shape = (32 * size, width)
        target = pl.BlockSpec((rows, width), lambda g, r: (g, 0))
    else:
        shape = (8 * size, 4 * width)
        target = pl.BlockSpec((rows, width), lambda g, r: (g & 1, g // 2))
    return pl.pallas_call(
        place_ffn_kernel,
        grid_spec=pltpu.PrefetchScalarGridSpec(
            num_scalar_prefetch=1, grid=(8,), in_specs=[source, source], out_specs=target
        ),
        out_shape=jax.ShapeDtypeStruct(shape, F32),
        compiler_params=params(),
        cost_estimate=cost(0, 8 * own.size + 8 * own.size),
        name="place_down" if down else "place_up",
    )(rank, own, got)


def place_pair_kernel(rank_ref, own_ref, got_ref, a_ref, b_ref):
    group = pl.program_id(0)
    rank = rank_ref[0]
    size = own_ref.shape[1]
    from_own = group // 2 == rank // 16

    def write(source, out_ref):
        for index in range(8):
            out_ref[index * size : (index + 1) * size, :] = source[index ^ (rank & 7)].astype(F32)

    for matrix, out_ref in enumerate((a_ref, b_ref)):
        here = group // 2 == matrix

        @pl.when(jnp.logical_and(here, from_own))
        def _(out_ref=out_ref):
            write(own_ref, out_ref)

        @pl.when(jnp.logical_and(here, jnp.logical_not(from_own)))
        def _(out_ref=out_ref):
            write(got_ref, out_ref)


def place_pair_call(rank, own, got, name):
    _, size, width = own.shape
    rows = 8 * size
    source = pl.BlockSpec((8, size, width), lambda g, r: ((g ^ (r[0] // 8)) & 1, 0, 0))
    shape = jax.ShapeDtypeStruct((2 * rows, width), F32)
    return pl.pallas_call(
        place_pair_kernel,
        grid_spec=pltpu.PrefetchScalarGridSpec(
            num_scalar_prefetch=1,
            grid=(4,),
            in_specs=[source, source],
            out_specs=[
                pl.BlockSpec((rows, width), lambda g, r: (jnp.minimum(g, 1), 0)),
                pl.BlockSpec((rows, width), lambda g, r: (jnp.maximum(g - 2, 0), 0)),
            ],
        ),
        out_shape=[shape, shape],
        compiler_params=params(),
        cost_estimate=cost(0, 16 * own.size),
        name=name,
    )(rank, own, got)


def swap(rows, stage):
    axis, bit = stage
    return lax.ppermute(rows, axis, [(i, i ^ bit) for i in range(lax.axis_size(axis))])


def stage_lists():
    def bits(axis):
        size = lax.axis_size(axis)
        return [(axis, 1 << k) for k in range(size.bit_length() - 1)]

    dp, seq = bits("dp"), bits("seq")
    rest = dp[2:] + seq[1:]
    return [dp[0], dp[1], seq[0]] + rest, [dp[0], seq[0], dp[1]] + rest


def rank_of(stages):
    rank = jnp.int32(0)
    for place, (axis, bit) in enumerate(stages[:5]):
        mine = (lax.axis_index(axis) // bit) & 1
        rank = rank + mine * (16 >> place)
    return rank.astype(jnp.int32)


def added(a, b):
    return (a.astype(F32) + b.astype(F32)).astype(BF)


def scatter_sums(chunks, stages, first):
    for place in range(first, 5):
        half = chunks.shape[0] // 2
        chunks = added(chunks[:half], swap(chunks[half:], stages[place]))
    for stage in stages[5:]:
        chunks = added(chunks, swap(chunks, stage))
    return chunks


def scatter_sums_with(chunks, extra, stages):
    for place in range(5):
        half = chunks.shape[0] // 2
        got = swap(jnp.concatenate([chunks[half:], extra], axis=0), stages[place])
        chunks = added(chunks[:half], got[:half])
        extra = added(extra, got[half:])
    for stage in stages[5:]:
        got = swap(jnp.concatenate([chunks, extra], axis=0), stage)
        chunks = added(chunks, got[:1])
        extra = added(extra, got[1:])
    return chunks, extra


def gather_chunks(chunks, stages):
    for place in range(4, 0, -1):
        chunks = jnp.concatenate([chunks, swap(chunks, stages[place])], axis=0)
    return chunks, swap(chunks, stages[0])


def from_peers(rows):
    size = lax.axis_size("seq")
    got = [
        lax.ppermute(rows, "seq", [(i, (i + shift) % size) for i in range(size)])
        for shift in range(1, size)
    ]
    return jnp.stack(got)


def shards(
    inputs, cluster_ids, masked, cotangent,
    w_query, w_key, w_value, w_out, w_up, w_down,
    bias_query, bias_value, bias_out, bias_up, bias_down,
    gain_attn, shift_attn, gain_ffn, shift_ffn,
):
    seqs, tokens, width = inputs.shape
    ff = w_up.shape[1]
    total = seqs * tokens

    def row(vector):
        return vector.reshape(1, -1)

    stages_a, stages_b = stage_lists()
    rank_a, rank_b = rank_of(stages_a), rank_of(stages_b)
    core = (rank_a // 16).reshape(1)
    rank_a, rank_b = rank_a.reshape(1), rank_b.reshape(1)
    slot = jnp.cumsum(masked, axis=1) - 1
    sel = jnp.where(masked == 1, slot, -1).astype(jnp.int32)[:, None, :]

    normed, keys, values, own, message = project_call(
        inputs, cluster_ids, w_query, w_key, w_value,
        row(bias_query), row(bias_value), row(gain_attn), row(shift_attn),
    )
    cent, count, out, lse, send = attend_call(own, message, from_peers(message), keys, values)
    (
        ctx, merged, lse_all, keep, away, ctx_m, attn_m, mid_m, own, message, vec,
    ) = masked_call(
        core, inputs, cotangent, sel, cluster_ids, out, lse, from_peers(send),
        w_out, w_up, w_down, row(bias_out), row(bias_up), row(gain_ffn), row(shift_ffn),
    )
    got_grad = from_peers(message)
    other = swap(away, stages_a[0])
    down = ffn_grad_call(rank_a & 15, keep, other, ff, width, True)
    up = ffn_grad_call(rank_b & 15, keep, other, ff, width, False)
    down = scatter_sums(down, stages_a, 1)
    up = scatter_sums(up, stages_b, 1)
    block_out = forward_call(
        inputs, ctx, w_out, w_up, w_down,
        row(bias_out), row(bias_up), row(bias_down), row(gain_ffn), row(shift_ffn),
    )
    grad_key, grad_value, part, send = attend_back_call(
        cent, lse_all, merged, own, got_grad, keys, values
    )
    got_part = from_peers(send)
    g_kv = back_kv_call(grad_key, grad_value, w_key, w_value)
    flat = (total, width)
    normed_flat = normed.reshape(flat)
    out_value = pair_grad_call(
        rank_a, ctx_m, attn_m, normed_flat, grad_value.reshape(flat), "grad_out_value"
    )
    out_value = scatter_sums(out_value, stages_a, 0)
    grad_query, grad_input, vec = back_input_call(
        part, got_part, count, cluster_ids, g_kv, grad_value, inputs, w_query,
        row(gain_attn), mid_m, sel, vec,
    )
    key_query = pair_grad_call(
        rank_b, normed_flat, grad_key.reshape(flat), normed_flat, grad_query.reshape(flat),
        "grad_key_query",
    )
    extra = jnp.pad(vec.astype(BF), ((0, key_query.shape[1] - VEC_ROWS), (0, 0)))[None]
    key_query, extra = scatter_sums_with(key_query, extra, stages_b)
    grad_w_down = place_ffn_call(rank_a, *gather_chunks(down, stages_a), True)
    grad_w_up = place_ffn_call(rank_b, *gather_chunks(up, stages_b), False)
    grad_w_out, grad_w_value = place_pair_call(
        rank_a, *gather_chunks(out_value, stages_a), "place_out_value"
    )
    grad_w_key, grad_w_query = place_pair_call(
        rank_b, *gather_chunks(key_query, stages_b), "place_key_query"
    )
    vec = extra[0].astype(F32)
    return (
        block_out, grad_input,
        grad_w_query, grad_w_key, grad_w_value, grad_w_out, grad_w_up, grad_w_down,
        vec[V_BQ], vec[V_BV], vec[V_BO], vec[V_BU : V_BU + ff // width].reshape(-1),
        vec[V_BD], vec[V_GA], vec[V_SA], vec[V_GF], vec[V_SF],
    )


def solution(mesh):
    rows = P("dp", "seq", None)
    return jax.shard_map(
        shards,
        mesh=mesh,
        in_specs=(rows, P("dp", None, "seq"), P("dp", "seq"), rows) + (P(),) * 15,
        out_specs=(rows, rows) + (P(),) * 15,
        check_vma=False,
    )
```

```python
import functools

import jax
import jax.numpy as jnp
from jax import lax
from jax.experimental import pallas as pl
from jax.experimental.pallas import tpu as pltpu
from jax.sharding import PartitionSpec as P

HEADS = 12
HDIM = 64
CLUSTERS = 100
MASK_MOST = 128
PAIRS = HEADS // 2
LANES = 2 * HDIM
ROWS = 112
SCALE = HDIM**-0.5
EPS = 1e-05
BF = jnp.bfloat16
F32 = jnp.float32

V_BQ, V_BV, V_BO, V_BU, V_BD, V_GA, V_SA, V_GF, V_SF = 0, 1, 2, 3, 7, 8, 9, 10, 11
VEC_ROWS = 16


def dot(a, b):
    return lax.dot_general(a, b, (((1,), (0,)), ((), ())), preferred_element_type=F32)


def dot_nt(a, b):
    return lax.dot_general(a, b, (((1,), (1,)), ((), ())), preferred_element_type=F32)


def dot_tn(a, b):
    return lax.dot_general(a, b, (((0,), (0,)), ((), ())), preferred_element_type=F32)


def norm_parts(rows):
    center = rows - jnp.mean(rows, axis=-1, keepdims=True)
    inverse = lax.rsqrt(jnp.mean(center * center, axis=-1, keepdims=True) + EPS)
    return center * inverse, inverse


def norm_back(incoming, unit, inverse, gain):
    scaled = incoming * gain
    return inverse * (
        scaled
        - jnp.mean(scaled, axis=-1, keepdims=True)
        - unit * jnp.mean(scaled * unit, axis=-1, keepdims=True)
    )


def normal_cdf(upper):
    return 0.5 * (1.0 + lax.erf(upper * (0.5**0.5)))


def lane_of(rows):
    return lax.broadcasted_iota(jnp.int32, (rows, LANES), 1)


def column(slab, index):
    picked = jnp.where(lane_of(slab.shape[0]) == index, slab, 0.0)
    return jnp.sum(picked, axis=1, keepdims=True)


def member_pair(ids, seq, pair):
    tokens = ids.shape[-1]
    rows = lax.broadcasted_iota(jnp.int32, (ROWS, tokens), 0)
    one = [
        jnp.where(rows == ids[2 * pair + side, seq : seq + 1, :], 1.0, 0.0).astype(BF)
        for side in range(2)
    ]
    return jnp.concatenate(one, axis=0)


def vector(ref):
    return ref[...].astype(F32).reshape(1, -1)


def pick_rows(sel):
    slots = lax.broadcasted_iota(jnp.int32, (MASK_MOST, sel.shape[-1]), 0)
    return jnp.where(slots == sel, 1.0, 0.0).astype(BF)


def stack_pair(both):
    left = lane_of(both.shape[0]) < HDIM
    return jnp.concatenate(
        [jnp.where(left, both, 0.0).astype(BF), jnp.where(left, 0.0, both).astype(BF)], axis=0
    )


def unstack_pair(stacked):
    left = lane_of(ROWS) < HDIM
    return jnp.where(left, stacked[:ROWS], stacked[ROWS:])


def pair_lanes(pair):
    return pl.ds(pl.multiple_of(pair * LANES, LANES), LANES)


class Hbm:
    def __init__(self, array):
        self.array = array


class Scalar:
    def __init__(self, array):
        self.array = array


def rank_from(here_ref, stages):
    rank = 0
    for place, (axis, bit) in enumerate(stages[:5]):
        index = here_ref[0 if axis == "dp" else 1]
        rank = rank + ((index >> (bit.bit_length() - 1)) & 1) * (16 >> place)
    return rank


def shapes(*items):
    return [jax.ShapeDtypeStruct(shape, dtype) for shape, dtype in items]


TOKEN = ((8, LANES), F32)
VMEM = pl.BlockSpec(memory_space=pltpu.VMEM)
HBM = pl.BlockSpec(memory_space=pltpu.HBM)
ANY = pl.BlockSpec(memory_space=pl.ANY)


def launch(kernel, name, args, outs, out_hbm=(), tokens=(), scratch=(), mib=16, work=(0, 0), aliases=None):
    count = len(tokens)
    operands, in_specs = list(tokens), [ANY] * count
    for arg in args:
        if isinstance(arg, Hbm):
            operands.append(pltpu.with_memory_space_constraint(arg.array, pltpu.HBM))
            in_specs.append(HBM)
        elif isinstance(arg, Scalar):
            operands.append(arg.array)
            in_specs.append(pl.BlockSpec(memory_space=pltpu.SMEM))
        else:
            operands.append(pltpu.with_memory_space_constraint(arg, pltpu.VMEM))
            in_specs.append(VMEM)
    out_shape = [pltpu.VMEM(shape, dtype) for shape, dtype in outs] + shapes(*out_hbm)
    return pl.pallas_call(
        lambda *refs: kernel(*refs[count:]),
        in_specs=in_specs,
        out_specs=[VMEM] * len(outs) + [HBM] * len(out_hbm),
        out_shape=out_shape,
        scratch_shapes=list(scratch),
        input_output_aliases={count + a: b for a, b in (aliases or {}).items()},
        compiler_params=pltpu.CompilerParams(vmem_limit_bytes=mib * 2**20),
        cost_estimate=cost(*work),
        name=name,
    )(*operands)


def cost(flops, moved):
    return pl.CostEstimate(flops=int(flops), bytes_accessed=int(moved), transcendentals=0)


def load(pairs, sems):
    copies = [
        pltpu.make_async_copy(source, target, sems.at[index])
        for index, (source, target) in enumerate(pairs)
    ]
    for copy in copies:
        copy.start()
    return copies


def project_rows(
    seq, x, ids_ref, wq_ref, wk_ref, wv_ref, bq_ref, bv_ref, gain_ref, shift_ref,
    masked_ref, normed_ref, key_ref, value_ref, own_ref, message_ref, sel_ref, query_s, ready,
):
    ready("x")
    if sel_ref is not None:
        tokens = masked_ref.shape[1]
        before = jnp.where(
            lax.broadcasted_iota(jnp.int32, (tokens, tokens), 0)
            <= lax.broadcasted_iota(jnp.int32, (tokens, tokens), 1),
            1.0,
            0.0,
        ).astype(BF)
        for s in range(masked_ref.shape[0]):
            row = masked_ref[s : s + 1, :]
            spread = jnp.broadcast_to(row.astype(F32), (16, tokens)).astype(BF)
            slot = dot(spread, before)[:1].astype(jnp.int32) - 1
            sel_ref[s : s + 1, :] = jnp.where(row == 1, slot, -1)
    unit, _ = norm_parts(x[seq].astype(F32))
    normed = (unit * vector(gain_ref) + vector(shift_ref)).astype(BF)
    normed_ref[...] = normed
    ready("q")
    query_s[...] = (dot(normed, wq_ref[...]) + vector(bq_ref)).astype(BF)
    lane = lane_of(ROWS)
    ones = jnp.ones((normed.shape[0], LANES), BF)

    def step(pair, slab):
        right = jnp.concatenate([query_s[:, pair_lanes(pair)], ones], axis=1)
        sums = dot(member_pair(ids_ref, seq, pair), right)
        own = unstack_pair(sums[:, :LANES])
        own_ref[pair] = own
        message_ref[pair] = own.astype(BF)
        for side in range(2):
            count = sums[side * ROWS : (side + 1) * ROWS, LANES:]
            low = jnp.minimum(count, 256.0)
            slab = slab + jnp.where(lane == 2 * pair + side, low, 0.0)
            slab = slab + jnp.where(lane == 16 + 2 * pair + side, count - low, 0.0)
        return slab

    slab = lax.fori_loop(0, PAIRS, step, jnp.zeros((ROWS, LANES), F32))
    message_ref[PAIRS] = slab.astype(BF)
    ready("kv")
    key_ref[...] = dot(normed_ref[...], wk_ref[...]).astype(BF)
    value_ref[...] = (dot(normed_ref[...], wv_ref[...]) + vector(bv_ref)).astype(BF)


SLAB = (PAIRS, ROWS, LANES)
SLAB_MORE = (PAIRS + 1, ROWS, LANES)


def project_outs(x):
    _, tokens, width = x.shape
    rows = ((tokens, width), BF)
    return [rows, rows, rows, (SLAB, F32), (SLAB_MORE, BF)], [pltpu.VMEM((tokens, width), BF)]


def project_call(seq, here, fetched, more):
    first = isinstance(fetched[0], Hbm)
    brought = [item.array for item in fetched] if first else []
    x = brought[0] if first else fetched[0]
    outs, scratch = project_outs(x)
    seqs = x.shape[0]
    count, extra = len(fetched), len(more)
    loads = count + seqs - 1 if first else 0
    own_outs = 6 if first else 5
    if first:
        outs = outs + [((seqs, x.shape[1]), jnp.int32)]

    def kernel(here_ref, *refs):
        sources, refs = refs[:count], refs[count:]
        more_in, refs = refs[:extra], refs[extra:]
        results, refs = refs[:own_outs], refs[own_outs:]
        targets, refs = (refs[:count], refs[count:]) if first else (sources, refs)
        more_out, refs = refs[:extra], refs[extra:]
        row_ref, refs = (refs[0], refs[1:]) if extra else (None, refs)
        query_s, sems = refs
        results = tuple(results) + (() if first else (None,))
        pairs = []
        if first:
            order = [seq] + [s for s in range(seqs) if s != seq]
            rows = [(sources[0].at[s], targets[0].at[s]) for s in order]
            pairs = [rows[0]] + list(zip(sources[1:], targets[1:])) + rows[1:]
        pairs = pairs + list(zip(more_in, more_out))
        copies = load(pairs, sems)
        groups = {"x": [], "q": [], "kv": []}
        if first:
            groups = {"x": [0, 7, 8, 9], "q": [1, 2, 5], "kv": [3, 4, 6]}
        waited = set()

        def ready(name):
            for index in groups[name]:
                copies[index].wait()
                waited.add(index)

        project_rows(seq, *targets, *results, query_s, ready)
        for index, copy in enumerate(copies):
            if index not in waited:
                copy.wait()
        if extra:
            row_ref[...] = vector(more_out[-1])

    brings = [(item.shape, item.dtype) for item in brought] + [
        (item.shape, item.dtype) for item in more
    ]
    if extra:
        brings.append(((1, more[-1].shape[0]), F32))
    results = launch(
        kernel, "project", [here] + list(fetched) + [Hbm(item) for item in more], outs + brings,
        scratch=scratch + [pltpu.SemaphoreType.DMA((loads + extra,))],
    )
    if first:
        return results[:5], results[6 : 6 + count], results[6 + count :], results[5]
    return results[:5], fetched, results[5:], None


def attend_kernel(
    own_ref, message_ref, got_ref, key_ref, value_ref,
    cent_ref, count_ref, out_ref, lse_ref, send_ref,
):
    peers = got_ref.shape[0]
    lane = lane_of(ROWS)
    slab = message_ref[PAIRS].astype(F32)
    for peer in range(peers):
        slab = slab + got_ref[peer, PAIRS].astype(F32)
    count = jnp.maximum(slab + pltpu.roll(slab, LANES - 16, 1), 1.0)
    count_ref[...] = count

    def step(pair, lses):
        total = own_ref[pair]
        for peer in range(peers):
            total = total + got_ref[peer, pair].astype(F32)
        divisor = jnp.where(lane < HDIM, column(count, 2 * pair), column(count, 2 * pair + 1))
        cent = (total / divisor).astype(BF)
        cent_ref[pair] = cent
        scores = dot_nt(stack_pair(cent.astype(F32)), key_ref[:, pair_lanes(pair)]) * SCALE
        peak = jnp.max(scores, axis=1, keepdims=True)
        raised = jnp.exp(scores - peak)
        mass = jnp.sum(raised, axis=1, keepdims=True)
        mixed = unstack_pair(dot(raised.astype(BF), value_ref[:, pair_lanes(pair)]) / mass)
        out_ref[pair] = mixed
        send_ref[pair] = mixed.astype(BF)
        lse = peak + jnp.log(mass)
        lses = lses + jnp.where(lane == 2 * pair, lse[:ROWS], 0.0)
        return lses + jnp.where(lane == 2 * pair + 1, lse[ROWS:], 0.0)

    lses = lax.fori_loop(0, PAIRS, step, jnp.zeros((ROWS, LANES), F32))
    lse_ref[...] = lses
    high = lses.astype(BF).astype(F32)
    rest = lses - high
    middle = rest.astype(BF).astype(F32)
    low = (rest - middle).astype(BF).astype(F32)
    send_ref[PAIRS] = (high + pltpu.roll(middle, 16, 1) + pltpu.roll(low, 32, 1)).astype(BF)


def attend_call(*args):
    one = ((ROWS, LANES), F32)
    return launch(
        attend_kernel, "attend", args, [(SLAB, BF), one, (SLAB, F32), one, (SLAB_MORE, BF)]
    )


def merge_kernel(
    seq, out_ref, lse_ref, got_ref, x_ref, cot_ref, sel_ref, ids_ref,
    ctx_ref, merged_ref, lse_all_ref, ctx_m_ref, x_m_ref, cot_m_ref,
):
    peers = got_ref.shape[0]
    lane = lane_of(ROWS)
    lses = [lse_ref[...]]
    for peer in range(peers):
        slab = got_ref[peer, PAIRS].astype(F32)
        lses.append(slab + pltpu.roll(slab, LANES - 16, 1) + pltpu.roll(slab, LANES - 32, 1))
    peak = functools.reduce(jnp.maximum, lses)
    merged = peak + jnp.log(sum(jnp.exp(item - peak) for item in lses))
    lse_all_ref[...] = merged
    portions = [jnp.exp(item - merged) for item in lses]

    def gather(pair, carry):
        total = jnp.zeros((ROWS, LANES), F32)
        for index, portion in enumerate(portions):
            part = out_ref[pair] if index == 0 else got_ref[index - 1, pair].astype(F32)
            weight = jnp.where(
                lane < HDIM, column(portion, 2 * pair), column(portion, 2 * pair + 1)
            )
            total = total + weight * part
        merged_ref[pair] = total
        member = member_pair(ids_ref, seq, pair)
        ctx_ref[:, pair_lanes(pair)] = dot_tn(member, stack_pair(total)).astype(BF)
        return carry

    lax.fori_loop(0, PAIRS, gather, 0)
    pick = pick_rows(sel_ref[seq : seq + 1, :])
    ctx_m_ref[...] = dot(pick, ctx_ref[...]).astype(BF)
    x_m_ref[...] = dot(pick, x_ref[seq]).astype(BF)
    cot_m_ref[...] = dot(pick, cot_ref[seq]).astype(BF)


def merge_call(seq, out, lse, got, x, cot, sel, ids):
    _, tokens, width = x.shape
    picked = ((MASK_MOST, width), BF)
    return launch(
        functools.partial(merge_kernel, seq), "merge", (out, lse, got, x, cot, sel, ids),
        [((tokens, width), BF), (SLAB, F32), ((ROWS, LANES), F32), picked, picked, picked],
    )


def masked_kernel(seqs, *refs):
    here_ref, sel_ref, ids_ref = refs[:3]
    rest = refs[3:]
    ctx_refs, x_refs, cot_refs = rest[:seqs], rest[seqs : 2 * seqs], rest[2 * seqs : 3 * seqs]
    (
        wo_ref, wu_ref, wd_ref, bo_ref, bu_ref, gain_ref, shift_ref,
        keep_ref, send_ref, ctx_m_ref, attn_m_ref, mid_m_ref, vec_ref,
    ) = rest[3 * seqs : 3 * seqs + 13]
    rest = rest[3 * seqs + 13 :]
    own_refs, message_refs = rest[:seqs], rest[seqs : 2 * seqs]
    middle_s, back_s = rest[2 * seqs :]
    width = wo_ref.shape[0]
    ff_block = width
    ff_blocks = wu_ref.shape[1] // ff_block
    half_blocks = ff_blocks // 2
    tail = 2 * half_blocks * ff_block
    core = here_ref[0] & 1
    vec_ref[...] = jnp.zeros_like(vec_ref)
    for s in range(seqs):
        rows = pl.ds(s * MASK_MOST, MASK_MOST)
        ctx_m_ref[rows, :] = ctx_refs[s][...]
        middle_s[rows, :] = x_refs[s][...].astype(F32)
        keep_ref[rows, tail : tail + width] = cot_refs[s][...]
        send_ref[rows, tail : tail + width] = cot_refs[s][...]
    middle = middle_s[...] + (dot(ctx_m_ref[...], wo_ref[...]) + vector(bo_ref))
    middle_s[...] = middle
    unit, _ = norm_parts(middle)
    low = (unit * vector(gain_ref) + vector(shift_ref)).astype(BF)
    keep_ref[:, tail + width :] = low
    send_ref[:, tail + width :] = low
    back_s[...] = jnp.zeros_like(back_s)

    def feed(block, carry):
        lanes = pl.ds(pl.multiple_of(block * ff_block, ff_block), ff_block)
        upper = dot(keep_ref[:, tail + width :], wu_ref[:, lanes]) + bu_ref[:, lanes]
        cdf = normal_cdf(upper)
        hidden = (upper * cdf).astype(BF)
        slope = cdf + upper * (jnp.exp(-0.5 * upper * upper) * 0.3989422804014327)
        grad_y = keep_ref[:, tail : tail + width]
        grad_upper = (dot_nt(grad_y, wd_ref[lanes, :]) * slope).astype(BF)
        back_s[...] += dot_nt(grad_upper, wu_ref[:, lanes])
        vec_ref[pl.ds(V_BU + block, 1), :] = jnp.sum(
            grad_upper.astype(F32), axis=0, keepdims=True
        )
        half = block // half_blocks
        inner = block - half * half_blocks
        first = pl.ds(pl.multiple_of(inner * ff_block, ff_block), ff_block)
        second = pl.ds(
            pl.multiple_of(inner * ff_block + half_blocks * ff_block, ff_block), ff_block
        )

        @pl.when(half == core)
        def _():
            keep_ref[:, first] = hidden
            keep_ref[:, second] = grad_upper

        @pl.when(half != core)
        def _():
            send_ref[:, first] = hidden
            send_ref[:, second] = grad_upper

        return carry

    lax.fori_loop(0, ff_blocks, feed, 0)
    unit, inverse = norm_parts(middle_s[...])
    incoming = back_s[...]
    grad_y = keep_ref[:, tail : tail + width].astype(F32)
    grad_middle = grad_y + norm_back(incoming, unit, inverse, vector(gain_ref))
    mid_m_ref[...] = grad_middle
    grad_attn = grad_middle.astype(BF)
    attn_m_ref[...] = grad_attn
    vec_ref[V_BD : V_BD + 1, :] = jnp.sum(grad_y, axis=0, keepdims=True)
    vec_ref[V_BO : V_BO + 1, :] = jnp.sum(grad_attn.astype(F32), axis=0, keepdims=True)
    vec_ref[V_GF : V_GF + 1, :] = jnp.sum(incoming * unit, axis=0, keepdims=True)
    vec_ref[V_SF : V_SF + 1, :] = jnp.sum(incoming, axis=0, keepdims=True)
    back_s[...] = dot_nt(grad_attn, wo_ref[...])
    for s in range(seqs):
        pick = pick_rows(sel_ref[s : s + 1, :])

        def scatter(pair, carry, s=s, pick=pick):
            member = dot_nt(member_pair(ids_ref, s, pair), pick).astype(BF)
            rows = back_s[s * MASK_MOST : (s + 1) * MASK_MOST, pair_lanes(pair)]
            high = rows.astype(BF)
            low = (rows - high.astype(F32)).astype(BF)
            own = unstack_pair(dot(member, high) + dot(member, low))
            own_refs[s][pair] = own
            message_refs[s][pair] = own.astype(BF)
            return carry

        lax.fori_loop(0, PAIRS, scatter, 0)


def masked_call(here, sel, ids, ctx, x, cot, *weights):
    seqs = len(ctx)
    width, ff = weights[1].shape
    picked = seqs * MASK_MOST
    wide = ((picked, ff + 2 * width), BF)
    out = launch(
        functools.partial(masked_kernel, seqs), "masked_rows",
        (here, sel, ids, *ctx, *x, *cot, *weights),
        [
            wide, wide, ((picked, width), BF), ((picked, width), BF), ((picked, width), F32),
            ((VEC_ROWS, width), F32), *[(SLAB, F32)] * seqs, *[(SLAB, BF)] * seqs,
        ],
        scratch=[pltpu.VMEM((picked, width), F32), pltpu.VMEM((picked, width), F32)],
    )
    return out[:6], out[6 : 6 + seqs], out[6 + seqs :]


def forward_kernel(
    seq, start, x_ref, ctx_ref, wo_ref, wu_ref, wd_ref, bo_ref, bu_ref, bd_ref, gain_ref, shift_ref,
    *rest,
):
    token_ref, y_ref, low_s, total_s, out_s, sem = rest[-6:]
    token_ref[...] = jnp.zeros_like(token_ref)
    rows = pl.ds(start, low_s.shape[0])
    middle = x_ref[seq, rows, :].astype(F32) + (dot(ctx_ref[rows, :], wo_ref[...]) + vector(bo_ref))
    unit, _ = norm_parts(middle)
    low_s[...] = (unit * vector(gain_ref) + vector(shift_ref)).astype(BF)
    total_s[...] = middle + vector(bd_ref)
    block = x_ref.shape[2]

    def feed(index, carry):
        lanes = pl.ds(pl.multiple_of(index * block, block), block)
        upper = dot(low_s[...], wu_ref[:, lanes]) + bu_ref[:, lanes]
        hidden = (upper * normal_cdf(upper)).astype(BF)
        total_s[...] += dot(hidden, wd_ref[lanes, :])
        return carry

    lax.fori_loop(0, wu_ref.shape[1] // block, feed, 0)
    out_s[...] = total_s[...].astype(BF)
    copy = pltpu.make_async_copy(out_s, y_ref.at[seq, rows], sem)
    copy.start()
    copy.wait()


def forward_call(seq, start, x, ctx, weights, former, tokens, block=256):
    width = x.shape[2]
    args = [x, ctx, *weights]
    aliases = {}
    if former is not None:
        aliases = {len(args): 1}
        args.append(Hbm(former))
    return launch(
        functools.partial(forward_kernel, seq, start), "forward_rows", args, [TOKEN],
        out_hbm=[(x.shape, BF)], tokens=tokens, aliases=aliases,
        scratch=[
            pltpu.VMEM((block, width), BF), pltpu.VMEM((block, width), F32),
            pltpu.VMEM((block, width), BF), pltpu.SemaphoreType.DMA,
        ],
    )


def attend_back_kernel(
    cent_ref, lse_ref, merged_ref, own_ref, got_ref, key_ref, value_ref,
    grad_key_ref, grad_value_ref, part_ref, send_ref,
):
    peers = got_ref.shape[0]
    lane = lane_of(ROWS)
    lses = lse_ref[...]

    def step(pair, carry):
        total = own_ref[pair]
        for peer in range(peers):
            total = total + got_ref[peer, pair].astype(F32)
        grad_cent = total.astype(BF).astype(F32)
        product = grad_cent * merged_ref[pair]
        delta = jnp.concatenate(
            [
                jnp.sum(jnp.where(lane < HDIM, product, 0.0), axis=1, keepdims=True),
                jnp.sum(jnp.where(lane < HDIM, 0.0, product), axis=1, keepdims=True),
            ],
            axis=0,
        )
        lse = jnp.concatenate([column(lses, 2 * pair), column(lses, 2 * pair + 1)], axis=0)
        cents = stack_pair(cent_ref[pair].astype(F32))
        grads = stack_pair(grad_cent)
        keys = key_ref[:, pair_lanes(pair)]
        weights = jnp.exp(dot_nt(cents, keys) * SCALE - lse)
        grad_weights = dot_nt(grads, value_ref[:, pair_lanes(pair)])
        grad_scores = (weights * (grad_weights - delta)).astype(BF)
        part = unstack_pair(dot(grad_scores, keys))
        part_ref[pair] = part
        send_ref[pair] = part.astype(BF)
        grad_key_ref[:, pair_lanes(pair)] = (dot_tn(grad_scores, cents) * SCALE).astype(BF)
        grad_value_ref[:, pair_lanes(pair)] = dot_tn(weights.astype(BF), grads).astype(BF)
        return carry

    lax.fori_loop(0, PAIRS, step, 0)


def attend_back_call(*args, tokens=()):
    rows = (args[5].shape, BF)
    return launch(
        attend_back_kernel, "attend_back", args, [rows, rows, (SLAB, F32), (SLAB, BF)],
        tokens=tokens,
    )


def query_kernel(seq, part_ref, got_ref, count_ref, ids_ref, gq_ref):
    peers = got_ref.shape[0]
    lane = lane_of(ROWS)
    count = count_ref[...]

    def step(pair, carry):
        total = part_ref[pair]
        for peer in range(peers):
            total = total + got_ref[peer, pair].astype(F32)
        grad_cent = (total * SCALE).astype(BF).astype(F32)
        divisor = jnp.where(lane < HDIM, column(count, 2 * pair), column(count, 2 * pair + 1))
        spread = stack_pair(grad_cent / divisor)
        member = member_pair(ids_ref, seq, pair)
        gq_ref[:, pair_lanes(pair)] = dot_tn(member, spread).astype(BF)
        return carry

    lax.fori_loop(0, PAIRS, step, 0)


def query_call(seq, part, got, count, ids, width, tokens=()):
    return launch(
        functools.partial(query_kernel, seq), "query_grad", (part, got, count, ids),
        [((ids.shape[-1], width), BF)], tokens=tokens,
    )[0]


def back_input_kernel(
    seq, gq_ref, gk_ref, gv_ref, x_ref, wq_ref, wk_ref, wv_ref, gain_ref, mid_ref, sel_ref,
    vec_in_ref, *rest,
):
    vec_ref, gx_ref, out_s, sem = rest[-4:]
    grad_query, grad_value = gq_ref[...], gv_ref[...]
    incoming = (
        dot_nt(grad_query, wq_ref[...])
        + dot_nt(gk_ref[...], wk_ref[...])
        + dot_nt(grad_value, wv_ref[...])
    )
    unit, inverse = norm_parts(x_ref[seq].astype(F32))
    grad = norm_back(incoming, unit, inverse, vector(gain_ref))
    pick = pick_rows(sel_ref[seq : seq + 1, :])
    middle = mid_ref[seq * MASK_MOST : (seq + 1) * MASK_MOST, :]
    high = middle.astype(BF)
    low = (middle - high.astype(F32)).astype(BF)
    grad = grad + (dot_tn(pick, high) + dot_tn(pick, low))
    out_s[...] = grad.astype(BF)
    copy = pltpu.make_async_copy(out_s, gx_ref.at[seq], sem)
    copy.start()
    vec_ref[...] = vec_in_ref[...]
    vec_ref[V_BQ : V_BQ + 1, :] += jnp.sum(grad_query.astype(F32), axis=0, keepdims=True)
    vec_ref[V_BV : V_BV + 1, :] += jnp.sum(grad_value.astype(F32), axis=0, keepdims=True)
    vec_ref[V_GA : V_GA + 1, :] += jnp.sum(incoming * unit, axis=0, keepdims=True)
    vec_ref[V_SA : V_SA + 1, :] += jnp.sum(incoming, axis=0, keepdims=True)
    copy.wait()


def back_input_call(seq, *args, former, tokens=()):
    args = list(args)
    x, vec = args[3], args[10]
    aliases = {}
    if former is not None:
        aliases = {len(args): 1}
        args.append(Hbm(former))
    vec, grad = launch(
        functools.partial(back_input_kernel, seq), "back_input", args, [(vec.shape, F32)],
        out_hbm=[(x.shape, BF)], tokens=tokens, aliases=aliases,
        scratch=[pltpu.VMEM(x.shape[1:], BF), pltpu.SemaphoreType.DMA],
    )
    return grad, vec


def store_chunks(out_ref, group, product, rank, per_group):
    size = product.shape[0] // per_group
    for index in range(per_group):
        out_ref[group * per_group + (index ^ (rank & (per_group - 1)))] = product[
            index * size : (index + 1) * size
        ].astype(BF)


def lanes_at(start, size):
    return pl.ds(pl.multiple_of(start * size, size), size)


def ffn_grad_kernel(ff, width, down, half, stages, here_ref, keep_ref, got_ref, out_ref):
    rank = rank_from(here_ref, stages) & 15
    rows = ff // 8

    def step(index, carry):
        group = (2 * half + index) ^ (rank // 4)
        if down:
            left, right = lanes_at(group, rows), pl.ds(ff, width)
        else:
            left = lanes_at((ff + width) // rows + (group & 1), rows)
            right = lanes_at(ff // 2 // width + group // 2, width)
        product = dot_tn(keep_ref[:, left], keep_ref[:, right]) + dot_tn(
            got_ref[:, left], got_ref[:, right]
        )
        store_chunks(out_ref, index, product, rank, 4)
        return carry

    lax.fori_loop(0, 2, step, 0)


def ffn_grad_call(here, stages, keep, got, ff, width, down, half, tokens=()):
    return launch(
        functools.partial(ffn_grad_kernel, ff, width, down, half, stages),
        "grad_down" if down else "grad_up", (here, keep, got),
        [((8, ff // 32, width), BF)], tokens=tokens,
    )[0]


def pair_grad_kernel(splits, half, stages, here_ref, *refs):
    out_ref = refs[-1]
    rank = rank_from(here_ref, stages)
    rows = refs[0].shape[1] // 2
    pairs = [(refs[2 * k], refs[2 * k + 1]) for k in range(len(refs) // 2)]

    def step(index, carry):
        group = (2 * half + index) ^ (rank // 8)
        lanes = lanes_at(group & 1, rows)

        def fill(some):
            product = sum(dot_tn(left[:, lanes], right[...]) for left, right in some)
            store_chunks(out_ref, index, product, rank, 8)

        @pl.when(group < 2)
        def _():
            fill(pairs[:splits])

        @pl.when(group >= 2)
        def _():
            fill(pairs[splits:])

        return carry

    lax.fori_loop(0, 2, step, 0)


def pair_grad_call(here, stages, first, second, half, name, tokens=()):
    args = [array for pair in first + second for array in pair]
    width = args[0].shape[1]
    return launch(
        functools.partial(pair_grad_kernel, len(first), half, stages), name, (here, *args),
        [((16, width // 16, width), BF)], tokens=tokens,
    )[0]


def add_kernel(keep_ref, got_ref, *out_refs):
    count = out_refs[0].shape[0]
    for index, out_ref in enumerate(out_refs):
        part = pl.ds(index * count, count)
        out_ref[...] = (keep_ref[part].astype(F32) + got_ref[part].astype(F32)).astype(BF)


def join_kernel(keep_ref, got_ref, out_ref):
    count = keep_ref.shape[0]
    out_ref[:count] = keep_ref[...]
    out_ref[count:] = got_ref[...]


def place_kernel(per_group, base, groups, target, stages, here_ref, chunks_ref, *rest):
    token_ref, *outs = rest[-target.outputs - 3 : -2]
    stage_s, sems = rest[-2:]
    token_ref[...] = jnp.zeros_like(token_ref)
    rank = rank_from(here_ref, stages)
    size = chunks_ref.shape[1]
    copies = []
    for index in range(groups):
        slot = index % 2
        if index >= 2:
            copies[index - 2].wait()
        for inner in range(per_group):
            stage_s[slot, inner * size : (inner + 1) * size, :] = chunks_ref[
                index * per_group + (inner ^ (rank & (per_group - 1)))
            ].astype(F32)
        group = (base + index) ^ (rank // per_group)
        copies.append(target(outs, group, stage_s.at[slot], sems.at[slot]))
    for copy in copies[-2:]:
        copy.wait()


class Copy:
    def __init__(self, choices):
        self.choices = choices
        for chosen, copy in choices:
            self.when(chosen, copy.start)

    def when(self, chosen, act):
        if chosen is None:
            act()
        else:
            pl.when(chosen)(act)

    def wait(self):
        self.choices[0][1].wait()


class DownTarget:
    outputs = 1

    def __call__(self, outs, group, source, sem):
        rows = source.shape[0]
        place = outs[0].at[pl.ds(pl.multiple_of(group * rows, rows), rows)]
        return Copy([(None, pltpu.make_async_copy(source, place, sem))])


class UpTarget:
    outputs = 1

    def __call__(self, outs, group, source, sem):
        rows, width = source.shape
        place = outs[0].at[lanes_at(group & 1, rows), lanes_at(group // 2, width)]
        return Copy([(None, pltpu.make_async_copy(source, place, sem))])


class PairTarget:
    outputs = 2

    def __call__(self, outs, group, source, sem):
        rows = source.shape[0]
        return Copy([
            (
                group // 2 == matrix,
                pltpu.make_async_copy(source, outs[matrix].at[lanes_at(group & 1, rows)], sem),
            )
            for matrix in range(2)
        ])


def place_call(here, stages, chunks, half, target, per_group, out_shapes, former, name, tokens=()):
    count, size, width = chunks.shape
    groups = count // per_group
    args = [here, chunks]
    aliases = {}
    if former is not None:
        aliases = {2 + index: 1 + index for index in range(len(former))}
        args += [Hbm(item) for item in former]
    return launch(
        functools.partial(place_kernel, per_group, half * groups, groups, target, stages), name, args,
        [TOKEN],
        out_hbm=[(shape, F32) for shape in out_shapes], tokens=tokens, aliases=aliases,
        scratch=[
            pltpu.VMEM((2, per_group * size, width), F32), pltpu.SemaphoreType.DMA((2,)),
        ],
    )


def swap(rows, stage):
    axis, bit = stage
    return lax.ppermute(rows, axis, [(i, i ^ bit) for i in range(lax.axis_size(axis))])


def stage_list(first):
    every = []
    for axis in ("dp", "seq"):
        every += [(axis, 1 << k) for k in range(lax.axis_size(axis).bit_length() - 1)]
    return first + [stage for stage in every if stage not in first]


class Stream:
    def __init__(self, here, send, keep, stages, first):
        self.here, self.stages, self.phase, self.keep = here, stages, first, keep
        self.got = swap(send, stages[first])
        self.placed = None

    def finished(self):
        return self.phase == len(self.stages) + 4

    def advance(self, *tokens):
        total = len(self.stages)
        count, size, width = self.keep.shape
        args = (self.keep, self.got)
        if self.phase < total:
            following = self.phase + 1 if self.phase + 1 < total else 4
            if self.phase < 4:
                shape = ((count // 2, size, width), BF)
                self.keep, send = launch(add_kernel, "add", args, [shape, shape], tokens=tokens)
            else:
                send = launch(add_kernel, "add", args, [(self.keep.shape, BF)], tokens=tokens)[0]
                self.keep = send
        else:
            shape = ((2 * count, size, width), BF)
            self.keep = send = launch(join_kernel, "join", args, [shape], tokens=tokens)[0]
            following = 3 - (self.phase - total)
        self.phase += 1
        self.got = swap(send, self.stages[following])
        return self.keep

    def place(self, target, per_group, out_shapes, name, *tokens):
        half = 0 if self.placed is None else 1
        token, *self.placed = place_call(
            self.here, self.stages, (self.keep, self.got)[half], half, target, per_group, out_shapes, self.placed,
            name, tokens,
        )
        return token


def add_rows_kernel(a_ref, b_ref, out_ref):
    out_ref[...] = a_ref[...] + b_ref[...]


def sum_everywhere(rows, stages):
    for stage in stages:
        args = (rows, swap(rows, stage))
        rows = launch(add_rows_kernel, "add_rows", args, [(rows.shape, F32)])[0]
    return rows


def unpack_kernel(vec_ref, *out_refs):
    for start, out_ref in zip((V_BQ, V_BV, V_BO, V_BU, V_BD, V_GA, V_SA, V_GF, V_SF), out_refs):
        count = out_ref.shape[0] // vec_ref.shape[1]
        rows = [vec_ref[start + index : start + index + 1, :] for index in range(count)]
        out_ref[...] = jnp.concatenate(rows, axis=1).reshape(out_ref.shape[0])


def unpack_call(vec, ff):
    width = vec.shape[1]
    outs = shapes(*[((ff if index == 3 else width,), F32) for index in range(9)])
    return pl.pallas_call(
        unpack_kernel,
        in_specs=[VMEM],
        out_specs=[VMEM] * 9,
        out_shape=outs,
        compiler_params=pltpu.CompilerParams(vmem_limit_bytes=4 * 2**20),
        name="unpack",
    )(pltpu.with_memory_space_constraint(vec, pltpu.VMEM))


def from_peers(rows):
    size = lax.axis_size("seq")
    got = [
        lax.ppermute(rows, "seq", [(i, (i + shift) % size) for i in range(size)])
        for shift in range(1, size)
    ]
    return jnp.stack(got)


def shards(
    inputs, cluster_ids, masked, cotangent,
    w_query, w_key, w_value, w_out, w_up, w_down,
    bias_query, bias_value, bias_out, bias_up, bias_down,
    gain_attn, shift_attn, gain_ffn, shift_ffn,
):
    seqs, tokens, width = inputs.shape
    every = range(seqs)
    ff = w_up.shape[1]
    core, x, y = ("dp", 1), ("dp", 2), ("seq", 1)
    z = ("dp", lax.axis_size("dp") // 4)
    stages_a = stage_list([core, x, y])
    stages_b = stage_list([core, z, y, x])
    stages_c = stage_list([core, x, y])
    stages_d = stage_list([core, z, x, y])
    here = Scalar(jnp.stack([lax.axis_index("dp"), lax.axis_index("seq")]).astype(jnp.int32))
    ids = cluster_ids.transpose(1, 0, 2)

    fetched = [
        Hbm(item)
        for item in (
            inputs, ids, w_query, w_key, w_value, bias_query, bias_value, gain_attn, shift_attn,
            masked,
        )
    ]
    more = [cotangent, w_out, w_up, w_down, bias_out, bias_down, gain_ffn, shift_ffn, bias_up]
    projected, sel = [], None
    for s in every:
        results, fetched, brought, found = project_call(
            s, here, fetched, more if s == seqs - 1 else []
        )
        projected.append(results)
        sel = found if s == 0 else sel
    normed, keys, values, own, message = zip(*projected)
    x_v, ids_v, wq_v, wk_v, wv_v, _, _, gain_v, _, _ = fetched
    cot_v, wo_v, wu_v, wd_v, bo_v, bd_v, gf_v, sf_v, _, up_rows = brought
    got = [from_peers(item) for item in message]
    cent, count, out, lse, send = zip(*[
        attend_call(own[s], message[s], got[s], keys[s], values[s]) for s in every
    ])
    got = [from_peers(item) for item in send]
    ctx, merged, lse_all, ctx_m, x_m, cot_m = zip(*[
        merge_call(s, out[s], lse[s], got[s], x_v, cot_v, sel, ids_v) for s in every
    ])
    (keep, away, ctx_m, attn_m, mid_m, vec), own, message = masked_call(
        here, sel, ids_v, ctx_m, x_m, cot_m, wo_v, wu_v, wd_v, bo_v, up_rows, gf_v, sf_v
    )
    got_grad = [from_peers(item) for item in message]
    other = swap(away, core)
    weights = (wo_v, wu_v, wd_v, bo_v, up_rows, bd_v, gf_v, sf_v)
    blocks = [(s, start) for s in every for start in range(0, tokens, 256)]
    block_out = None

    def forward(*earlier):
        nonlocal block_out
        if blocks:
            s, start = blocks.pop(0)
            token, block_out = forward_call(s, start, x_v, ctx[s], weights, block_out, earlier)
            return token
        return earlier[0]

    def ffn_stream(stages, down, *earlier):
        send = ffn_grad_call(here, stages, keep, other, ff, width, down, 1, earlier)
        own = ffn_grad_call(here, stages, keep, other, ff, width, down, 0, (send,))
        return Stream(here, send, own, stages, 1)

    def pair_stream(stages, first, second, name, *earlier):
        send = pair_grad_call(here, stages, first, second, 1, name, earlier)
        own = pair_grad_call(here, stages, first, second, 0, name, (send,))
        return Stream(here, send, own, stages, 0)

    last = forward(vec)
    down = ffn_stream(stages_a, True, last)
    up = ffn_stream(stages_b, False, down.keep)
    grad_key, grad_value, part, send = [], [], [], []
    last = up.keep
    for s in every:
        results = attend_back_call(
            cent[s], lse_all[s], merged[s], own[s], got_grad[s], keys[s], values[s], tokens=(last,)
        )
        for items, result in zip((grad_key, grad_value, part, send), results):
            items.append(result)
        last = send[s]
    got_part = [from_peers(item) for item in send]
    out_value = pair_stream(
        stages_c, [(ctx_m, attn_m)], [(normed[s], grad_value[s]) for s in every],
        "grad_out_value", last,
    )
    last = down.advance(out_value.keep)
    grad_query = []
    for s in every:
        last = query_call(s, part[s], got_part[s], count[s], ids_v, width, (last,))
        grad_query.append(last)
    last = out_value.advance(last)
    last = up.advance(last)
    key_query = pair_stream(
        stages_d, [(normed[s], grad_key[s]) for s in every],
        [(normed[s], grad_query[s]) for s in every], "grad_key_query", last,
    )
    last = key_query.keep
    grad_input = None
    for s in every:
        grad_input, vec = back_input_call(
            s, grad_query[s], grad_key[s], grad_value[s], x_v, wq_v, wk_v, wv_v, gain_v, mid_m, sel,
            vec, former=grad_input, tokens=(last,),
        )
        last = key_query.advance(vec) if s == 0 else vec
    last = down.advance(last)
    last = forward(last)
    last = up.advance(last)
    last = out_value.advance(last)
    last = forward(last)
    last = key_query.advance(last)
    last = forward(last)
    vec = sum_everywhere(vec, stages_a)
    places = {
        down: (DownTarget(), 4, [(ff, width)], "place_down"),
        up: (UpTarget(), 4, [(width, ff)], "place_up"),
        out_value: (PairTarget(), 8, [(width, width)] * 2, "place_out_value"),
        key_query: (PairTarget(), 8, [(width, width)] * 2, "place_key_query"),
    }
    order = (down, up, out_value, key_query)
    while not all(stream.finished() for stream in order):
        for stream in order:
            if not stream.finished():
                last = stream.advance(last)
    for _ in range(2):
        for stream in order:
            last = stream.place(*places[stream], last)
    (grad_w_down,), (grad_w_up,) = down.placed, up.placed
    grad_w_out, grad_w_value = out_value.placed
    grad_w_key, grad_w_query = key_query.placed
    return (
        block_out, grad_input,
        grad_w_query, grad_w_key, grad_w_value, grad_w_out, grad_w_up, grad_w_down,
        *unpack_call(vec, ff),
    )


def solution(mesh):
    rows = P("dp", "seq", None)
    return jax.shard_map(
        shards,
        mesh=mesh,
        in_specs=(rows, P("dp", None, "seq"), P("dp", "seq"), rows) + (P(),) * 15,
        out_specs=(rows, rows) + (P(),) * 15,
        check_vma=False,
    )
```

```python
import functools

import jax
import jax.numpy as jnp
from jax import lax
from jax.experimental import pallas as pl
from jax.experimental.pallas import tpu as pltpu
from jax.sharding import PartitionSpec as P

HEADS = 12
HDIM = 64
CLUSTERS = 100
MASK_MOST = 128
PAIRS = HEADS // 2
LANES = 2 * HDIM
ROWS = 112
SCALE = HDIM**-0.5
EPS = 1e-05
BF = jnp.bfloat16
F32 = jnp.float32

V_BQ, V_BV, V_BO, V_BU, V_BD, V_GA, V_SA, V_GF, V_SF = 0, 1, 2, 3, 7, 8, 9, 10, 11
VEC_ROWS = 16


def dot(a, b):
    return lax.dot_general(a, b, (((1,), (0,)), ((), ())), preferred_element_type=F32)


def dot_nt(a, b):
    return lax.dot_general(a, b, (((1,), (1,)), ((), ())), preferred_element_type=F32)


def dot_tn(a, b):
    return lax.dot_general(a, b, (((0,), (0,)), ((), ())), preferred_element_type=F32)


def norm_parts(rows):
    center = rows - jnp.mean(rows, axis=-1, keepdims=True)
    inverse = lax.rsqrt(jnp.mean(center * center, axis=-1, keepdims=True) + EPS)
    return center * inverse, inverse


def norm_back(incoming, unit, inverse, gain):
    scaled = incoming * gain
    return inverse * (
        scaled
        - jnp.mean(scaled, axis=-1, keepdims=True)
        - unit * jnp.mean(scaled * unit, axis=-1, keepdims=True)
    )


def normal_cdf(upper):
    return 0.5 * (1.0 + lax.erf(upper * (0.5**0.5)))


def lane_of(rows):
    return lax.broadcasted_iota(jnp.int32, (rows, LANES), 1)


def column(slab, index):
    picked = jnp.where(lane_of(slab.shape[0]) == index, slab, 0.0)
    return jnp.sum(picked, axis=1, keepdims=True)


def member_pair(ids, seq, pair):
    tokens = ids.shape[-1]
    rows = lax.broadcasted_iota(jnp.int32, (ROWS, tokens), 0)
    one = [
        jnp.where(rows == ids[2 * pair + side, seq : seq + 1, :], 1.0, 0.0).astype(BF)
        for side in range(2)
    ]
    return jnp.concatenate(one, axis=0)


def vector(ref):
    return ref[...].astype(F32).reshape(1, -1)


def pick_rows(sel):
    slots = lax.broadcasted_iota(jnp.int32, (MASK_MOST, sel.shape[-1]), 0)
    return jnp.where(slots == sel, 1.0, 0.0).astype(BF)


def stack_pair(both):
    left = lane_of(both.shape[0]) < HDIM
    return jnp.concatenate(
        [jnp.where(left, both, 0.0).astype(BF), jnp.where(left, 0.0, both).astype(BF)], axis=0
    )


def unstack_pair(stacked):
    left = lane_of(ROWS) < HDIM
    return jnp.where(left, stacked[:ROWS], stacked[ROWS:])


def pair_lanes(pair):
    return pl.ds(pl.multiple_of(pair * LANES, LANES), LANES)


class Hbm:
    def __init__(self, array):
        self.array = array


class Scalar:
    def __init__(self, array):
        self.array = array


def rank_from(here_ref, stages):
    rank = 0
    for place, (axis, bit) in enumerate(stages[:5]):
        index = here_ref[0 if axis == "dp" else 1]
        rank = rank + ((index >> (bit.bit_length() - 1)) & 1) * (16 >> place)
    return rank


def shapes(*items):
    return [jax.ShapeDtypeStruct(shape, dtype) for shape, dtype in items]


SMALL = 1.0
TOKEN = ((8, LANES), F32)
VMEM = pl.BlockSpec(memory_space=pltpu.VMEM)
HBM = pl.BlockSpec(memory_space=pltpu.HBM)
ANY = pl.BlockSpec(memory_space=pl.ANY)


def launch(kernel, name, args, outs, out_hbm=(), tokens=(), scratch=(), mib=16, work=5.0, aliases=None):
    count = len(tokens)
    operands, in_specs = list(tokens), [ANY] * count
    for arg in args:
        if isinstance(arg, Hbm):
            operands.append(pltpu.with_memory_space_constraint(arg.array, pltpu.HBM))
            in_specs.append(HBM)
        elif isinstance(arg, Scalar):
            operands.append(arg.array)
            in_specs.append(pl.BlockSpec(memory_space=pltpu.SMEM))
        else:
            operands.append(pltpu.with_memory_space_constraint(arg, pltpu.VMEM))
            in_specs.append(VMEM)
    out_shape = [pltpu.VMEM(shape, dtype) for shape, dtype in outs] + shapes(*out_hbm)
    return pl.pallas_call(
        lambda *refs: kernel(*refs[count:]),
        in_specs=in_specs,
        out_specs=[VMEM] * len(outs) + [HBM] * len(out_hbm),
        out_shape=out_shape,
        scratch_shapes=list(scratch),
        input_output_aliases={count + a: b for a, b in (aliases or {}).items()},
        compiler_params=pltpu.CompilerParams(vmem_limit_bytes=mib * 2**20),
        cost_estimate=pl.CostEstimate(
            flops=int(work * 1e9), bytes_accessed=0, transcendentals=0
        ),
        name=name,
    )(*operands)


def load(pairs, sems):
    copies = [
        pltpu.make_async_copy(source, target, sems.at[index])
        for index, (source, target) in enumerate(pairs)
    ]
    for copy in copies:
        copy.start()
    return copies


def project_rows(
    seq, x, ids_ref, wq_ref, wk_ref, wv_ref, bq_ref, bv_ref, gain_ref, shift_ref,
    masked_ref, normed_ref, key_ref, value_ref, own_ref, message_ref, sel_ref, query_s, ready,
):
    ready("x")
    if sel_ref is not None:
        tokens = masked_ref.shape[1]
        before = jnp.where(
            lax.broadcasted_iota(jnp.int32, (tokens, tokens), 0)
            <= lax.broadcasted_iota(jnp.int32, (tokens, tokens), 1),
            1.0,
            0.0,
        ).astype(BF)
        for s in range(masked_ref.shape[0]):
            row = masked_ref[s : s + 1, :]
            spread = jnp.broadcast_to(row.astype(F32), (16, tokens)).astype(BF)
            slot = dot(spread, before)[:1].astype(jnp.int32) - 1
            sel_ref[s : s + 1, :] = jnp.where(row == 1, slot, -1)
    unit, _ = norm_parts(x[seq].astype(F32))
    normed = (unit * vector(gain_ref) + vector(shift_ref)).astype(BF)
    normed_ref[...] = normed
    ready("q")
    query_s[...] = (dot(normed, wq_ref[...]) + vector(bq_ref)).astype(BF)
    lane = lane_of(ROWS)
    ones = jnp.ones((normed.shape[0], LANES), BF)

    def step(pair, slab):
        right = jnp.concatenate([query_s[:, pair_lanes(pair)], ones], axis=1)
        sums = dot(member_pair(ids_ref, seq, pair), right)
        own = unstack_pair(sums[:, :LANES])
        own_ref[pair] = own
        message_ref[pair] = own.astype(BF)
        for side in range(2):
            count = sums[side * ROWS : (side + 1) * ROWS, LANES:]
            low = jnp.minimum(count, 256.0)
            slab = slab + jnp.where(lane == 2 * pair + side, low, 0.0)
            slab = slab + jnp.where(lane == 16 + 2 * pair + side, count - low, 0.0)
        return slab

    slab = lax.fori_loop(0, PAIRS, step, jnp.zeros((ROWS, LANES), F32))
    message_ref[PAIRS] = slab.astype(BF)
    ready("kv")
    key_ref[...] = dot(normed_ref[...], wk_ref[...]).astype(BF)
    value_ref[...] = (dot(normed_ref[...], wv_ref[...]) + vector(bv_ref)).astype(BF)


SLAB = (PAIRS, ROWS, LANES)
SLAB_MORE = (PAIRS + 1, ROWS, LANES)


def project_outs(x):
    _, tokens, width = x.shape
    rows = ((tokens, width), BF)
    return [rows, rows, rows, (SLAB, F32), (SLAB_MORE, BF)], [pltpu.VMEM((tokens, width), BF)]


def project_call(seq, here, fetched, more):
    first = isinstance(fetched[0], Hbm)
    brought = [item.array for item in fetched] if first else []
    x = brought[0] if first else fetched[0]
    outs, scratch = project_outs(x)
    seqs = x.shape[0]
    count, extra = len(fetched), len(more)
    loads = count + seqs - 1 if first else 0
    own_outs = 6 if first else 5
    if first:
        outs = outs + [((seqs, x.shape[1]), jnp.int32)]

    def kernel(here_ref, *refs):
        sources, refs = refs[:count], refs[count:]
        more_in, refs = refs[:extra], refs[extra:]
        results, refs = refs[:own_outs], refs[own_outs:]
        targets, refs = (refs[:count], refs[count:]) if first else (sources, refs)
        more_out, refs = refs[:extra], refs[extra:]
        row_ref, refs = (refs[0], refs[1:]) if extra else (None, refs)
        query_s, sems = refs
        results = tuple(results) + (() if first else (None,))
        pairs = []
        if first:
            order = [seq] + [s for s in range(seqs) if s != seq]
            rows = [(sources[0].at[s], targets[0].at[s]) for s in order]
            pairs = [rows[0]] + list(zip(sources[1:], targets[1:])) + rows[1:]
        pairs = pairs + list(zip(more_in, more_out))
        copies = load(pairs, sems)
        groups = {"x": [], "q": [], "kv": []}
        if first:
            groups = {"x": [0, 7, 8, 9], "q": [1, 2, 5], "kv": [3, 4, 6]}
        waited = set()

        def ready(name):
            for index in groups[name]:
                copies[index].wait()
                waited.add(index)

        project_rows(seq, *targets, *results, query_s, ready)
        for index, copy in enumerate(copies):
            if index not in waited:
                copy.wait()
        if extra:
            row_ref[...] = vector(more_out[-1])

    brings = [(item.shape, item.dtype) for item in brought] + [
        (item.shape, item.dtype) for item in more
    ]
    if extra:
        brings.append(((1, more[-1].shape[0]), F32))
    results = launch(
        kernel, "project", [here] + list(fetched) + [Hbm(item) for item in more], outs + brings,
        scratch=scratch + [pltpu.SemaphoreType.DMA((loads + extra,))],
    )
    if first:
        return results[:5], results[6 : 6 + count], results[6 + count :], results[5]
    return results[:5], fetched, results[5:], None


def attend_kernel(
    own_ref, message_ref, got_ref, key_ref, value_ref,
    cent_ref, count_ref, out_ref, lse_ref, send_ref,
):
    peers = got_ref.shape[0]
    lane = lane_of(ROWS)
    slab = message_ref[PAIRS].astype(F32)
    for peer in range(peers):
        slab = slab + got_ref[peer, PAIRS].astype(F32)
    count = jnp.maximum(slab + pltpu.roll(slab, LANES - 16, 1), 1.0)
    count_ref[...] = count

    def step(pair, lses):
        total = own_ref[pair]
        for peer in range(peers):
            total = total + got_ref[peer, pair].astype(F32)
        divisor = jnp.where(lane < HDIM, column(count, 2 * pair), column(count, 2 * pair + 1))
        cent = (total / divisor).astype(BF)
        cent_ref[pair] = cent
        scores = dot_nt(stack_pair(cent.astype(F32)), key_ref[:, pair_lanes(pair)]) * SCALE
        peak = jnp.max(scores, axis=1, keepdims=True)
        raised = jnp.exp(scores - peak)
        mass = jnp.sum(raised, axis=1, keepdims=True)
        mixed = unstack_pair(dot(raised.astype(BF), value_ref[:, pair_lanes(pair)]) / mass)
        out_ref[pair] = mixed
        send_ref[pair] = mixed.astype(BF)
        lse = peak + jnp.log(mass)
        lses = lses + jnp.where(lane == 2 * pair, lse[:ROWS], 0.0)
        return lses + jnp.where(lane == 2 * pair + 1, lse[ROWS:], 0.0)

    lses = lax.fori_loop(0, PAIRS, step, jnp.zeros((ROWS, LANES), F32))
    lse_ref[...] = lses
    high = lses.astype(BF).astype(F32)
    rest = lses - high
    middle = rest.astype(BF).astype(F32)
    low = (rest - middle).astype(BF).astype(F32)
    send_ref[PAIRS] = (high + pltpu.roll(middle, 16, 1) + pltpu.roll(low, 32, 1)).astype(BF)


def attend_call(*args, tokens=()):
    one = ((ROWS, LANES), F32)
    return launch(
        attend_kernel, "attend", args, [(SLAB, BF), one, (SLAB, F32), one, (SLAB_MORE, BF)],
        tokens=tokens,
    )


def merge_kernel(
    seq, out_ref, lse_ref, got_ref, x_ref, cot_ref, sel_ref, ids_ref,
    ctx_ref, merged_ref, lse_all_ref, ctx_m_ref, x_m_ref, cot_m_ref,
):
    peers = got_ref.shape[0]
    lane = lane_of(ROWS)
    lses = [lse_ref[...]]
    for peer in range(peers):
        slab = got_ref[peer, PAIRS].astype(F32)
        lses.append(slab + pltpu.roll(slab, LANES - 16, 1) + pltpu.roll(slab, LANES - 32, 1))
    peak = functools.reduce(jnp.maximum, lses)
    merged = peak + jnp.log(sum(jnp.exp(item - peak) for item in lses))
    lse_all_ref[...] = merged
    portions = [jnp.exp(item - merged) for item in lses]

    def gather(pair, carry):
        total = jnp.zeros((ROWS, LANES), F32)
        for index, portion in enumerate(portions):
            part = out_ref[pair] if index == 0 else got_ref[index - 1, pair].astype(F32)
            weight = jnp.where(
                lane < HDIM, column(portion, 2 * pair), column(portion, 2 * pair + 1)
            )
            total = total + weight * part
        merged_ref[pair] = total
        member = member_pair(ids_ref, seq, pair)
        ctx_ref[:, pair_lanes(pair)] = dot_tn(member, stack_pair(total)).astype(BF)
        return carry

    lax.fori_loop(0, PAIRS, gather, 0)
    pick = pick_rows(sel_ref[seq : seq + 1, :])
    ctx_m_ref[...] = dot(pick, ctx_ref[...]).astype(BF)
    x_m_ref[...] = dot(pick, x_ref[seq]).astype(BF)
    cot_m_ref[...] = dot(pick, cot_ref[seq]).astype(BF)


def merge_call(seq, out, lse, got, x, cot, sel, ids, tokens=()):
    _, length, width = x.shape
    picked = ((MASK_MOST, width), BF)
    return launch(
        functools.partial(merge_kernel, seq), "merge", (out, lse, got, x, cot, sel, ids),
        [((length, width), BF), (SLAB, F32), ((ROWS, LANES), F32), picked, picked, picked],
        tokens=tokens,
    )


def masked_kernel(seqs, *refs):
    here_ref, sel_ref, ids_ref = refs[:3]
    rest = refs[3:]
    ctx_refs, x_refs, cot_refs = rest[:seqs], rest[seqs : 2 * seqs], rest[2 * seqs : 3 * seqs]
    (
        wo_ref, wu_ref, wd_ref, bo_ref, bu_ref, gain_ref, shift_ref,
        keep_ref, send_ref, ctx_m_ref, attn_m_ref, mid_m_ref, vec_ref,
    ) = rest[3 * seqs : 3 * seqs + 13]
    rest = rest[3 * seqs + 13 :]
    own_refs, message_refs = rest[:seqs], rest[seqs : 2 * seqs]
    middle_s, back_s = rest[2 * seqs :]
    width = wo_ref.shape[0]
    ff_block = width
    ff_blocks = wu_ref.shape[1] // ff_block
    half_blocks = ff_blocks // 2
    tail = 2 * half_blocks * ff_block
    core = here_ref[0] & 1
    vec_ref[...] = jnp.zeros_like(vec_ref)
    for s in range(seqs):
        rows = pl.ds(s * MASK_MOST, MASK_MOST)
        ctx_m_ref[rows, :] = ctx_refs[s][...]
        middle_s[rows, :] = x_refs[s][...].astype(F32)
        keep_ref[rows, tail : tail + width] = cot_refs[s][...]
        send_ref[rows, tail : tail + width] = cot_refs[s][...]
    middle = middle_s[...] + (dot(ctx_m_ref[...], wo_ref[...]) + vector(bo_ref))
    middle_s[...] = middle
    unit, _ = norm_parts(middle)
    low = (unit * vector(gain_ref) + vector(shift_ref)).astype(BF)
    keep_ref[:, tail + width :] = low
    send_ref[:, tail + width :] = low
    back_s[...] = jnp.zeros_like(back_s)

    def feed(block, carry):
        lanes = pl.ds(pl.multiple_of(block * ff_block, ff_block), ff_block)
        upper = dot(keep_ref[:, tail + width :], wu_ref[:, lanes]) + bu_ref[:, lanes]
        cdf = normal_cdf(upper)
        hidden = (upper * cdf).astype(BF)
        slope = cdf + upper * (jnp.exp(-0.5 * upper * upper) * 0.3989422804014327)
        grad_y = keep_ref[:, tail : tail + width]
        grad_upper = (dot_nt(grad_y, wd_ref[lanes, :]) * slope).astype(BF)
        back_s[...] += dot_nt(grad_upper, wu_ref[:, lanes])
        vec_ref[pl.ds(V_BU + block, 1), :] = jnp.sum(
            grad_upper.astype(F32), axis=0, keepdims=True
        )
        half = block // half_blocks
        inner = block - half * half_blocks
        first = pl.ds(pl.multiple_of(inner * ff_block, ff_block), ff_block)
        second = pl.ds(
            pl.multiple_of(inner * ff_block + half_blocks * ff_block, ff_block), ff_block
        )

        @pl.when(half == core)
        def _():
            keep_ref[:, first] = hidden
            keep_ref[:, second] = grad_upper

        @pl.when(half != core)
        def _():
            send_ref[:, first] = hidden
            send_ref[:, second] = grad_upper

        return carry

    lax.fori_loop(0, ff_blocks, feed, 0)
    unit, inverse = norm_parts(middle_s[...])
    incoming = back_s[...]
    grad_y = keep_ref[:, tail : tail + width].astype(F32)
    grad_middle = grad_y + norm_back(incoming, unit, inverse, vector(gain_ref))
    mid_m_ref[...] = grad_middle
    grad_attn = grad_middle.astype(BF)
    attn_m_ref[...] = grad_attn
    vec_ref[V_BD : V_BD + 1, :] = jnp.sum(grad_y, axis=0, keepdims=True)
    vec_ref[V_BO : V_BO + 1, :] = jnp.sum(grad_attn.astype(F32), axis=0, keepdims=True)
    vec_ref[V_GF : V_GF + 1, :] = jnp.sum(incoming * unit, axis=0, keepdims=True)
    vec_ref[V_SF : V_SF + 1, :] = jnp.sum(incoming, axis=0, keepdims=True)
    back_s[...] = dot_nt(grad_attn, wo_ref[...])
    for s in range(seqs):
        pick = pick_rows(sel_ref[s : s + 1, :])

        def scatter(pair, carry, s=s, pick=pick):
            member = dot_nt(member_pair(ids_ref, s, pair), pick).astype(BF)
            rows = back_s[s * MASK_MOST : (s + 1) * MASK_MOST, pair_lanes(pair)]
            high = rows.astype(BF)
            low = (rows - high.astype(F32)).astype(BF)
            own = unstack_pair(dot(member, high) + dot(member, low))
            own_refs[s][pair] = own
            message_refs[s][pair] = own.astype(BF)
            return carry

        lax.fori_loop(0, PAIRS, scatter, 0)


def masked_call(here, sel, ids, ctx, x, cot, *weights):
    seqs = len(ctx)
    width, ff = weights[1].shape
    picked = seqs * MASK_MOST
    wide = ((picked, ff + 2 * width), BF)
    out = launch(
        functools.partial(masked_kernel, seqs), "masked_rows",
        (here, sel, ids, *ctx, *x, *cot, *weights),
        [
            wide, wide, ((picked, width), BF), ((picked, width), BF), ((picked, width), F32),
            ((VEC_ROWS, width), F32), *[(SLAB, F32)] * seqs, *[(SLAB, BF)] * seqs,
        ],
        scratch=[pltpu.VMEM((picked, width), F32), pltpu.VMEM((picked, width), F32)],
    )
    return out[:6], out[6 : 6 + seqs], out[6 + seqs :]


def forward_kernel(
    seq, start, x_ref, ctx_ref, wo_ref, wu_ref, wd_ref, bo_ref, bu_ref, bd_ref, gain_ref, shift_ref,
    *rest,
):
    token_ref, y_ref, low_s, total_s, out_s, sem = rest[-6:]
    token_ref[...] = jnp.zeros_like(token_ref)
    rows = pl.ds(start, low_s.shape[0])
    middle = x_ref[seq, rows, :].astype(F32) + (dot(ctx_ref[rows, :], wo_ref[...]) + vector(bo_ref))
    unit, _ = norm_parts(middle)
    low_s[...] = (unit * vector(gain_ref) + vector(shift_ref)).astype(BF)
    total_s[...] = middle + vector(bd_ref)
    block = x_ref.shape[2]

    def feed(index, carry):
        lanes = pl.ds(pl.multiple_of(index * block, block), block)
        upper = dot(low_s[...], wu_ref[:, lanes]) + bu_ref[:, lanes]
        hidden = (upper * normal_cdf(upper)).astype(BF)
        total_s[...] += dot(hidden, wd_ref[lanes, :])
        return carry

    lax.fori_loop(0, wu_ref.shape[1] // block, feed, 0)
    out_s[...] = total_s[...].astype(BF)
    copy = pltpu.make_async_copy(out_s, y_ref.at[seq, rows], sem)
    copy.start()
    copy.wait()


def forward_call(seq, start, x, ctx, weights, former, tokens, block=256):
    width = x.shape[2]
    args = [x, ctx, *weights]
    aliases = {}
    if former is not None:
        aliases = {len(args): 1}
        args.append(Hbm(former))
    return launch(
        functools.partial(forward_kernel, seq, start), "forward_rows", args, [TOKEN],
        out_hbm=[(x.shape, BF)], tokens=tokens, aliases=aliases,
        scratch=[
            pltpu.VMEM((block, width), BF), pltpu.VMEM((block, width), F32),
            pltpu.VMEM((block, width), BF), pltpu.SemaphoreType.DMA,
        ],
    )


def attend_back_kernel(
    cent_ref, lse_ref, merged_ref, own_ref, got_ref, key_ref, value_ref,
    grad_key_ref, grad_value_ref, part_ref, send_ref,
):
    peers = got_ref.shape[0]
    lane = lane_of(ROWS)
    lses = lse_ref[...]

    def step(pair, carry):
        total = own_ref[pair]
        for peer in range(peers):
            total = total + got_ref[peer, pair].astype(F32)
        grad_cent = total.astype(BF).astype(F32)
        product = grad_cent * merged_ref[pair]
        delta = jnp.concatenate(
            [
                jnp.sum(jnp.where(lane < HDIM, product, 0.0), axis=1, keepdims=True),
                jnp.sum(jnp.where(lane < HDIM, 0.0, product), axis=1, keepdims=True),
            ],
            axis=0,
        )
        lse = jnp.concatenate([column(lses, 2 * pair), column(lses, 2 * pair + 1)], axis=0)
        cents = stack_pair(cent_ref[pair].astype(F32))
        grads = stack_pair(grad_cent)
        keys = key_ref[:, pair_lanes(pair)]
        weights = jnp.exp(dot_nt(cents, keys) * SCALE - lse)
        grad_weights = dot_nt(grads, value_ref[:, pair_lanes(pair)])
        grad_scores = (weights * (grad_weights - delta)).astype(BF)
        part = unstack_pair(dot(grad_scores, keys))
        part_ref[pair] = part
        send_ref[pair] = part.astype(BF)
        grad_key_ref[:, pair_lanes(pair)] = (dot_tn(grad_scores, cents) * SCALE).astype(BF)
        grad_value_ref[:, pair_lanes(pair)] = dot_tn(weights.astype(BF), grads).astype(BF)
        return carry

    lax.fori_loop(0, PAIRS, step, 0)


def attend_back_call(*args, tokens=()):
    rows = (args[5].shape, BF)
    return launch(
        attend_back_kernel, "attend_back", args, [rows, rows, (SLAB, F32), (SLAB, BF)],
        tokens=tokens,
    )


def query_kernel(seq, part_ref, got_ref, count_ref, ids_ref, gq_ref):
    peers = got_ref.shape[0]
    lane = lane_of(ROWS)
    count = count_ref[...]

    def step(pair, carry):
        total = part_ref[pair]
        for peer in range(peers):
            total = total + got_ref[peer, pair].astype(F32)
        grad_cent = (total * SCALE).astype(BF).astype(F32)
        divisor = jnp.where(lane < HDIM, column(count, 2 * pair), column(count, 2 * pair + 1))
        spread = stack_pair(grad_cent / divisor)
        member = member_pair(ids_ref, seq, pair)
        gq_ref[:, pair_lanes(pair)] = dot_tn(member, spread).astype(BF)
        return carry

    lax.fori_loop(0, PAIRS, step, 0)


def query_call(seq, part, got, count, ids, width, tokens=()):
    return launch(
        functools.partial(query_kernel, seq), "query_grad", (part, got, count, ids),
        [((ids.shape[-1], width), BF)], tokens=tokens,
    )[0]


def back_input_kernel(
    seq, gq_ref, gk_ref, gv_ref, x_ref, wq_ref, wk_ref, wv_ref, gain_ref, mid_ref, sel_ref,
    vec_in_ref, *rest,
):
    vec_ref, gx_ref, out_s, sem = rest[-4:]
    grad_query, grad_value = gq_ref[...], gv_ref[...]
    incoming = (
        dot_nt(grad_query, wq_ref[...])
        + dot_nt(gk_ref[...], wk_ref[...])
        + dot_nt(grad_value, wv_ref[...])
    )
    unit, inverse = norm_parts(x_ref[seq].astype(F32))
    grad = norm_back(incoming, unit, inverse, vector(gain_ref))
    pick = pick_rows(sel_ref[seq : seq + 1, :])
    middle = mid_ref[seq * MASK_MOST : (seq + 1) * MASK_MOST, :]
    high = middle.astype(BF)
    low = (middle - high.astype(F32)).astype(BF)
    grad = grad + (dot_tn(pick, high) + dot_tn(pick, low))
    out_s[...] = grad.astype(BF)
    copy = pltpu.make_async_copy(out_s, gx_ref.at[seq], sem)
    copy.start()
    vec_ref[...] = vec_in_ref[...]
    vec_ref[V_BQ : V_BQ + 1, :] += jnp.sum(grad_query.astype(F32), axis=0, keepdims=True)
    vec_ref[V_BV : V_BV + 1, :] += jnp.sum(grad_value.astype(F32), axis=0, keepdims=True)
    vec_ref[V_GA : V_GA + 1, :] += jnp.sum(incoming * unit, axis=0, keepdims=True)
    vec_ref[V_SA : V_SA + 1, :] += jnp.sum(incoming, axis=0, keepdims=True)
    copy.wait()


def back_input_call(seq, *args, former, tokens=()):
    args = list(args)
    x, vec = args[3], args[10]
    aliases = {}
    if former is not None:
        aliases = {len(args): 1}
        args.append(Hbm(former))
    vec, grad = launch(
        functools.partial(back_input_kernel, seq), "back_input", args, [(vec.shape, F32)],
        out_hbm=[(x.shape, BF)], tokens=tokens, aliases=aliases,
        scratch=[pltpu.VMEM(x.shape[1:], BF), pltpu.SemaphoreType.DMA],
    )
    return grad, vec


def store_chunks(out_ref, base, product, rank, per_group):
    size = product.shape[0] // per_group
    for index in range(per_group):
        out_ref[base + (index ^ (rank & (per_group - 1)))] = product[
            index * size : (index + 1) * size
        ].astype(BF)


def lanes_at(start, size):
    return pl.ds(pl.multiple_of(start * size, size), size)


def ffn_grad_kernel(ff, width, down, half, stages, here_ref, keep_ref, got_ref, *out_refs):
    rank = rank_from(here_ref, stages) & 15
    rows = ff // 8
    for index, out_ref in enumerate(out_refs):
        group = (2 * half + 1 - index) ^ (rank // 4)
        if down:
            left, right = lanes_at(group, rows), pl.ds(ff, width)
        else:
            left = lanes_at((ff + width) // rows + (group & 1), rows)
            right = lanes_at(ff // 2 // width + group // 2, width)
        product = dot_tn(keep_ref[:, left], keep_ref[:, right]) + dot_tn(
            got_ref[:, left], got_ref[:, right]
        )
        store_chunks(out_ref, 0, product, rank, 4)


def ffn_grad_call(here, stages, keep, got, ff, width, down, half, tokens=()):
    return launch(
        functools.partial(ffn_grad_kernel, ff, width, down, half, stages),
        "grad_down" if down else "grad_up", (here, keep, got),
        [((4, ff // 32, width), BF)] * 2, tokens=tokens,
    )


def pair_grad_kernel(splits, half, stages, here_ref, *refs):
    out_ref = refs[-1]
    rank = rank_from(here_ref, stages)
    rows = refs[0].shape[1] // 2
    pairs = [(refs[2 * k], refs[2 * k + 1]) for k in range(len(refs) // 2)]

    def step(index, carry):
        group = (2 * half + index) ^ (rank // 8)
        lanes = lanes_at(group & 1, rows)

        def fill(some):
            product = sum(dot_tn(left[:, lanes], right[...]) for left, right in some)
            store_chunks(out_ref, 8 * index, product, rank, 8)

        @pl.when(group < 2)
        def _():
            fill(pairs[:splits])

        @pl.when(group >= 2)
        def _():
            fill(pairs[splits:])

        return carry

    lax.fori_loop(0, 2, step, 0)


def pair_grad_call(here, stages, first, second, half, name, tokens=()):
    args = [array for pair in first + second for array in pair]
    width = args[0].shape[1]
    return launch(
        functools.partial(pair_grad_kernel, len(first), half, stages), name, (here, *args),
        [((16, width // 16, width), BF)], tokens=tokens,
    )[0]


def add_kernel(terms, *refs):
    inputs, outs = refs[:terms], refs[terms:]
    count = outs[0].shape[0]

    def step(index, carry):
        for place, out_ref in enumerate(reversed(outs)):
            total = inputs[0][place * count + index].astype(F32)
            for more in inputs[1:]:
                total = total + more[place * count + index].astype(F32)
            out_ref[index] = total.astype(BF)
        return carry

    lax.fori_loop(0, count, step, 0)


def add_call(args, parts, tokens=()):
    count, size, width = args[0].shape
    return launch(
        functools.partial(add_kernel, len(args)), "add", args,
        [((count // parts, size, width), BF)] * parts, tokens=tokens, work=SMALL,
    )


def join_kernel(keep_ref, got_ref, out_ref):
    count = keep_ref.shape[0]
    out_ref[:count] = keep_ref[...]
    out_ref[count:] = got_ref[...]


def join_call(keep, got, tokens=()):
    count, size, width = keep.shape
    return launch(
        join_kernel, "join", (keep, got), [((2 * count, size, width), BF)], tokens=tokens,
        work=SMALL,
    )[0]


def place_kernel(pieces, target, stages, here_ref, *refs):
    sources, refs = refs[: len(pieces)], refs[-target.outputs - 3 :]
    token_ref, outs, stage_s, sems = refs[0], refs[1:-2], refs[-2], refs[-1]
    token_ref[...] = jnp.zeros_like(token_ref)
    rank = rank_from(here_ref, stages)
    size = sources[0].shape[1]
    copies = []
    for index, (piece, source) in enumerate(zip(pieces, sources)):
        slot = index % 2
        if index >= 2:
            copies[index - 2].wait()

        def step(inner, carry, source=source, slot=slot):
            rows = pl.ds(pl.multiple_of(inner * size, size), size)
            stage_s[slot, rows, :] = source[inner ^ (rank & 3)].astype(F32)
            return carry

        lax.fori_loop(0, 4, step, 0)
        copies.append(target(outs, piece ^ (rank // 4), stage_s.at[slot], sems.at[slot]))
    for copy in copies[-2:]:
        copy.wait()


class Copy:
    def __init__(self, choices):
        self.choices = choices
        for chosen, copy in choices:
            if chosen is None:
                copy.start()
            else:
                pl.when(chosen)(copy.start)

    def wait(self):
        self.choices[0][1].wait()


class DownTarget:
    outputs = 1

    def __call__(self, outs, piece, source, sem):
        place = outs[0].at[lanes_at(piece, source.shape[0])]
        return Copy([(None, pltpu.make_async_copy(source, place, sem))])


class UpTarget:
    outputs = 1

    def __call__(self, outs, piece, source, sem):
        rows, width = source.shape
        place = outs[0].at[lanes_at(piece & 1, rows), lanes_at(piece // 2, width)]
        return Copy([(None, pltpu.make_async_copy(source, place, sem))])


class PairTarget:
    outputs = 2

    def __call__(self, outs, piece, source, sem):
        rows = source.shape[0]
        return Copy([
            (
                piece // 4 == matrix,
                pltpu.make_async_copy(source, outs[matrix].at[lanes_at(piece & 3, rows)], sem),
            )
            for matrix in range(2)
        ])


def swap(rows, stage):
    axis, bit = stage
    return lax.ppermute(rows, axis, [(i, i ^ bit) for i in range(lax.axis_size(axis))])


def stage_list(first):
    every = []
    for axis in ("dp", "seq"):
        every += [(axis, 1 << k) for k in range(lax.axis_size(axis).bit_length() - 1)]
    return first + [stage for stage in every if stage not in first]


class Stream:
    def __init__(self, here, stages, target, out_shapes, name):
        self.here, self.stages, self.target = here, stages, target
        self.out_shapes, self.name, self.placed = out_shapes, name, None
        self.pieces = {}

    def begin(self, sent, kept):
        self.kept = kept
        self.got = [swap(piece, self.stages[1]) for piece in sent]

    def begin_core(self, sent, kept):
        self.kept, self.got = kept, swap(sent, self.stages[0])

    def a0(self, tokens):
        first, second, third, fourth = add_call((self.kept, self.got), 4, tokens)
        self.begin((first, second), (third, fourth))
        return first

    def a1(self, tokens):
        total = add_call((self.kept[0], self.got[0]), 1, tokens)[0]
        self.more = swap(total, self.stages[2])
        return total

    def a2(self, tokens):
        send, self.kept = add_call((self.kept[1], self.got[1], self.more), 2, tokens)
        self.got = swap(send, self.stages[3])
        return send

    def a3(self, tokens):
        send, self.kept = add_call((self.kept, self.got), 2, tokens)
        self.got = swap(send, self.stages[4])
        return send

    def a4(self, tokens):
        total = add_call((self.kept, self.got), 1, tokens)[0]
        for stage in self.stages[5:]:
            total = add_call((total, swap(total, stage)), 1)[0]
        self.kept, self.got = total, swap(total, self.stages[4])
        return total

    def j4(self, tokens):
        self.kept = join_call(self.kept, self.got, tokens)
        self.got = swap(self.kept, self.stages[3])
        return self.kept

    def j3(self, tokens):
        piece = join_call(self.kept, self.got, tokens)
        core, s1, s2 = self.stages[:3]
        near = swap(piece, s2)
        self.pieces = {0: piece, 1: near, 2: swap(piece, s1), 3: swap(near, s1)}
        for number in range(4):
            self.pieces[4 + number] = swap(self.pieces[number], core)
        return piece

    def place(self, numbers, tokens):
        sources = [self.pieces[number] for number in numbers]
        _, size, width = sources[0].shape
        args = [self.here] + sources
        aliases = {}
        if self.placed is not None:
            aliases = {len(args) + index: 1 + index for index in range(len(self.placed))}
            args += [Hbm(item) for item in self.placed]
        token, *self.placed = launch(
            functools.partial(place_kernel, numbers, self.target, self.stages), self.name, args,
            [TOKEN], out_hbm=[(shape, F32) for shape in self.out_shapes], tokens=tokens,
            aliases=aliases,
            scratch=[pltpu.VMEM((2, 4 * size, width), F32), pltpu.SemaphoreType.DMA((2,))],
        )
        return token

    def p0(self, tokens):
        return self.place((0, 4), tokens)

    def p1(self, tokens):
        return self.place((1, 2, 5, 6), tokens)

    def p2(self, tokens):
        return self.place((3, 7), tokens)


def add_rows_kernel(a_ref, b_ref, out_ref):
    out_ref[...] = a_ref[...] + b_ref[...]


def add_rows_call(rows, got, tokens):
    return launch(
        add_rows_kernel, "add_rows", (rows, got), [(rows.shape, F32)], tokens=tokens, work=SMALL
    )[0]


def unpack_kernel(vec_ref, *out_refs):
    for start, out_ref in zip((V_BQ, V_BV, V_BO, V_BU, V_BD, V_GA, V_SA, V_GF, V_SF), out_refs):
        count = out_ref.shape[0] // vec_ref.shape[1]
        rows = [vec_ref[start + index : start + index + 1, :] for index in range(count)]
        out_ref[...] = jnp.concatenate(rows, axis=1).reshape(out_ref.shape[0])


def unpack_call(vec, ff):
    width = vec.shape[1]
    outs = shapes(*[((ff if index == 3 else width,), F32) for index in range(9)])
    return pl.pallas_call(
        unpack_kernel,
        in_specs=[VMEM],
        out_specs=[VMEM] * 9,
        out_shape=outs,
        compiler_params=pltpu.CompilerParams(vmem_limit_bytes=4 * 2**20),
        name="unpack",
    )(pltpu.with_memory_space_constraint(vec, pltpu.VMEM))


def from_peers(rows):
    size = lax.axis_size("seq")
    got = [
        lax.ppermute(rows, "seq", [(i, (i + shift) % size) for i in range(size)])
        for shift in range(1, size)
    ]
    return jnp.stack(got)


def shards(
    inputs, cluster_ids, masked, cotangent,
    w_query, w_key, w_value, w_out, w_up, w_down,
    bias_query, bias_value, bias_out, bias_up, bias_down,
    gain_attn, shift_attn, gain_ffn, shift_ffn,
):
    seqs, tokens, width = inputs.shape
    every = range(seqs)
    ff = w_up.shape[1]
    core, x, y = ("dp", 1), ("dp", 2), ("seq", 1)
    z = ("dp", lax.axis_size("dp") // 4)
    stages_a = stage_list([core, x, y])
    stages_b = stage_list([core, z, y, x])
    stages_c = stage_list([core, y, z, x])
    stages_d = stage_list([core, x, y])
    here = Scalar(jnp.stack([lax.axis_index("dp"), lax.axis_index("seq")]).astype(jnp.int32))
    ids = cluster_ids.transpose(1, 0, 2)

    fetched = [
        Hbm(item)
        for item in (
            inputs, ids, w_query, w_key, w_value, bias_query, bias_value, gain_attn, shift_attn,
            masked,
        )
    ]
    more = [cotangent, w_out, w_up, w_down, bias_out, bias_down, gain_ffn, shift_ffn, bias_up]
    projected, sel = [], None
    for s in every:
        results, fetched, brought, found = project_call(
            s, here, fetched, more if s == seqs - 1 else []
        )
        projected.append(results)
        sel = found if s == 0 else sel
    normed, keys, values, own, message = zip(*projected)
    x_v, ids_v, wq_v, wk_v, wv_v, _, _, gain_v, _, _ = fetched
    cot_v, wo_v, wu_v, wd_v, bo_v, bd_v, gf_v, sf_v, _, up_rows = brought
    got = [from_peers(item) for item in message]
    attended, tokens_in = [], ()
    for s in every:
        attended.append(
            attend_call(own[s], message[s], got[s], keys[s], values[s], tokens=tokens_in)
        )
        tokens_in = (attended[s][1],)
    cent, count, out, lse, send = zip(*attended)
    got = [from_peers(item) for item in send]
    merges = []
    for s in every:
        merges.append(
            merge_call(s, out[s], lse[s], got[s], x_v, cot_v, sel, ids_v, tokens=tokens_in)
        )
        tokens_in = (merges[s][2],)
    ctx, merged, lse_all, ctx_m, x_m, cot_m = zip(*merges)
    (keep, away, ctx_m, attn_m, mid_m, vec), own, message = masked_call(
        here, sel, ids_v, ctx_m, x_m, cot_m, wo_v, wu_v, wd_v, bo_v, up_rows, gf_v, sf_v
    )
    got_grad = [from_peers(item) for item in message]
    other = swap(away, core)
    weights = (wo_v, wu_v, wd_v, bo_v, up_rows, bd_v, gf_v, sf_v)
    blocks = [(s, start) for s in every for start in range(0, tokens, 256)]
    block_out = None

    def forward(*earlier):
        nonlocal block_out
        if blocks:
            s, start = blocks.pop(0)
            token, block_out = forward_call(s, start, x_v, ctx[s], weights, block_out, earlier)
            return token
        return earlier[0]

    a = Stream(here, stages_a, DownTarget(), [(ff, width)], "place_down")
    b = Stream(here, stages_b, UpTarget(), [(width, ff)], "place_up")
    c = Stream(here, stages_c, PairTarget(), [(width, width)] * 2, "place_out_value")
    d = Stream(here, stages_d, PairTarget(), [(width, width)] * 2, "place_key_query")
    back = {}
    waiting = {}
    grad_input = None

    def ffn_grads(stream, down, half):
        def act(tokens):
            waiting[stream, half] = ffn_grad_call(
                here, stream.stages, keep, other, ff, width, down, half, tokens
            )
            if half == 0:
                stream.begin(waiting[stream, 1], waiting[stream, 0])
            return waiting[stream, half][0]

        return act

    def pair_grads(stream, name, half):
        def act(tokens):
            if stream is c:
                first = [(ctx_m, attn_m)]
                second = [(normed[s], back[s][1]) for s in every]
            else:
                first = [(normed[s], back[s][0]) for s in every]
                second = [(normed[s], waiting["query", s]) for s in every]
            result = pair_grad_call(here, stream.stages, first, second, half, name, tokens)
            waiting[stream, half] = result
            if half == 0:
                stream.begin_core(waiting[stream, 1], result)
            return result

        return act

    def attend_back(s):
        def act(tokens):
            back[s] = attend_back_call(
                cent[s], lse_all[s], merged[s], own[s], got_grad[s], keys[s], values[s],
                tokens=tokens,
            )
            waiting["part", s] = from_peers(back[s][3])
            return back[s][3]

        return act

    def query(s):
        def act(tokens):
            waiting["query", s] = query_call(
                s, back[s][2], waiting["part", s], count[s], ids_v, width, tokens
            )
            return waiting["query", s]

        return act

    def back_input(s):
        def act(tokens):
            nonlocal grad_input, vec
            grad_input, vec = back_input_call(
                s, waiting["query", s], back[s][0], back[s][1], x_v, wq_v, wk_v, wv_v, gain_v, mid_m,
                sel, vec, former=grad_input, tokens=tokens,
            )
            return vec

        return act

    def forward_step(tokens):
        return forward(*tokens)

    def vector_step(stage):
        def act(tokens):
            nonlocal vec
            vec = add_rows_call(vec, waiting["vec"], tokens)
            place = stages_a.index(stage) + 1
            waiting["vec"] = swap(vec, stages_a[place]) if place < len(stages_a) else None
            return vec

        return act

    def vector_first(tokens):
        waiting["vec"] = swap(vec, stages_a[0])
        return tokens[0]

    def all_seqs(make):
        return [make(s) for s in every]

    def streams(*steps):
        return [getattr(stream, step) for stream, step in steps]

    order = (
        [forward_step, ffn_grads(a, True, 1), ffn_grads(a, True, 0)]
        + [ffn_grads(b, False, 1), ffn_grads(b, False, 0)]
        + all_seqs(attend_back)
        + streams((a, "a1"), (b, "a1"))
        + [pair_grads(c, "grad_out_value", 1), pair_grads(c, "grad_out_value", 0)]
        + all_seqs(query)
        + [pair_grads(d, "grad_key_query", 1), pair_grads(d, "grad_key_query", 0)]
        + streams((c, "a0"), (a, "a2"), (d, "a0"))
        + all_seqs(back_input)
        + [vector_first]
        + streams((b, "a2"), (a, "a3"), (d, "a1"))
        + [vector_step(stages_a[0])]
        + streams((c, "a1"))
        + [forward_step]
        + streams((b, "a3"), (a, "a4"))
        + [vector_step(stages_a[1])]
        + streams((d, "a2"), (c, "a2"))
        + [vector_step(stages_a[2]), forward_step]
        + streams((b, "a4"), (c, "a3"), (a, "j4"), (d, "a3"))
        + [vector_step(stages_a[3])]
        + [forward_step] * len(blocks)
        + streams((b, "j4"), (c, "a4"), (a, "j3"), (d, "a4"), (b, "j3"), (c, "j4"))
        + streams((a, "p0"), (d, "j4"), (b, "p0"))
        + [vector_step(stage) for stage in stages_a[4:]]
        + streams((c, "j3"), (a, "p1"), (d, "j3"), (b, "p1"), (c, "p0"), (a, "p2"), (d, "p0"))
        + streams((c, "p1"), (b, "p2"), (c, "p2"), (d, "p1"), (d, "p2"))
    )
    last = vec
    for step in order:
        last = step((last,))
    (grad_w_down,), (grad_w_up,) = a.placed, b.placed
    grad_w_out, grad_w_value = c.placed
    grad_w_key, grad_w_query = d.placed
    return (
        block_out, grad_input,
        grad_w_query, grad_w_key, grad_w_value, grad_w_out, grad_w_up, grad_w_down,
        *unpack_call(vec, ff),
    )


def solution(mesh):
    rows = P("dp", "seq", None)
    return jax.shard_map(
        shards,
        mesh=mesh,
        in_specs=(rows, P("dp", None, "seq"), P("dp", "seq"), rows) + (P(),) * 15,
        out_specs=(rows, rows) + (P(),) * 15,
        check_vma=False,
    )
```

```python
import functools

import jax
import jax.numpy as jnp
from jax import lax
from jax.experimental import pallas as pl
from jax.experimental.pallas import tpu as pltpu
from jax.sharding import PartitionSpec as P

HEADS = 12
HDIM = 64
CLUSTERS = 100
MASK_MOST = 128
PAIRS = HEADS // 2
LANES = 2 * HDIM
ROWS = 112
SCALE = HDIM**-0.5
EPS = 1e-05
BF = jnp.bfloat16
F32 = jnp.float32

V_BQ, V_BV, V_BO, V_BU, V_BD, V_GA, V_SA, V_GF, V_SF = 0, 1, 2, 3, 7, 8, 9, 10, 11
VEC_ROWS = 16


def dot(a, b):
    return lax.dot_general(a, b, (((1,), (0,)), ((), ())), preferred_element_type=F32)


def dot_nt(a, b):
    return lax.dot_general(a, b, (((1,), (1,)), ((), ())), preferred_element_type=F32)


def dot_tn(a, b):
    return lax.dot_general(a, b, (((0,), (0,)), ((), ())), preferred_element_type=F32)


def norm_parts(rows):
    center = rows - jnp.mean(rows, axis=-1, keepdims=True)
    inverse = lax.rsqrt(jnp.mean(center * center, axis=-1, keepdims=True) + EPS)
    return center * inverse, inverse


def norm_back(incoming, unit, inverse, gain):
    scaled = incoming * gain
    return inverse * (
        scaled
        - jnp.mean(scaled, axis=-1, keepdims=True)
        - unit * jnp.mean(scaled * unit, axis=-1, keepdims=True)
    )


def normal_cdf(upper):
    return 0.5 * (1.0 + lax.erf(upper * (0.5**0.5)))


def lane_of(rows):
    return lax.broadcasted_iota(jnp.int32, (rows, LANES), 1)


def column(slab, index):
    picked = jnp.where(lane_of(slab.shape[0]) == index, slab, 0.0)
    return jnp.sum(picked, axis=1, keepdims=True)


def member_pair(ids, seq, pair):
    tokens = ids.shape[-1]
    rows = lax.broadcasted_iota(jnp.int32, (ROWS, tokens), 0)
    one = [
        jnp.where(rows == ids[2 * pair + side, seq : seq + 1, :], 1.0, 0.0).astype(BF)
        for side in range(2)
    ]
    return jnp.concatenate(one, axis=0)


def row_blocks(rows, act, block=256):
    def step(index, carry):
        act(pl.ds(pl.multiple_of(index * block, block), block))
        return carry

    lax.fori_loop(0, rows // block, step, 0)


def vector(ref):
    return ref[...].astype(F32).reshape(1, -1)


def pick_rows(sel):
    slots = lax.broadcasted_iota(jnp.int32, (MASK_MOST, sel.shape[-1]), 0)
    return jnp.where(slots == sel, 1.0, 0.0).astype(BF)


def stack_pair(both):
    left = lane_of(both.shape[0]) < HDIM
    return jnp.concatenate(
        [jnp.where(left, both, 0.0).astype(BF), jnp.where(left, 0.0, both).astype(BF)], axis=0
    )


def unstack_pair(stacked):
    left = lane_of(ROWS) < HDIM
    return jnp.where(left, stacked[:ROWS], stacked[ROWS:])


def pair_lanes(pair):
    return pl.ds(pl.multiple_of(pair * LANES, LANES), LANES)


class Hbm:
    def __init__(self, array):
        self.array = array


class Scalar:
    def __init__(self, array):
        self.array = array


def rank_from(here_ref, stages):
    rank = 0
    for place, (axis, bit) in enumerate(stages[:5]):
        index = here_ref[0 if axis == "dp" else 1]
        rank = rank + ((index >> (bit.bit_length() - 1)) & 1) * (16 >> place)
    return rank


def shapes(*items):
    return [jax.ShapeDtypeStruct(shape, dtype) for shape, dtype in items]


WORK = dict(
    project=5.0, attend=5.0, merge=5.0, masked_rows=5.0, forward_rows=5.0, attend_back=5.0,
    query_grad=5.0, back_input=10.283, grad_down=5.0, grad_up=5.0, grad_out_value=5.0,
    grad_key_query=17.445, add=1.0, join=1.0, add_rows=1.0, place_down=5.0, place_up=5.0,
    place_out_value=8.151, place_key_query=16.247,
)
TOKEN = ((8, LANES), F32)
VMEM = pl.BlockSpec(memory_space=pltpu.VMEM)
HBM = pl.BlockSpec(memory_space=pltpu.HBM)
ANY = pl.BlockSpec(memory_space=pl.ANY)


def launch(kernel, name, args, outs, out_hbm=(), tokens=(), scratch=(), mib=16, aliases=None):
    count = len(tokens)
    operands, in_specs = list(tokens), [ANY] * count
    for arg in args:
        if isinstance(arg, Hbm):
            operands.append(pltpu.with_memory_space_constraint(arg.array, pltpu.HBM))
            in_specs.append(HBM)
        elif isinstance(arg, Scalar):
            operands.append(arg.array)
            in_specs.append(pl.BlockSpec(memory_space=pltpu.SMEM))
        else:
            operands.append(pltpu.with_memory_space_constraint(arg, pltpu.VMEM))
            in_specs.append(VMEM)
    out_shape = [pltpu.VMEM(shape, dtype) for shape, dtype in outs] + shapes(*out_hbm)
    return pl.pallas_call(
        lambda *refs: kernel(*refs[count:]),
        in_specs=in_specs,
        out_specs=[VMEM] * len(outs) + [HBM] * len(out_hbm),
        out_shape=out_shape,
        scratch_shapes=list(scratch),
        input_output_aliases={count + a: b for a, b in (aliases or {}).items()},
        compiler_params=pltpu.CompilerParams(vmem_limit_bytes=mib * 2**20),
        cost_estimate=pl.CostEstimate(
            flops=int(WORK[name] * 1e9), bytes_accessed=0, transcendentals=0
        ),
        name=name,
    )(*operands)


def load(pairs, sems):
    copies = [
        pltpu.make_async_copy(source, target, sems.at[index])
        for index, (source, target) in enumerate(pairs)
    ]
    for copy in copies:
        copy.start()
    return copies


def project_rows(
    seq, x, ids_ref, wq_ref, wk_ref, wv_ref, bq_ref, bv_ref, gain_ref, shift_ref,
    masked_ref, normed_ref, key_ref, value_ref, own_ref, message_ref, sel_ref, query_s, ready,
):
    ready("x")
    if sel_ref is not None:
        tokens = masked_ref.shape[1]
        before = jnp.where(
            lax.broadcasted_iota(jnp.int32, (tokens, tokens), 0)
            <= lax.broadcasted_iota(jnp.int32, (tokens, tokens), 1),
            1.0,
            0.0,
        ).astype(BF)
        for s in range(masked_ref.shape[0]):
            row = masked_ref[s : s + 1, :]
            spread = jnp.broadcast_to(row.astype(F32), (16, tokens)).astype(BF)
            slot = dot(spread, before)[:1].astype(jnp.int32) - 1
            sel_ref[s : s + 1, :] = jnp.where(row == 1, slot, -1)
    length = normed_ref.shape[0]

    def norm(rows):
        unit, _ = norm_parts(x[seq, rows, :].astype(F32))
        normed_ref[rows, :] = (unit * vector(gain_ref) + vector(shift_ref)).astype(BF)

    def query(rows):
        query_s[rows, :] = (dot(normed_ref[rows, :], wq_ref[...]) + vector(bq_ref)).astype(BF)

    def key_value(rows):
        normed = normed_ref[rows, :]
        key_ref[rows, :] = dot(normed, wk_ref[...]).astype(BF)
        value_ref[rows, :] = (dot(normed, wv_ref[...]) + vector(bv_ref)).astype(BF)

    row_blocks(length, norm)
    ready("q")
    row_blocks(length, query)
    lane = lane_of(ROWS)
    ones = jnp.ones((length, LANES), BF)

    def step(pair, slab):
        right = jnp.concatenate([query_s[:, pair_lanes(pair)], ones], axis=1)
        sums = dot(member_pair(ids_ref, seq, pair), right)
        own = unstack_pair(sums[:, :LANES])
        own_ref[pair] = own
        message_ref[pair] = own.astype(BF)
        for side in range(2):
            count = sums[side * ROWS : (side + 1) * ROWS, LANES:]
            low = jnp.minimum(count, 256.0)
            slab = slab + jnp.where(lane == 2 * pair + side, low, 0.0)
            slab = slab + jnp.where(lane == 16 + 2 * pair + side, count - low, 0.0)
        return slab

    slab = lax.fori_loop(0, PAIRS, step, jnp.zeros((ROWS, LANES), F32), unroll=2)
    message_ref[PAIRS] = slab.astype(BF)
    ready("kv")
    row_blocks(length, key_value)


SLAB = (PAIRS, ROWS, LANES)
SLAB_MORE = (PAIRS + 1, ROWS, LANES)


def project_outs(x):
    _, tokens, width = x.shape
    rows = ((tokens, width), BF)
    return [rows, rows, rows, (SLAB, F32), (SLAB_MORE, BF)], [pltpu.VMEM((tokens, width), BF)]


def project_call(seq, here, fetched, more):
    first = isinstance(fetched[0], Hbm)
    brought = [item.array for item in fetched] if first else []
    x = brought[0] if first else fetched[0]
    outs, scratch = project_outs(x)
    seqs = x.shape[0]
    count, extra = len(fetched), len(more)
    loads = count + seqs - 1 if first else 0
    own_outs = 6 if first else 5
    if first:
        outs = outs + [((seqs, x.shape[1]), jnp.int32)]

    def kernel(here_ref, *refs):
        sources, refs = refs[:count], refs[count:]
        more_in, refs = refs[:extra], refs[extra:]
        results, refs = refs[:own_outs], refs[own_outs:]
        targets, refs = (refs[:count], refs[count:]) if first else (sources, refs)
        more_out, refs = refs[:extra], refs[extra:]
        row_ref, refs = (refs[0], refs[1:]) if extra else (None, refs)
        query_s, sems = refs
        results = tuple(results) + (() if first else (None,))
        pairs = []
        if first:
            order = [seq] + [s for s in range(seqs) if s != seq]
            rows = [(sources[0].at[s], targets[0].at[s]) for s in order]
            pairs = [rows[0]] + list(zip(sources[1:], targets[1:])) + rows[1:]
        pairs = pairs + list(zip(more_in, more_out))
        copies = load(pairs, sems)
        groups = {"x": [], "q": [], "kv": []}
        if first:
            groups = {"x": [0, 7, 8, 9], "q": [1, 2, 5], "kv": [3, 4, 6]}
        waited = set()

        def ready(name):
            for index in groups[name]:
                copies[index].wait()
                waited.add(index)

        project_rows(seq, *targets, *results, query_s, ready)
        for index, copy in enumerate(copies):
            if index not in waited:
                copy.wait()
        if extra:
            row_ref[...] = vector(more_out[-1])

    brings = [(item.shape, item.dtype) for item in brought] + [
        (item.shape, item.dtype) for item in more
    ]
    if extra:
        brings.append(((1, more[-1].shape[0]), F32))
    results = launch(
        kernel, "project", [here] + list(fetched) + [Hbm(item) for item in more], outs + brings,
        scratch=scratch + [pltpu.SemaphoreType.DMA((loads + extra,))],
    )
    if first:
        return results[:5], results[6 : 6 + count], results[6 + count :], results[5]
    return results[:5], fetched, results[5:], None


def attend_kernel(
    own_ref, message_ref, got_ref, key_ref, value_ref,
    cent_ref, count_ref, out_ref, lse_ref, send_ref,
):
    peers = got_ref.shape[0]
    lane = lane_of(ROWS)
    slab = message_ref[PAIRS].astype(F32)
    for peer in range(peers):
        slab = slab + got_ref[peer, PAIRS].astype(F32)
    count = jnp.maximum(slab + pltpu.roll(slab, LANES - 16, 1), 1.0)
    count_ref[...] = count

    def step(pair, lses):
        total = own_ref[pair]
        for peer in range(peers):
            total = total + got_ref[peer, pair].astype(F32)
        divisor = jnp.where(lane < HDIM, column(count, 2 * pair), column(count, 2 * pair + 1))
        cent = (total / divisor).astype(BF)
        cent_ref[pair] = cent
        scores = dot_nt(stack_pair(cent.astype(F32)), key_ref[:, pair_lanes(pair)]) * SCALE
        peak = jnp.max(scores, axis=1, keepdims=True)
        raised = jnp.exp(scores - peak)
        mass = jnp.sum(raised, axis=1, keepdims=True)
        mixed = unstack_pair(dot(raised.astype(BF), value_ref[:, pair_lanes(pair)]) / mass)
        out_ref[pair] = mixed
        send_ref[pair] = mixed.astype(BF)
        lse = peak + jnp.log(mass)
        lses = lses + jnp.where(lane == 2 * pair, lse[:ROWS], 0.0)
        return lses + jnp.where(lane == 2 * pair + 1, lse[ROWS:], 0.0)

    lses = lax.fori_loop(0, PAIRS, step, jnp.zeros((ROWS, LANES), F32), unroll=2)
    lse_ref[...] = lses
    high = lses.astype(BF).astype(F32)
    rest = lses - high
    middle = rest.astype(BF).astype(F32)
    low = (rest - middle).astype(BF).astype(F32)
    send_ref[PAIRS] = (high + pltpu.roll(middle, 16, 1) + pltpu.roll(low, 32, 1)).astype(BF)


def attend_call(*args, tokens=()):
    one = ((ROWS, LANES), F32)
    return launch(
        attend_kernel, "attend", args, [(SLAB, BF), one, (SLAB, F32), one, (SLAB_MORE, BF)],
        tokens=tokens,
    )


def merge_kernel(
    seq, out_ref, lse_ref, got_ref, x_ref, cot_ref, sel_ref, ids_ref,
    ctx_ref, merged_ref, lse_all_ref, ctx_m_ref, x_m_ref, cot_m_ref, ids_m_ref,
):
    peers = got_ref.shape[0]
    lane = lane_of(ROWS)
    lses = [lse_ref[...]]
    for peer in range(peers):
        slab = got_ref[peer, PAIRS].astype(F32)
        lses.append(slab + pltpu.roll(slab, LANES - 16, 1) + pltpu.roll(slab, LANES - 32, 1))
    peak = functools.reduce(jnp.maximum, lses)
    merged = peak + jnp.log(sum(jnp.exp(item - peak) for item in lses))
    lse_all_ref[...] = merged
    portions = [jnp.exp(item - merged) for item in lses]

    def gather(pair, carry):
        total = jnp.zeros((ROWS, LANES), F32)
        for index, portion in enumerate(portions):
            part = out_ref[pair] if index == 0 else got_ref[index - 1, pair].astype(F32)
            weight = jnp.where(
                lane < HDIM, column(portion, 2 * pair), column(portion, 2 * pair + 1)
            )
            total = total + weight * part
        merged_ref[pair] = total
        member = member_pair(ids_ref, seq, pair)
        ctx_ref[:, pair_lanes(pair)] = dot_tn(member, stack_pair(total)).astype(BF)
        return carry

    lax.fori_loop(0, PAIRS, gather, 0, unroll=2)
    pick = pick_rows(sel_ref[seq : seq + 1, :])
    ctx_m_ref[...] = dot(pick, ctx_ref[...]).astype(BF)
    x_m_ref[...] = dot(pick, x_ref[seq]).astype(BF)
    cot_m_ref[...] = dot(pick, cot_ref[seq]).astype(BF)
    heads = [ids_ref[head, seq : seq + 1, :].astype(F32) for head in range(HEADS)]
    heads = jnp.concatenate(heads + [jnp.zeros_like(heads[0])] * (16 - HEADS), axis=0)
    ids_m_ref[...] = dot_nt(heads.astype(BF), pick).astype(jnp.int32)


def merge_call(seq, out, lse, got, x, cot, sel, ids, tokens=()):
    _, length, width = x.shape
    picked = ((MASK_MOST, width), BF)
    return launch(
        functools.partial(merge_kernel, seq), "merge", (out, lse, got, x, cot, sel, ids),
        [((length, width), BF), (SLAB, F32), ((ROWS, LANES), F32), picked, picked, picked,
            ((16, MASK_MOST), jnp.int32)],
        tokens=tokens,
    )


def masked_kernel(seqs, *refs):
    here_ref, ids_refs = refs[0], refs[1 : 1 + seqs]
    rest = refs[1 + seqs :]
    ctx_refs, x_refs, cot_refs = rest[:seqs], rest[seqs : 2 * seqs], rest[2 * seqs : 3 * seqs]
    (
        wo_ref, wu_ref, wd_ref, bo_ref, bu_ref, gain_ref, shift_ref,
        keep_ref, send_ref, ctx_m_ref, attn_m_ref, mid_m_ref, vec_ref,
    ) = rest[3 * seqs : 3 * seqs + 13]
    rest = rest[3 * seqs + 13 :]
    own_refs, message_refs = rest[:seqs], rest[seqs : 2 * seqs]
    middle_s, back_s = rest[2 * seqs :]
    width = wo_ref.shape[0]
    ff_block = width
    ff_blocks = wu_ref.shape[1] // ff_block
    half_blocks = ff_blocks // 2
    tail = 2 * half_blocks * ff_block
    core = here_ref[0] & 1
    vec_ref[...] = jnp.zeros_like(vec_ref)
    for s in range(seqs):
        rows = pl.ds(s * MASK_MOST, MASK_MOST)
        ctx_m_ref[rows, :] = ctx_refs[s][...]
        middle_s[rows, :] = x_refs[s][...].astype(F32)
        keep_ref[rows, tail : tail + width] = cot_refs[s][...]
        send_ref[rows, tail : tail + width] = cot_refs[s][...]
    middle = middle_s[...] + (dot(ctx_m_ref[...], wo_ref[...]) + vector(bo_ref))
    middle_s[...] = middle
    unit, _ = norm_parts(middle)
    low = (unit * vector(gain_ref) + vector(shift_ref)).astype(BF)
    keep_ref[:, tail + width :] = low
    send_ref[:, tail + width :] = low
    back_s[...] = jnp.zeros_like(back_s)

    def feed(block, carry):
        lanes = pl.ds(pl.multiple_of(block * ff_block, ff_block), ff_block)
        upper = dot(keep_ref[:, tail + width :], wu_ref[:, lanes]) + bu_ref[:, lanes]
        cdf = normal_cdf(upper)
        hidden = (upper * cdf).astype(BF)
        slope = cdf + upper * (jnp.exp(-0.5 * upper * upper) * 0.3989422804014327)
        grad_y = keep_ref[:, tail : tail + width]
        grad_upper = (dot_nt(grad_y, wd_ref[lanes, :]) * slope).astype(BF)
        back_s[...] += dot_nt(grad_upper, wu_ref[:, lanes])
        vec_ref[pl.ds(V_BU + block, 1), :] = jnp.sum(
            grad_upper.astype(F32), axis=0, keepdims=True
        )
        half = block // half_blocks
        inner = block - half * half_blocks
        first = pl.ds(pl.multiple_of(inner * ff_block, ff_block), ff_block)
        second = pl.ds(
            pl.multiple_of(inner * ff_block + half_blocks * ff_block, ff_block), ff_block
        )

        @pl.when(half == core)
        def _():
            keep_ref[:, first] = hidden
            keep_ref[:, second] = grad_upper

        @pl.when(half != core)
        def _():
            send_ref[:, first] = hidden
            send_ref[:, second] = grad_upper

        return carry

    lax.fori_loop(0, ff_blocks, feed, 0, unroll=1)
    unit, inverse = norm_parts(middle_s[...])
    incoming = back_s[...]
    grad_y = keep_ref[:, tail : tail + width].astype(F32)
    grad_middle = grad_y + norm_back(incoming, unit, inverse, vector(gain_ref))
    mid_m_ref[...] = grad_middle
    grad_attn = grad_middle.astype(BF)
    attn_m_ref[...] = grad_attn
    vec_ref[V_BD : V_BD + 1, :] = jnp.sum(grad_y, axis=0, keepdims=True)
    vec_ref[V_BO : V_BO + 1, :] = jnp.sum(grad_attn.astype(F32), axis=0, keepdims=True)
    vec_ref[V_GF : V_GF + 1, :] = jnp.sum(incoming * unit, axis=0, keepdims=True)
    vec_ref[V_SF : V_SF + 1, :] = jnp.sum(incoming, axis=0, keepdims=True)
    back_s[...] = dot_nt(grad_attn, wo_ref[...])
    for s in range(seqs):
        clusters = lax.broadcasted_iota(jnp.int32, (ROWS, MASK_MOST), 0)

        def scatter(pair, carry, s=s, clusters=clusters):
            sides = [
                jnp.where(clusters == ids_refs[s][pl.ds(2 * pair + side, 1), :], 1.0, 0.0)
                for side in range(2)
            ]
            member = jnp.concatenate(sides, axis=0).astype(BF)
            rows = back_s[s * MASK_MOST : (s + 1) * MASK_MOST, pair_lanes(pair)]
            high = rows.astype(BF)
            low = (rows - high.astype(F32)).astype(BF)
            own = unstack_pair(dot(member, high) + dot(member, low))
            own_refs[s][pair] = own
            message_refs[s][pair] = own.astype(BF)
            return carry

        lax.fori_loop(0, PAIRS, scatter, 0, unroll=2)


def masked_call(here, ids, ctx, x, cot, *weights):
    seqs = len(ctx)
    width, ff = weights[1].shape
    picked = seqs * MASK_MOST
    wide = ((picked, ff + 2 * width), BF)
    out = launch(
        functools.partial(masked_kernel, seqs), "masked_rows",
        (here, *ids, *ctx, *x, *cot, *weights),
        [
            wide, wide, ((picked, width), BF), ((picked, width), BF), ((picked, width), F32),
            ((VEC_ROWS, width), F32), *[(SLAB, F32)] * seqs, *[(SLAB, BF)] * seqs,
        ],
        scratch=[pltpu.VMEM((picked, width), F32), pltpu.VMEM((picked, width), F32)],
    )
    return out[:6], out[6 : 6 + seqs], out[6 + seqs :]


def forward_kernel(
    seq, start, x_ref, ctx_ref, wo_ref, wu_ref, wd_ref, bo_ref, bu_ref, bd_ref, gain_ref, shift_ref,
    *rest,
):
    token_ref, y_ref, low_s, total_s, out_s, sem = rest[-6:]
    token_ref[...] = jnp.zeros_like(token_ref)
    rows = pl.ds(start, low_s.shape[0])
    middle = x_ref[seq, rows, :].astype(F32) + (dot(ctx_ref[rows, :], wo_ref[...]) + vector(bo_ref))
    unit, _ = norm_parts(middle)
    low_s[...] = (unit * vector(gain_ref) + vector(shift_ref)).astype(BF)
    total_s[...] = middle + vector(bd_ref)
    block = x_ref.shape[2]

    def feed(index, carry):
        lanes = pl.ds(pl.multiple_of(index * block, block), block)
        upper = dot(low_s[...], wu_ref[:, lanes]) + bu_ref[:, lanes]
        hidden = (upper * normal_cdf(upper)).astype(BF)
        total_s[...] += dot(hidden, wd_ref[lanes, :])
        return carry

    lax.fori_loop(0, wu_ref.shape[1] // block, feed, 0, unroll=1)
    out_s[...] = total_s[...].astype(BF)
    copy = pltpu.make_async_copy(out_s, y_ref.at[seq, rows], sem)
    copy.start()
    copy.wait()


def forward_call(seq, start, x, ctx, weights, former, tokens, block=256):
    width = x.shape[2]
    args = [x, ctx, *weights]
    aliases = {}
    if former is not None:
        aliases = {len(args): 1}
        args.append(Hbm(former))
    return launch(
        functools.partial(forward_kernel, seq, start), "forward_rows", args, [TOKEN],
        out_hbm=[(x.shape, BF)], tokens=tokens, aliases=aliases,
        scratch=[
            pltpu.VMEM((block, width), BF), pltpu.VMEM((block, width), F32),
            pltpu.VMEM((block, width), BF), pltpu.SemaphoreType.DMA,
        ],
    )


def attend_back_kernel(
    cent_ref, lse_ref, merged_ref, own_ref, got_ref, key_ref, value_ref,
    grad_key_ref, grad_value_ref, part_ref, send_ref,
):
    peers = got_ref.shape[0]
    lane = lane_of(ROWS)
    lses = lse_ref[...]

    def step(pair, carry):
        total = own_ref[pair]
        for peer in range(peers):
            total = total + got_ref[peer, pair].astype(F32)
        grad_cent = total.astype(BF).astype(F32)
        product = grad_cent * merged_ref[pair]
        delta = jnp.concatenate(
            [
                jnp.sum(jnp.where(lane < HDIM, product, 0.0), axis=1, keepdims=True),
                jnp.sum(jnp.where(lane < HDIM, 0.0, product), axis=1, keepdims=True),
            ],
            axis=0,
        )
        lse = jnp.concatenate([column(lses, 2 * pair), column(lses, 2 * pair + 1)], axis=0)
        cents = stack_pair(cent_ref[pair].astype(F32))
        grads = stack_pair(grad_cent)
        keys = key_ref[:, pair_lanes(pair)]
        weights = jnp.exp(dot_nt(cents, keys) * SCALE - lse)
        grad_weights = dot_nt(grads, value_ref[:, pair_lanes(pair)])
        grad_scores = (weights * (grad_weights - delta)).astype(BF)
        part = unstack_pair(dot(grad_scores, keys))
        part_ref[pair] = part
        send_ref[pair] = part.astype(BF)
        grad_key_ref[:, pair_lanes(pair)] = (dot_tn(grad_scores, cents) * SCALE).astype(BF)
        grad_value_ref[:, pair_lanes(pair)] = dot_tn(weights.astype(BF), grads).astype(BF)
        return carry

    lax.fori_loop(0, PAIRS, step, 0, unroll=2)


def attend_back_call(*args, tokens=()):
    rows = (args[5].shape, BF)
    return launch(
        attend_back_kernel, "attend_back", args, [rows, rows, (SLAB, F32), (SLAB, BF)],
        tokens=tokens,
    )


def query_kernel(seq, part_ref, got_ref, count_ref, ids_ref, gq_ref):
    peers = got_ref.shape[0]
    lane = lane_of(ROWS)
    count = count_ref[...]

    def step(pair, carry):
        total = part_ref[pair]
        for peer in range(peers):
            total = total + got_ref[peer, pair].astype(F32)
        grad_cent = (total * SCALE).astype(BF).astype(F32)
        divisor = jnp.where(lane < HDIM, column(count, 2 * pair), column(count, 2 * pair + 1))
        spread = stack_pair(grad_cent / divisor)
        member = member_pair(ids_ref, seq, pair)
        gq_ref[:, pair_lanes(pair)] = dot_tn(member, spread).astype(BF)
        return carry

    lax.fori_loop(0, PAIRS, step, 0, unroll=2)


def query_call(seq, part, got, count, ids, width, tokens=()):
    return launch(
        functools.partial(query_kernel, seq), "query_grad", (part, got, count, ids),
        [((ids.shape[-1], width), BF)], tokens=tokens,
    )[0]


def back_input_kernel(
    seq, gq_ref, gk_ref, gv_ref, x_ref, wq_ref, wk_ref, wv_ref, gain_ref, mid_ref, sel_ref,
    vec_in_ref, *rest,
):
    vec_ref, gx_ref, out_s, sem = rest[-4:]
    vec_ref[...] = vec_in_ref[...]
    middle = mid_ref[seq * MASK_MOST : (seq + 1) * MASK_MOST, :]
    high = middle.astype(BF)
    low = (middle - high.astype(F32)).astype(BF)

    def act(rows):
        grad_query, grad_value = gq_ref[rows, :], gv_ref[rows, :]
        incoming = (
            dot_nt(grad_query, wq_ref[...])
            + dot_nt(gk_ref[rows, :], wk_ref[...])
            + dot_nt(grad_value, wv_ref[...])
        )
        unit, inverse = norm_parts(x_ref[seq, rows, :].astype(F32))
        grad = norm_back(incoming, unit, inverse, vector(gain_ref))
        pick = pick_rows(sel_ref[seq : seq + 1, rows])
        out_s[rows, :] = (grad + (dot_tn(pick, high) + dot_tn(pick, low))).astype(BF)
        vec_ref[V_BQ : V_BQ + 1, :] += jnp.sum(grad_query.astype(F32), axis=0, keepdims=True)
        vec_ref[V_BV : V_BV + 1, :] += jnp.sum(grad_value.astype(F32), axis=0, keepdims=True)
        vec_ref[V_GA : V_GA + 1, :] += jnp.sum(incoming * unit, axis=0, keepdims=True)
        vec_ref[V_SA : V_SA + 1, :] += jnp.sum(incoming, axis=0, keepdims=True)

    row_blocks(gq_ref.shape[0], act)
    copy = pltpu.make_async_copy(out_s, gx_ref.at[seq], sem)
    copy.start()
    copy.wait()


def back_input_call(seq, *args, former, tokens=()):
    args = list(args)
    x, vec = args[3], args[10]
    aliases = {}
    if former is not None:
        aliases = {len(args): 1}
        args.append(Hbm(former))
    vec, grad = launch(
        functools.partial(back_input_kernel, seq), "back_input", args, [(vec.shape, F32)],
        out_hbm=[(x.shape, BF)], tokens=tokens, aliases=aliases,
        scratch=[pltpu.VMEM(x.shape[1:], BF), pltpu.SemaphoreType.DMA],
    )
    return grad, vec


def store_chunks(out_ref, base, product, rank, per_group):
    size = product.shape[0] // per_group
    for index in range(per_group):
        out_ref[base + (index ^ (rank & (per_group - 1)))] = product[
            index * size : (index + 1) * size
        ].astype(BF)


def lanes_at(start, size):
    return pl.ds(pl.multiple_of(start * size, size), size)


def ffn_grad_kernel(ff, width, down, half, stages, here_ref, keep_ref, got_ref, *out_refs):
    rank = rank_from(here_ref, stages) & 15
    rows = ff // 8
    for index, out_ref in enumerate(out_refs):
        group = (2 * half + 1 - index) ^ (rank // 4)
        if down:
            left, right = lanes_at(group, rows), pl.ds(ff, width)
        else:
            left = lanes_at((ff + width) // rows + (group & 1), rows)
            right = lanes_at(ff // 2 // width + group // 2, width)
        product = dot_tn(keep_ref[:, left], keep_ref[:, right]) + dot_tn(
            got_ref[:, left], got_ref[:, right]
        )
        store_chunks(out_ref, 0, product, rank, 4)


def ffn_grad_call(here, stages, keep, got, ff, width, down, half, tokens=()):
    return launch(
        functools.partial(ffn_grad_kernel, ff, width, down, half, stages),
        "grad_down" if down else "grad_up", (here, keep, got),
        [((4, ff // 32, width), BF)] * 2, tokens=tokens,
    )


def pair_grad_kernel(splits, half, stages, here_ref, *refs):
    out_ref = refs[-1]
    rank = rank_from(here_ref, stages)
    rows = refs[0].shape[1] // 2
    pairs = [(refs[2 * k], refs[2 * k + 1]) for k in range(len(refs) // 2)]

    def step(index, carry):
        group = (2 * half + index) ^ (rank // 8)
        lanes = lanes_at(group & 1, rows)

        def fill(some):
            product = sum(dot_tn(left[:, lanes], right[...]) for left, right in some)
            store_chunks(out_ref, 8 * index, product, rank, 8)

        @pl.when(group < 2)
        def _():
            fill(pairs[:splits])

        @pl.when(group >= 2)
        def _():
            fill(pairs[splits:])

        return carry

    lax.fori_loop(0, 2, step, 0)


def pair_grad_call(here, stages, first, second, half, name, tokens=()):
    args = [array for pair in first + second for array in pair]
    width = args[0].shape[1]
    return launch(
        functools.partial(pair_grad_kernel, len(first), half, stages), name, (here, *args),
        [((16, width // 16, width), BF)], tokens=tokens,
    )[0]


def add_kernel(terms, *refs):
    inputs, outs = refs[:terms], refs[terms:]
    count = outs[0].shape[0]

    def step(index, carry):
        for place, out_ref in enumerate(reversed(outs)):
            total = inputs[0][place * count + index].astype(F32)
            for more in inputs[1:]:
                total = total + more[place * count + index].astype(F32)
            out_ref[index] = total.astype(BF)
        return carry

    lax.fori_loop(0, count, step, 0)


def add_call(args, parts, tokens=()):
    count, size, width = args[0].shape
    return launch(
        functools.partial(add_kernel, len(args)), "add", args,
        [((count // parts, size, width), BF)] * parts, tokens=tokens,
    )


def join_kernel(keep_ref, got_ref, out_ref):
    count = keep_ref.shape[0]
    out_ref[:count] = keep_ref[...]
    out_ref[count:] = got_ref[...]


def join_call(keep, got, tokens=()):
    count, size, width = keep.shape
    return launch(
        join_kernel, "join", (keep, got), [((2 * count, size, width), BF)], tokens=tokens,
    )[0]


def place_kernel(pieces, target, stages, here_ref, *refs):
    sources, refs = refs[: len(pieces)], refs[-target.outputs - 3 :]
    token_ref, outs, stage_s, sems = refs[0], refs[1:-2], refs[-2], refs[-1]
    token_ref[...] = jnp.zeros_like(token_ref)
    rank = rank_from(here_ref, stages)
    size = sources[0].shape[1]
    copies = []
    for index, (piece, source) in enumerate(zip(pieces, sources)):
        slot = index % 2
        if index >= 2:
            copies[index - 2].wait()

        def step(inner, carry, source=source, slot=slot):
            rows = pl.ds(pl.multiple_of(inner * size, size), size)
            stage_s[slot, rows, :] = source[inner ^ (rank & 3)].astype(F32)
            return carry

        lax.fori_loop(0, 4, step, 0)
        copies.append(target(outs, piece ^ (rank // 4), stage_s.at[slot], sems.at[slot]))
    for copy in copies[-2:]:
        copy.wait()


class Copy:
    def __init__(self, choices):
        self.choices = choices
        for chosen, copy in choices:
            if chosen is None:
                copy.start()
            else:
                pl.when(chosen)(copy.start)

    def wait(self):
        self.choices[0][1].wait()


class DownTarget:
    outputs = 1

    def __call__(self, outs, piece, source, sem):
        place = outs[0].at[lanes_at(piece, source.shape[0])]
        return Copy([(None, pltpu.make_async_copy(source, place, sem))])


class UpTarget:
    outputs = 1

    def __call__(self, outs, piece, source, sem):
        rows, width = source.shape
        place = outs[0].at[lanes_at(piece & 1, rows), lanes_at(piece // 2, width)]
        return Copy([(None, pltpu.make_async_copy(source, place, sem))])


class PairTarget:
    outputs = 2

    def __call__(self, outs, piece, source, sem):
        rows = source.shape[0]
        return Copy([
            (
                piece // 4 == matrix,
                pltpu.make_async_copy(source, outs[matrix].at[lanes_at(piece & 3, rows)], sem),
            )
            for matrix in range(2)
        ])


def swap(rows, stage):
    axis, bit = stage
    return lax.ppermute(rows, axis, [(i, i ^ bit) for i in range(lax.axis_size(axis))])


def stage_list(first):
    every = []
    for axis in ("dp", "seq"):
        every += [(axis, 1 << k) for k in range(lax.axis_size(axis).bit_length() - 1)]
    return first + [stage for stage in every if stage not in first]


class Stream:
    def __init__(self, here, stages, target, out_shapes, name):
        self.here, self.stages, self.target = here, stages, target
        self.out_shapes, self.name, self.placed = out_shapes, name, None
        self.pieces = {}

    def begin(self, sent, kept):
        self.kept = kept
        self.got = [swap(piece, self.stages[1]) for piece in sent]

    def begin_core(self, sent, kept):
        self.kept, self.got = kept, swap(sent, self.stages[0])

    def a0(self, tokens):
        first, second, third, fourth = add_call((self.kept, self.got), 4, tokens)
        self.begin((first, second), (third, fourth))
        return first

    def a1(self, tokens):
        total = add_call((self.kept[0], self.got[0]), 1, tokens)[0]
        self.more = swap(total, self.stages[2])
        return total

    def a2(self, tokens):
        send, self.kept = add_call((self.kept[1], self.got[1], self.more), 2, tokens)
        self.got = swap(send, self.stages[3])
        return send

    def a3(self, tokens):
        send, self.kept = add_call((self.kept, self.got), 2, tokens)
        self.got = swap(send, self.stages[4])
        return send

    def a4(self, tokens):
        total = add_call((self.kept, self.got), 1, tokens)[0]
        for stage in self.stages[5:]:
            total = add_call((total, swap(total, stage)), 1)[0]
        self.kept, self.got = total, swap(total, self.stages[4])
        return total

    def j4(self, tokens):
        self.kept = join_call(self.kept, self.got, tokens)
        self.got = swap(self.kept, self.stages[3])
        return self.kept

    def j3(self, tokens):
        piece = join_call(self.kept, self.got, tokens)
        core, s1, s2 = self.stages[:3]
        near = swap(piece, s2)
        self.pieces = {0: piece, 1: near, 2: swap(piece, s1), 3: swap(near, s1)}
        for number in range(4):
            self.pieces[4 + number] = swap(self.pieces[number], core)
        return piece

    def place(self, numbers, tokens):
        sources = [self.pieces[number] for number in numbers]
        _, size, width = sources[0].shape
        args = [self.here] + sources
        aliases = {}
        if self.placed is not None:
            aliases = {len(args) + index: 1 + index for index in range(len(self.placed))}
            args += [Hbm(item) for item in self.placed]
        token, *self.placed = launch(
            functools.partial(place_kernel, numbers, self.target, self.stages), self.name, args,
            [TOKEN], out_hbm=[(shape, F32) for shape in self.out_shapes], tokens=tokens,
            aliases=aliases,
            scratch=[pltpu.VMEM((2, 4 * size, width), F32), pltpu.SemaphoreType.DMA((2,))],
        )
        return token

    def p0(self, tokens):
        return self.place((0, 4), tokens)

    def p1(self, tokens):
        return self.place((1, 2, 5, 6), tokens)

    def p2(self, tokens):
        return self.place((3, 7), tokens)


def add_rows_kernel(a_ref, b_ref, out_ref):
    out_ref[...] = a_ref[...] + b_ref[...]


def add_rows_call(rows, got, tokens):
    return launch(
        add_rows_kernel, "add_rows", (rows, got), [(rows.shape, F32)], tokens=tokens
    )[0]


def unpack_kernel(vec_ref, *out_refs):
    for start, out_ref in zip((V_BQ, V_BV, V_BO, V_BU, V_BD, V_GA, V_SA, V_GF, V_SF), out_refs):
        count = out_ref.shape[0] // vec_ref.shape[1]
        rows = [vec_ref[start + index : start + index + 1, :] for index in range(count)]
        out_ref[...] = jnp.concatenate(rows, axis=1).reshape(out_ref.shape[0])


def unpack_call(vec, ff):
    width = vec.shape[1]
    outs = shapes(*[((ff if index == 3 else width,), F32) for index in range(9)])
    return pl.pallas_call(
        unpack_kernel,
        in_specs=[VMEM],
        out_specs=[VMEM] * 9,
        out_shape=outs,
        compiler_params=pltpu.CompilerParams(vmem_limit_bytes=4 * 2**20),
        name="unpack",
    )(pltpu.with_memory_space_constraint(vec, pltpu.VMEM))


def from_peers(rows):
    size = lax.axis_size("seq")
    got = [
        lax.ppermute(rows, "seq", [(i, (i + shift) % size) for i in range(size)])
        for shift in range(1, size)
    ]
    return jnp.stack(got)


def shards(
    inputs, cluster_ids, masked, cotangent,
    w_query, w_key, w_value, w_out, w_up, w_down,
    bias_query, bias_value, bias_out, bias_up, bias_down,
    gain_attn, shift_attn, gain_ffn, shift_ffn,
):
    seqs, tokens, width = inputs.shape
    every = range(seqs)
    ff = w_up.shape[1]
    core, x, y = ("dp", 1), ("dp", 2), ("seq", 1)
    z = ("dp", lax.axis_size("dp") // 4)
    stages_a = stage_list([core, x, y])
    stages_b = stage_list([core, z, y, x])
    stages_c = stage_list([core, y, z, x])
    stages_d = stage_list([core, x, y])
    here = Scalar(jnp.stack([lax.axis_index("dp"), lax.axis_index("seq")]).astype(jnp.int32))
    ids = cluster_ids.transpose(1, 0, 2)

    fetched = [
        Hbm(item)
        for item in (
            inputs, ids, w_query, w_key, w_value, bias_query, bias_value, gain_attn, shift_attn,
            masked,
        )
    ]
    more = [cotangent, w_out, w_up, w_down, bias_out, bias_down, gain_ffn, shift_ffn, bias_up]
    projected, sel = [], None
    for s in every:
        results, fetched, brought, found = project_call(
            s, here, fetched, more if s == seqs - 1 else []
        )
        projected.append(results)
        sel = found if s == 0 else sel
    normed, keys, values, own, message = zip(*projected)
    x_v, ids_v, wq_v, wk_v, wv_v, _, _, gain_v, _, _ = fetched
    cot_v, wo_v, wu_v, wd_v, bo_v, bd_v, gf_v, sf_v, _, up_rows = brought
    got = [from_peers(item) for item in message]
    attended, tokens_in = [], ()
    for s in every:
        attended.append(
            attend_call(own[s], message[s], got[s], keys[s], values[s], tokens=tokens_in)
        )
        tokens_in = (attended[s][1],)
    cent, count, out, lse, send = zip(*attended)
    got = [from_peers(item) for item in send]
    merges = []
    for s in every:
        merges.append(
            merge_call(s, out[s], lse[s], got[s], x_v, cot_v, sel, ids_v, tokens=tokens_in)
        )
        tokens_in = (merges[s][2],)
    ctx, merged, lse_all, ctx_m, x_m, cot_m, ids_m = zip(*merges)
    (keep, away, ctx_m, attn_m, mid_m, vec), own, message = masked_call(
        here, ids_m, ctx_m, x_m, cot_m, wo_v, wu_v, wd_v, bo_v, up_rows, gf_v, sf_v
    )
    got_grad = [from_peers(item) for item in message]
    other = swap(away, core)
    weights = (wo_v, wu_v, wd_v, bo_v, up_rows, bd_v, gf_v, sf_v)
    blocks = [(s, start) for s in every for start in range(0, tokens, 256)]
    block_out = None

    def forward(*earlier):
        nonlocal block_out
        if blocks:
            s, start = blocks.pop(0)
            token, block_out = forward_call(s, start, x_v, ctx[s], weights, block_out, earlier)
            return token
        return earlier[0]

    a = Stream(here, stages_a, DownTarget(), [(ff, width)], "place_down")
    b = Stream(here, stages_b, UpTarget(), [(width, ff)], "place_up")
    c = Stream(here, stages_c, PairTarget(), [(width, width)] * 2, "place_out_value")
    d = Stream(here, stages_d, PairTarget(), [(width, width)] * 2, "place_key_query")
    back = {}
    waiting = {}
    grad_input = None

    def ffn_grads(stream, down, half):
        def act(tokens):
            waiting[stream, half] = ffn_grad_call(
                here, stream.stages, keep, other, ff, width, down, half, tokens
            )
            if half == 0:
                stream.begin(waiting[stream, 1], waiting[stream, 0])
            return waiting[stream, half][0]

        return act

    def pair_grads(stream, name, half):
        def act(tokens):
            if stream is c:
                first = [(ctx_m, attn_m)]
                second = [(normed[s], back[s][1]) for s in every]
            else:
                first = [(normed[s], back[s][0]) for s in every]
                second = [(normed[s], waiting["query", s]) for s in every]
            result = pair_grad_call(here, stream.stages, first, second, half, name, tokens)
            waiting[stream, half] = result
            if half == 0:
                stream.begin_core(waiting[stream, 1], result)
            return result

        return act

    def attend_back(s):
        def act(tokens):
            back[s] = attend_back_call(
                cent[s], lse_all[s], merged[s], own[s], got_grad[s], keys[s], values[s],
                tokens=tokens,
            )
            waiting["part", s] = from_peers(back[s][3])
            return back[s][3]

        return act

    def query(s):
        def act(tokens):
            waiting["query", s] = query_call(
                s, back[s][2], waiting["part", s], count[s], ids_v, width, tokens
            )
            return waiting["query", s]

        return act

    def back_input(s):
        def act(tokens):
            nonlocal grad_input, vec
            grad_input, vec = back_input_call(
                s, waiting["query", s], back[s][0], back[s][1], x_v, wq_v, wk_v, wv_v, gain_v, mid_m,
                sel, vec, former=grad_input, tokens=tokens,
            )
            return vec

        return act

    def forward_step(tokens):
        return forward(*tokens)

    def vector_step(stage):
        def act(tokens):
            nonlocal vec
            vec = add_rows_call(vec, waiting["vec"], tokens)
            place = stages_a.index(stage) + 1
            waiting["vec"] = swap(vec, stages_a[place]) if place < len(stages_a) else None
            return vec

        return act

    def vector_first(tokens):
        waiting["vec"] = swap(vec, stages_a[0])
        return tokens[0]

    def all_seqs(make):
        return [make(s) for s in every]

    def streams(*steps):
        return [getattr(stream, step) for stream, step in steps]

    order = (
        [forward_step, ffn_grads(a, True, 1), ffn_grads(a, True, 0)]
        + [ffn_grads(b, False, 1), ffn_grads(b, False, 0)]
        + all_seqs(attend_back)
        + streams((a, "a1"), (b, "a1"))
        + [pair_grads(c, "grad_out_value", 1), pair_grads(c, "grad_out_value", 0)]
        + all_seqs(query)
        + [pair_grads(d, "grad_key_query", 1), pair_grads(d, "grad_key_query", 0)]
        + streams((c, "a0"), (a, "a2"), (d, "a0"))
        + all_seqs(back_input)
        + [vector_first]
        + streams((b, "a2"), (a, "a3"), (d, "a1"))
        + [vector_step(stages_a[0])]
        + streams((c, "a1"))
        + [forward_step]
        + streams((b, "a3"), (a, "a4"))
        + [vector_step(stages_a[1])]
        + streams((d, "a2"), (c, "a2"))
        + [vector_step(stages_a[2]), forward_step]
        + streams((b, "a4"), (c, "a3"), (a, "j4"), (d, "a3"))
        + [vector_step(stages_a[3])]
        + [forward_step] * len(blocks)
        + streams((b, "j4"), (c, "a4"), (a, "j3"), (d, "a4"), (b, "j3"), (c, "j4"))
        + streams((a, "p0"), (d, "j4"), (b, "p0"))
        + [vector_step(stage) for stage in stages_a[4:]]
        + streams((c, "j3"), (a, "p1"), (d, "j3"), (b, "p1"), (c, "p0"), (a, "p2"), (d, "p0"))
        + streams((c, "p1"), (b, "p2"), (c, "p2"), (d, "p1"), (d, "p2"))
    )
    last = vec
    for step in order:
        last = step((last,))
    (grad_w_down,), (grad_w_up,) = a.placed, b.placed
    grad_w_out, grad_w_value = c.placed
    grad_w_key, grad_w_query = d.placed
    return (
        block_out, grad_input,
        grad_w_query, grad_w_key, grad_w_value, grad_w_out, grad_w_up, grad_w_down,
        *unpack_call(vec, ff),
    )


def solution(mesh):
    rows = P("dp", "seq", None)
    return jax.shard_map(
        shards,
        mesh=mesh,
        in_specs=(rows, P("dp", None, "seq"), P("dp", "seq"), rows) + (P(),) * 15,
        out_specs=(rows, rows) + (P(),) * 15,
        check_vma=False,
    )
```

```python
import functools

import jax
import jax.numpy as jnp
from jax import lax
from jax.experimental import pallas as pl
from jax.experimental.pallas import tpu as pltpu
from jax.sharding import PartitionSpec as P

HEADS = 12
HDIM = 64
CLUSTERS = 100
MASK_MOST = 128
PAIRS = HEADS // 2
LANES = 2 * HDIM
ROWS = 112
SCALE = HDIM**-0.5
EPS = 1e-05
BF = jnp.bfloat16
F32 = jnp.float32

V_BQ, V_BV, V_BO, V_BU, V_BD, V_GA, V_SA, V_GF, V_SF = 0, 1, 2, 3, 7, 8, 9, 10, 11
VEC_ROWS = 16


def dot(a, b):
    return lax.dot_general(a, b, (((1,), (0,)), ((), ())), preferred_element_type=F32)


def dot_nt(a, b):
    return lax.dot_general(a, b, (((1,), (1,)), ((), ())), preferred_element_type=F32)


def dot_tn(a, b):
    return lax.dot_general(a, b, (((0,), (0,)), ((), ())), preferred_element_type=F32)


def norm_parts(rows):
    center = rows - jnp.mean(rows, axis=-1, keepdims=True)
    inverse = lax.rsqrt(jnp.mean(center * center, axis=-1, keepdims=True) + EPS)
    return center * inverse, inverse


def norm_back(incoming, unit, inverse, gain):
    scaled = incoming * gain
    return inverse * (
        scaled
        - jnp.mean(scaled, axis=-1, keepdims=True)
        - unit * jnp.mean(scaled * unit, axis=-1, keepdims=True)
    )


def normal_cdf(upper):
    return 0.5 * (1.0 + lax.erf(upper * (0.5**0.5)))


def lane_of(rows):
    return lax.broadcasted_iota(jnp.int32, (rows, LANES), 1)


def column(slab, index):
    picked = jnp.where(lane_of(slab.shape[0]) == index, slab, 0.0)
    return jnp.sum(picked, axis=1, keepdims=True)


def member_pair(ids, seq, pair):
    tokens = ids.shape[-1]
    rows = lax.broadcasted_iota(jnp.int32, (ROWS, tokens), 0)
    one = [
        jnp.where(rows == ids[2 * pair + side, seq : seq + 1, :], 1.0, 0.0).astype(BF)
        for side in range(2)
    ]
    return jnp.concatenate(one, axis=0)


def row_blocks(rows, act, block=256):
    def step(index, carry):
        act(pl.ds(pl.multiple_of(index * block, block), block))
        return carry

    lax.fori_loop(0, rows // block, step, 0)


def vector(ref):
    return ref[...].astype(F32).reshape(1, -1)


def pick_rows(sel):
    slots = lax.broadcasted_iota(jnp.int32, (MASK_MOST, sel.shape[-1]), 0)
    return jnp.where(slots == sel, 1.0, 0.0).astype(BF)


def stack_pair(both):
    left = lane_of(both.shape[0]) < HDIM
    return jnp.concatenate(
        [jnp.where(left, both, 0.0).astype(BF), jnp.where(left, 0.0, both).astype(BF)], axis=0
    )


def unstack_pair(stacked):
    left = lane_of(ROWS) < HDIM
    return jnp.where(left, stacked[:ROWS], stacked[ROWS:])


def pair_lanes(pair):
    return pl.ds(pl.multiple_of(pair * LANES, LANES), LANES)


class Hbm:
    def __init__(self, array):
        self.array = array


class Scalar:
    def __init__(self, array):
        self.array = array


def rank_from(here_ref, stages):
    rank = 0
    for place, (axis, bit) in enumerate(stages[:5]):
        index = here_ref[0 if axis == "dp" else 1]
        rank = rank + ((index >> (bit.bit_length() - 1)) & 1) * (16 >> place)
    return rank


def shapes(*items):
    return [jax.ShapeDtypeStruct(shape, dtype) for shape, dtype in items]


class Estimate:
    now = 5.0


TOKEN = ((8, LANES), F32)
VMEM = pl.BlockSpec(memory_space=pltpu.VMEM)
HBM = pl.BlockSpec(memory_space=pltpu.HBM)
ANY = pl.BlockSpec(memory_space=pl.ANY)


def launch(kernel, name, args, outs, out_hbm=(), tokens=(), scratch=(), mib=16, aliases=None):
    count = len(tokens)
    operands, in_specs = list(tokens), [ANY] * count
    for arg in args:
        if isinstance(arg, Hbm):
            operands.append(pltpu.with_memory_space_constraint(arg.array, pltpu.HBM))
            in_specs.append(HBM)
        elif isinstance(arg, Scalar):
            operands.append(arg.array)
            in_specs.append(pl.BlockSpec(memory_space=pltpu.SMEM))
        else:
            operands.append(pltpu.with_memory_space_constraint(arg, pltpu.VMEM))
            in_specs.append(VMEM)
    out_shape = [pltpu.VMEM(shape, dtype) for shape, dtype in outs] + shapes(*out_hbm)
    return pl.pallas_call(
        lambda *refs: kernel(*refs[count:]),
        in_specs=in_specs,
        out_specs=[VMEM] * len(outs) + [HBM] * len(out_hbm),
        out_shape=out_shape,
        scratch_shapes=list(scratch),
        input_output_aliases={count + a: b for a, b in (aliases or {}).items()},
        compiler_params=pltpu.CompilerParams(vmem_limit_bytes=mib * 2**20),
        cost_estimate=pl.CostEstimate(
            flops=int(Estimate.now * 1e9), bytes_accessed=0, transcendentals=0
        ),
        name=name,
    )(*operands)


def load(pairs, sems):
    copies = [
        pltpu.make_async_copy(source, target, sems.at[index])
        for index, (source, target) in enumerate(pairs)
    ]
    for copy in copies:
        copy.start()
    return copies


def project_rows(
    seq, x, ids_ref, wq_ref, wk_ref, wv_ref, bq_ref, bv_ref, gain_ref, shift_ref,
    masked_ref, normed_ref, key_ref, value_ref, own_ref, message_ref, sel_ref, query_s, ready,
):
    ready("x")
    if sel_ref is not None:
        tokens = masked_ref.shape[1]
        before = jnp.where(
            lax.broadcasted_iota(jnp.int32, (tokens, tokens), 0)
            <= lax.broadcasted_iota(jnp.int32, (tokens, tokens), 1),
            1.0,
            0.0,
        ).astype(BF)
        for s in range(masked_ref.shape[0]):
            row = masked_ref[s : s + 1, :]
            spread = jnp.broadcast_to(row.astype(F32), (16, tokens)).astype(BF)
            slot = dot(spread, before)[:1].astype(jnp.int32) - 1
            sel_ref[s : s + 1, :] = jnp.where(row == 1, slot, -1)
    length = normed_ref.shape[0]

    def norm(rows):
        unit, _ = norm_parts(x[seq, rows, :].astype(F32))
        normed_ref[rows, :] = (unit * vector(gain_ref) + vector(shift_ref)).astype(BF)

    def query(rows):
        query_s[rows, :] = (dot(normed_ref[rows, :], wq_ref[...]) + vector(bq_ref)).astype(BF)

    def key_value(rows):
        normed = normed_ref[rows, :]
        key_ref[rows, :] = dot(normed, wk_ref[...]).astype(BF)
        value_ref[rows, :] = (dot(normed, wv_ref[...]) + vector(bv_ref)).astype(BF)

    row_blocks(length, norm)
    ready("q")
    row_blocks(length, query)
    lane = lane_of(ROWS)
    ones = jnp.ones((length, LANES), BF)

    def step(pair, slab):
        right = jnp.concatenate([query_s[:, pair_lanes(pair)], ones], axis=1)
        sums = dot(member_pair(ids_ref, seq, pair), right)
        own = unstack_pair(sums[:, :LANES])
        own_ref[pair] = own
        message_ref[pair] = own.astype(BF)
        for side in range(2):
            count = sums[side * ROWS : (side + 1) * ROWS, LANES:]
            low = jnp.minimum(count, 256.0)
            slab = slab + jnp.where(lane == 2 * pair + side, low, 0.0)
            slab = slab + jnp.where(lane == 16 + 2 * pair + side, count - low, 0.0)
        return slab

    slab = lax.fori_loop(0, PAIRS, step, jnp.zeros((ROWS, LANES), F32), unroll=2)
    message_ref[PAIRS] = slab.astype(BF)
    ready("kv")
    row_blocks(length, key_value)


SLAB = (PAIRS, ROWS, LANES)
SLAB_MORE = (PAIRS + 1, ROWS, LANES)


def project_outs(x):
    _, tokens, width = x.shape
    rows = ((tokens, width), BF)
    return [rows, rows, rows, (SLAB, F32), (SLAB_MORE, BF)], [pltpu.VMEM((tokens, width), BF)]


def project_call(seq, here, fetched, more):
    first = isinstance(fetched[0], Hbm)
    brought = [item.array for item in fetched] if first else []
    x = brought[0] if first else fetched[0]
    outs, scratch = project_outs(x)
    seqs = x.shape[0]
    count, extra = len(fetched), len(more)
    loads = count + seqs - 1 if first else 0
    own_outs = 6 if first else 5
    if first:
        outs = outs + [((seqs, x.shape[1]), jnp.int32)]

    def kernel(here_ref, *refs):
        sources, refs = refs[:count], refs[count:]
        more_in, refs = refs[:extra], refs[extra:]
        results, refs = refs[:own_outs], refs[own_outs:]
        targets, refs = (refs[:count], refs[count:]) if first else (sources, refs)
        more_out, refs = refs[:extra], refs[extra:]
        row_ref, refs = (refs[0], refs[1:]) if extra else (None, refs)
        query_s, sems = refs
        results = tuple(results) + (() if first else (None,))
        pairs = []
        if first:
            order = [seq] + [s for s in range(seqs) if s != seq]
            rows = [(sources[0].at[s], targets[0].at[s]) for s in order]
            pairs = [rows[0]] + list(zip(sources[1:], targets[1:])) + rows[1:]
        pairs = pairs + list(zip(more_in, more_out))
        copies = load(pairs, sems)
        groups = {"x": [], "q": [], "kv": []}
        if first:
            groups = {"x": [0, 7, 8, 9], "q": [1, 2, 5], "kv": [3, 4, 6]}
        waited = set()

        def ready(name):
            for index in groups[name]:
                copies[index].wait()
                waited.add(index)

        project_rows(seq, *targets, *results, query_s, ready)
        for index, copy in enumerate(copies):
            if index not in waited:
                copy.wait()
        if extra:
            row_ref[...] = vector(more_out[-1])

    brings = [(item.shape, item.dtype) for item in brought] + [
        (item.shape, item.dtype) for item in more
    ]
    if extra:
        brings.append(((1, more[-1].shape[0]), F32))
    results = launch(
        kernel, "project", [here] + list(fetched) + [Hbm(item) for item in more], outs + brings,
        scratch=scratch + [pltpu.SemaphoreType.DMA((loads + extra,))],
    )
    if first:
        return results[:5], results[6 : 6 + count], results[6 + count :], results[5]
    return results[:5], fetched, results[5:], None


def attend_kernel(
    own_ref, message_ref, got_ref, key_ref, value_ref,
    cent_ref, count_ref, out_ref, lse_ref, send_ref,
):
    peers = got_ref.shape[0]
    lane = lane_of(ROWS)
    slab = message_ref[PAIRS].astype(F32)
    for peer in range(peers):
        slab = slab + got_ref[peer, PAIRS].astype(F32)
    count = jnp.maximum(slab + pltpu.roll(slab, LANES - 16, 1), 1.0)
    count_ref[...] = count

    def step(pair, lses):
        total = own_ref[pair]
        for peer in range(peers):
            total = total + got_ref[peer, pair].astype(F32)
        divisor = jnp.where(lane < HDIM, column(count, 2 * pair), column(count, 2 * pair + 1))
        cent = (total / divisor).astype(BF)
        cent_ref[pair] = cent
        scores = dot_nt(stack_pair(cent.astype(F32)), key_ref[:, pair_lanes(pair)]) * SCALE
        peak = jnp.max(scores, axis=1, keepdims=True)
        raised = jnp.exp(scores - peak)
        mass = jnp.sum(raised, axis=1, keepdims=True)
        mixed = unstack_pair(dot(raised.astype(BF), value_ref[:, pair_lanes(pair)]) / mass)
        out_ref[pair] = mixed
        send_ref[pair] = mixed.astype(BF)
        lse = peak + jnp.log(mass)
        lses = lses + jnp.where(lane == 2 * pair, lse[:ROWS], 0.0)
        return lses + jnp.where(lane == 2 * pair + 1, lse[ROWS:], 0.0)

    lses = lax.fori_loop(0, PAIRS, step, jnp.zeros((ROWS, LANES), F32), unroll=2)
    lse_ref[...] = lses
    high = lses.astype(BF).astype(F32)
    rest = lses - high
    middle = rest.astype(BF).astype(F32)
    low = (rest - middle).astype(BF).astype(F32)
    send_ref[PAIRS] = (high + pltpu.roll(middle, 16, 1) + pltpu.roll(low, 32, 1)).astype(BF)


def attend_call(*args, tokens=()):
    one = ((ROWS, LANES), F32)
    return launch(
        attend_kernel, "attend", args, [(SLAB, BF), one, (SLAB, F32), one, (SLAB_MORE, BF)],
        tokens=tokens,
    )


def merge_kernel(
    seq, out_ref, lse_ref, got_ref, x_ref, cot_ref, sel_ref, ids_ref,
    ctx_ref, merged_ref, lse_all_ref, ctx_m_ref, x_m_ref, cot_m_ref, ids_m_ref,
):
    peers = got_ref.shape[0]
    lane = lane_of(ROWS)
    lses = [lse_ref[...]]
    for peer in range(peers):
        slab = got_ref[peer, PAIRS].astype(F32)
        lses.append(slab + pltpu.roll(slab, LANES - 16, 1) + pltpu.roll(slab, LANES - 32, 1))
    peak = functools.reduce(jnp.maximum, lses)
    merged = peak + jnp.log(sum(jnp.exp(item - peak) for item in lses))
    lse_all_ref[...] = merged
    portions = [jnp.exp(item - merged) for item in lses]

    def gather(pair, carry):
        total = jnp.zeros((ROWS, LANES), F32)
        for index, portion in enumerate(portions):
            part = out_ref[pair] if index == 0 else got_ref[index - 1, pair].astype(F32)
            weight = jnp.where(
                lane < HDIM, column(portion, 2 * pair), column(portion, 2 * pair + 1)
            )
            total = total + weight * part
        merged_ref[pair] = total
        member = member_pair(ids_ref, seq, pair)
        ctx_ref[:, pair_lanes(pair)] = dot_tn(member, stack_pair(total)).astype(BF)
        return carry

    lax.fori_loop(0, PAIRS, gather, 0, unroll=2)
    pick = pick_rows(sel_ref[seq : seq + 1, :])
    ctx_m_ref[...] = dot(pick, ctx_ref[...]).astype(BF)
    x_m_ref[...] = dot(pick, x_ref[seq]).astype(BF)
    cot_m_ref[...] = dot(pick, cot_ref[seq]).astype(BF)
    heads = [ids_ref[head, seq : seq + 1, :].astype(F32) for head in range(HEADS)]
    heads = jnp.concatenate(heads + [jnp.zeros_like(heads[0])] * (16 - HEADS), axis=0)
    ids_m_ref[...] = dot_nt(heads.astype(BF), pick).astype(jnp.int32)


def merge_call(seq, out, lse, got, x, cot, sel, ids, tokens=()):
    _, length, width = x.shape
    picked = ((MASK_MOST, width), BF)
    return launch(
        functools.partial(merge_kernel, seq), "merge", (out, lse, got, x, cot, sel, ids),
        [((length, width), BF), (SLAB, F32), ((ROWS, LANES), F32), picked, picked, picked,
            ((16, MASK_MOST), jnp.int32)],
        tokens=tokens,
    )


def masked_kernel(seqs, *refs):
    here_ref, ids_refs = refs[0], refs[1 : 1 + seqs]
    rest = refs[1 + seqs :]
    ctx_refs, x_refs, cot_refs = rest[:seqs], rest[seqs : 2 * seqs], rest[2 * seqs : 3 * seqs]
    (
        wo_ref, wu_ref, wd_ref, bo_ref, bu_ref, gain_ref, shift_ref,
        keep_ref, send_ref, ctx_m_ref, attn_m_ref, mid_m_ref, vec_ref,
    ) = rest[3 * seqs : 3 * seqs + 13]
    own_ref, message_ref, middle_s, back_s = rest[3 * seqs + 13 :]
    width = wo_ref.shape[0]
    ff_block = width
    ff_blocks = wu_ref.shape[1] // ff_block
    half_blocks = ff_blocks // 2
    tail = 2 * half_blocks * ff_block
    core = here_ref[0] & 1
    vec_ref[...] = jnp.zeros_like(vec_ref)
    for s in range(seqs):
        rows = pl.ds(s * MASK_MOST, MASK_MOST)
        ctx_m_ref[rows, :] = ctx_refs[s][...]
        middle_s[rows, :] = x_refs[s][...].astype(F32)
        keep_ref[rows, tail : tail + width] = cot_refs[s][...]
        send_ref[rows, tail : tail + width] = cot_refs[s][...]
    middle = middle_s[...] + (dot(ctx_m_ref[...], wo_ref[...]) + vector(bo_ref))
    middle_s[...] = middle
    unit, _ = norm_parts(middle)
    low = (unit * vector(gain_ref) + vector(shift_ref)).astype(BF)
    keep_ref[:, tail + width :] = low
    send_ref[:, tail + width :] = low
    back_s[...] = jnp.zeros_like(back_s)

    def feed(block, carry):
        lanes = pl.ds(pl.multiple_of(block * ff_block, ff_block), ff_block)
        upper = dot(keep_ref[:, tail + width :], wu_ref[:, lanes]) + bu_ref[:, lanes]
        cdf = normal_cdf(upper)
        hidden = (upper * cdf).astype(BF)
        slope = cdf + upper * (jnp.exp(-0.5 * upper * upper) * 0.3989422804014327)
        grad_y = keep_ref[:, tail : tail + width]
        grad_upper = (dot_nt(grad_y, wd_ref[lanes, :]) * slope).astype(BF)
        back_s[...] += dot_nt(grad_upper, wu_ref[:, lanes])
        vec_ref[pl.ds(V_BU + block, 1), :] = jnp.sum(
            grad_upper.astype(F32), axis=0, keepdims=True
        )
        half = block // half_blocks
        inner = block - half * half_blocks
        first = pl.ds(pl.multiple_of(inner * ff_block, ff_block), ff_block)
        second = pl.ds(
            pl.multiple_of(inner * ff_block + half_blocks * ff_block, ff_block), ff_block
        )

        @pl.when(half == core)
        def _():
            keep_ref[:, first] = hidden
            keep_ref[:, second] = grad_upper

        @pl.when(half != core)
        def _():
            send_ref[:, first] = hidden
            send_ref[:, second] = grad_upper

        return carry

    lax.fori_loop(0, ff_blocks, feed, 0, unroll=1)
    unit, inverse = norm_parts(middle_s[...])
    incoming = back_s[...]
    grad_y = keep_ref[:, tail : tail + width].astype(F32)
    grad_middle = grad_y + norm_back(incoming, unit, inverse, vector(gain_ref))
    mid_m_ref[...] = grad_middle
    grad_attn = grad_middle.astype(BF)
    attn_m_ref[...] = grad_attn
    vec_ref[V_BD : V_BD + 1, :] = jnp.sum(grad_y, axis=0, keepdims=True)
    vec_ref[V_BO : V_BO + 1, :] = jnp.sum(grad_attn.astype(F32), axis=0, keepdims=True)
    vec_ref[V_GF : V_GF + 1, :] = jnp.sum(incoming * unit, axis=0, keepdims=True)
    vec_ref[V_SF : V_SF + 1, :] = jnp.sum(incoming, axis=0, keepdims=True)
    back_s[...] = dot_nt(grad_attn, wo_ref[...])
    for s in range(seqs):
        clusters = lax.broadcasted_iota(jnp.int32, (ROWS, MASK_MOST), 0)

        def scatter(pair, carry, s=s, clusters=clusters):
            sides = [
                jnp.where(clusters == ids_refs[s][pl.ds(2 * pair + side, 1), :], 1.0, 0.0)
                for side in range(2)
            ]
            member = jnp.concatenate(sides, axis=0).astype(BF)
            rows = back_s[s * MASK_MOST : (s + 1) * MASK_MOST, pair_lanes(pair)]
            high = rows.astype(BF)
            low = (rows - high.astype(F32)).astype(BF)
            own = unstack_pair(dot(member, high) + dot(member, low))
            own_ref[s, pair] = own
            message_ref[s, pair] = own.astype(BF)
            return carry

        lax.fori_loop(0, PAIRS, scatter, 0, unroll=2)


def masked_call(here, ids, ctx, x, cot, *weights):
    seqs = len(ctx)
    width, ff = weights[1].shape
    picked = seqs * MASK_MOST
    wide = ((picked, ff + 2 * width), BF)
    out = launch(
        functools.partial(masked_kernel, seqs), "masked_rows",
        (here, *ids, *ctx, *x, *cot, *weights),
        [
            wide, wide, ((picked, width), BF), ((picked, width), BF), ((picked, width), F32),
            ((VEC_ROWS, width), F32), ((seqs,) + SLAB, F32), ((seqs,) + SLAB, BF),
        ],
        scratch=[pltpu.VMEM((picked, width), F32), pltpu.VMEM((picked, width), F32)],
    )
    return out


def forward_kernel(
    seq, start, x_ref, ctx_ref, wo_ref, wu_ref, wd_ref, bo_ref, bu_ref, bd_ref, gain_ref, shift_ref,
    *rest,
):
    token_ref, y_ref, low_s, total_s, out_s, sem = rest[-6:]
    token_ref[...] = jnp.zeros_like(token_ref)
    rows = pl.ds(start, low_s.shape[0])
    middle = x_ref[seq, rows, :].astype(F32) + (dot(ctx_ref[rows, :], wo_ref[...]) + vector(bo_ref))
    unit, _ = norm_parts(middle)
    low_s[...] = (unit * vector(gain_ref) + vector(shift_ref)).astype(BF)
    total_s[...] = middle + vector(bd_ref)
    block = x_ref.shape[2]

    def feed(index, carry):
        lanes = pl.ds(pl.multiple_of(index * block, block), block)
        upper = dot(low_s[...], wu_ref[:, lanes]) + bu_ref[:, lanes]
        hidden = (upper * normal_cdf(upper)).astype(BF)
        total_s[...] += dot(hidden, wd_ref[lanes, :])
        return carry

    lax.fori_loop(0, wu_ref.shape[1] // block, feed, 0, unroll=1)
    out_s[...] = total_s[...].astype(BF)
    copy = pltpu.make_async_copy(out_s, y_ref.at[seq, rows], sem)
    copy.start()
    copy.wait()


def forward_call(seq, start, x, ctx, weights, former, tokens, block=256):
    width = x.shape[2]
    args = [x, ctx, *weights]
    aliases = {}
    if former is not None:
        aliases = {len(args): 1}
        args.append(Hbm(former))
    return launch(
        functools.partial(forward_kernel, seq, start), "forward_rows", args, [TOKEN],
        out_hbm=[(x.shape, BF)], tokens=tokens, aliases=aliases,
        scratch=[
            pltpu.VMEM((block, width), BF), pltpu.VMEM((block, width), F32),
            pltpu.VMEM((block, width), BF), pltpu.SemaphoreType.DMA,
        ],
    )


def attend_back_kernel(
    seq, cent_ref, lse_ref, merged_ref, own_ref, got_ref, key_ref, value_ref,
    grad_key_ref, grad_value_ref, part_ref, send_ref,
):
    peers = got_ref.shape[0]
    lane = lane_of(ROWS)
    lses = lse_ref[...]

    def step(pair, carry):
        total = own_ref[seq, pair]
        for peer in range(peers):
            total = total + got_ref[peer, seq, pair].astype(F32)
        grad_cent = total.astype(BF).astype(F32)
        product = grad_cent * merged_ref[pair]
        delta = jnp.concatenate(
            [
                jnp.sum(jnp.where(lane < HDIM, product, 0.0), axis=1, keepdims=True),
                jnp.sum(jnp.where(lane < HDIM, 0.0, product), axis=1, keepdims=True),
            ],
            axis=0,
        )
        lse = jnp.concatenate([column(lses, 2 * pair), column(lses, 2 * pair + 1)], axis=0)
        cents = stack_pair(cent_ref[pair].astype(F32))
        grads = stack_pair(grad_cent)
        keys = key_ref[:, pair_lanes(pair)]
        weights = jnp.exp(dot_nt(cents, keys) * SCALE - lse)
        grad_weights = dot_nt(grads, value_ref[:, pair_lanes(pair)])
        grad_scores = (weights * (grad_weights - delta)).astype(BF)
        part = unstack_pair(dot(grad_scores, keys))
        part_ref[pair] = part
        send_ref[pair] = part.astype(BF)
        grad_key_ref[:, pair_lanes(pair)] = (dot_tn(grad_scores, cents) * SCALE).astype(BF)
        grad_value_ref[:, pair_lanes(pair)] = dot_tn(weights.astype(BF), grads).astype(BF)
        return carry

    lax.fori_loop(0, PAIRS, step, 0, unroll=2)


def attend_back_call(seq, *args, tokens=()):
    rows = (args[5].shape, BF)
    return launch(
        functools.partial(attend_back_kernel, seq), "attend_back", args, [rows, rows, (SLAB, F32), (SLAB, BF)],
        tokens=tokens,
    )


def query_kernel(seq, part_ref, got_ref, count_ref, ids_ref, gq_ref):
    peers = got_ref.shape[0]
    lane = lane_of(ROWS)
    count = count_ref[...]

    def step(pair, carry):
        total = part_ref[pair]
        for peer in range(peers):
            total = total + got_ref[peer, pair].astype(F32)
        grad_cent = (total * SCALE).astype(BF).astype(F32)
        divisor = jnp.where(lane < HDIM, column(count, 2 * pair), column(count, 2 * pair + 1))
        spread = stack_pair(grad_cent / divisor)
        member = member_pair(ids_ref, seq, pair)
        gq_ref[:, pair_lanes(pair)] = dot_tn(member, spread).astype(BF)
        return carry

    lax.fori_loop(0, PAIRS, step, 0, unroll=2)


def query_call(seq, part, got, count, ids, width, tokens=()):
    return launch(
        functools.partial(query_kernel, seq), "query_grad", (part, got, count, ids),
        [((ids.shape[-1], width), BF)], tokens=tokens,
    )[0]


def back_input_kernel(
    seq, gq_ref, gk_ref, gv_ref, x_ref, wq_ref, wk_ref, wv_ref, gain_ref, mid_ref, sel_ref,
    vec_in_ref, *rest,
):
    vec_ref, gx_ref, out_s, sem = rest[-4:]
    vec_ref[...] = vec_in_ref[...]
    middle = mid_ref[seq * MASK_MOST : (seq + 1) * MASK_MOST, :]
    high = middle.astype(BF)
    low = (middle - high.astype(F32)).astype(BF)

    def act(rows):
        grad_query, grad_value = gq_ref[rows, :], gv_ref[rows, :]
        incoming = (
            dot_nt(grad_query, wq_ref[...])
            + dot_nt(gk_ref[rows, :], wk_ref[...])
            + dot_nt(grad_value, wv_ref[...])
        )
        unit, inverse = norm_parts(x_ref[seq, rows, :].astype(F32))
        grad = norm_back(incoming, unit, inverse, vector(gain_ref))
        pick = pick_rows(sel_ref[seq : seq + 1, rows])
        out_s[rows, :] = (grad + (dot_tn(pick, high) + dot_tn(pick, low))).astype(BF)
        vec_ref[V_BQ : V_BQ + 1, :] += jnp.sum(grad_query.astype(F32), axis=0, keepdims=True)
        vec_ref[V_BV : V_BV + 1, :] += jnp.sum(grad_value.astype(F32), axis=0, keepdims=True)
        vec_ref[V_GA : V_GA + 1, :] += jnp.sum(incoming * unit, axis=0, keepdims=True)
        vec_ref[V_SA : V_SA + 1, :] += jnp.sum(incoming, axis=0, keepdims=True)

    row_blocks(gq_ref.shape[0], act)
    copy = pltpu.make_async_copy(out_s, gx_ref.at[seq], sem)
    copy.start()
    copy.wait()


def back_input_call(seq, *args, former, tokens=()):
    args = list(args)
    x, vec = args[3], args[10]
    aliases = {}
    if former is not None:
        aliases = {len(args): 1}
        args.append(Hbm(former))
    vec, grad = launch(
        functools.partial(back_input_kernel, seq), "back_input", args, [(vec.shape, F32)],
        out_hbm=[(x.shape, BF)], tokens=tokens, aliases=aliases,
        scratch=[pltpu.VMEM(x.shape[1:], BF), pltpu.SemaphoreType.DMA],
    )
    return grad, vec


def store_chunks(out_ref, base, product, rank, per_group):
    size = product.shape[0] // per_group
    for index in range(per_group):
        out_ref[base + (index ^ (rank & (per_group - 1)))] = product[
            index * size : (index + 1) * size
        ].astype(BF)


def lanes_at(start, size):
    return pl.ds(pl.multiple_of(start * size, size), size)


def ffn_grad_kernel(ff, width, down, half, stages, here_ref, keep_ref, got_ref, *out_refs):
    rank = rank_from(here_ref, stages) & 15
    rows = ff // 8
    for index, out_ref in enumerate(out_refs):
        group = (2 * half + 1 - index) ^ (rank // 4)
        if down:
            left, right = lanes_at(group, rows), pl.ds(ff, width)
        else:
            left = lanes_at((ff + width) // rows + (group & 1), rows)
            right = lanes_at(ff // 2 // width + group // 2, width)
        product = dot_tn(keep_ref[:, left], keep_ref[:, right]) + dot_tn(
            got_ref[:, left], got_ref[:, right]
        )
        store_chunks(out_ref, 0, product, rank, 4)


def ffn_grad_call(here, stages, keep, got, ff, width, down, half, tokens=()):
    return launch(
        functools.partial(ffn_grad_kernel, ff, width, down, half, stages),
        "grad_down" if down else "grad_up", (here, keep, got),
        [((4, ff // 32, width), BF)] * 2, tokens=tokens,
    )


def pair_grad_kernel(splits, half, stages, here_ref, *refs):
    out_ref = refs[-1]
    rank = rank_from(here_ref, stages)
    rows = refs[0].shape[1] // 2
    pairs = [(refs[2 * k], refs[2 * k + 1]) for k in range(len(refs) // 2)]

    def step(index, carry):
        group = (2 * half + index) ^ (rank // 8)
        lanes = lanes_at(group & 1, rows)

        def fill(some):
            product = sum(dot_tn(left[:, lanes], right[...]) for left, right in some)
            store_chunks(out_ref, 8 * index, product, rank, 8)

        @pl.when(group < 2)
        def _():
            fill(pairs[:splits])

        @pl.when(group >= 2)
        def _():
            fill(pairs[splits:])

        return carry

    lax.fori_loop(0, 2, step, 0)


def pair_grad_call(here, stages, first, second, half, name, tokens=()):
    args = [array for pair in first + second for array in pair]
    width = args[0].shape[1]
    return launch(
        functools.partial(pair_grad_kernel, len(first), half, stages), name, (here, *args),
        [((16, width // 16, width), BF)], tokens=tokens,
    )[0]


def add_kernel(terms, *refs):
    inputs, outs = refs[:terms], refs[terms:]
    count = outs[0].shape[0]

    def step(index, carry):
        for place, out_ref in enumerate(reversed(outs)):
            total = inputs[0][place * count + index].astype(F32)
            for more in inputs[1:]:
                total = total + more[place * count + index].astype(F32)
            out_ref[index] = total.astype(BF)
        return carry

    lax.fori_loop(0, count, step, 0)


def add_call(args, parts, tokens=()):
    count, size, width = args[0].shape
    return launch(
        functools.partial(add_kernel, len(args)), "add", args,
        [((count // parts, size, width), BF)] * parts, tokens=tokens,
    )


def join_kernel(keep_ref, got_ref, out_ref):
    count = keep_ref.shape[0]
    out_ref[:count] = keep_ref[...]
    out_ref[count:] = got_ref[...]


def join_call(keep, got, tokens=()):
    count, size, width = keep.shape
    return launch(
        join_kernel, "join", (keep, got), [((2 * count, size, width), BF)], tokens=tokens,
    )[0]


def place_kernel(pieces, target, stages, here_ref, *refs):
    sources, refs = refs[: len(pieces)], refs[-target.outputs - 3 :]
    token_ref, outs, stage_s, sems = refs[0], refs[1:-2], refs[-2], refs[-1]
    token_ref[...] = jnp.zeros_like(token_ref)
    rank = rank_from(here_ref, stages)
    size = sources[0].shape[1]
    copies = []
    for index, (piece, source) in enumerate(zip(pieces, sources)):
        slot = index % 2
        if index >= 2:
            copies[index - 2].wait()

        def step(inner, carry, source=source, slot=slot):
            rows = pl.ds(pl.multiple_of(inner * size, size), size)
            stage_s[slot, rows, :] = source[inner ^ (rank & 3)].astype(F32)
            return carry

        lax.fori_loop(0, 4, step, 0)
        copies.append(target(outs, piece ^ (rank // 4), stage_s.at[slot], sems.at[slot]))
    for copy in copies[-2:]:
        copy.wait()


class Copy:
    def __init__(self, choices):
        self.choices = choices
        for chosen, copy in choices:
            if chosen is None:
                copy.start()
            else:
                pl.when(chosen)(copy.start)

    def wait(self):
        self.choices[0][1].wait()


class DownTarget:
    outputs = 1

    def __call__(self, outs, piece, source, sem):
        place = outs[0].at[lanes_at(piece, source.shape[0])]
        return Copy([(None, pltpu.make_async_copy(source, place, sem))])


class UpTarget:
    outputs = 1

    def __call__(self, outs, piece, source, sem):
        rows, width = source.shape
        place = outs[0].at[lanes_at(piece & 1, rows), lanes_at(piece // 2, width)]
        return Copy([(None, pltpu.make_async_copy(source, place, sem))])


class PairTarget:
    outputs = 2

    def __call__(self, outs, piece, source, sem):
        rows = source.shape[0]
        return Copy([
            (
                piece // 4 == matrix,
                pltpu.make_async_copy(source, outs[matrix].at[lanes_at(piece & 3, rows)], sem),
            )
            for matrix in range(2)
        ])


def swap(rows, stage):
    axis, bit = stage
    return lax.ppermute(rows, axis, [(i, i ^ bit) for i in range(lax.axis_size(axis))])


def stage_list(first):
    every = []
    for axis in ("dp", "seq"):
        every += [(axis, 1 << k) for k in range(lax.axis_size(axis).bit_length() - 1)]
    return first + [stage for stage in every if stage not in first]


class Stream:
    def __init__(self, here, stages, target, out_shapes, name):
        self.here, self.stages, self.target = here, stages, target
        self.out_shapes, self.name, self.placed = out_shapes, name, None
        self.pieces = {}

    def begin(self, sent, kept):
        self.kept = kept
        self.got = [swap(piece, self.stages[1]) for piece in sent]

    def begin_core(self, sent, kept):
        self.kept, self.got = kept, swap(sent, self.stages[0])

    def a0(self, tokens):
        first, second, third, fourth = add_call((self.kept, self.got), 4, tokens)
        self.begin((first, second), (third, fourth))
        return first

    def a1(self, tokens):
        total = add_call((self.kept[0], self.got[0]), 1, tokens)[0]
        self.more = swap(total, self.stages[2])
        return total

    def a2(self, tokens):
        send, self.kept = add_call((self.kept[1], self.got[1], self.more), 2, tokens)
        self.got = swap(send, self.stages[3])
        return send

    def a3(self, tokens):
        send, self.kept = add_call((self.kept, self.got), 2, tokens)
        self.got = swap(send, self.stages[4])
        return send

    def a4(self, tokens):
        total = add_call((self.kept, self.got), 1, tokens)[0]
        for stage in self.stages[5:]:
            total = add_call((total, swap(total, stage)), 1)[0]
        self.kept, self.got = total, swap(total, self.stages[4])
        return total

    def j4(self, tokens):
        self.kept = join_call(self.kept, self.got, tokens)
        self.got = swap(self.kept, self.stages[3])
        return self.kept

    def j3(self, tokens):
        piece = join_call(self.kept, self.got, tokens)
        core, s1, s2 = self.stages[:3]
        near = swap(piece, s2)
        self.pieces = {0: piece, 1: near, 2: swap(piece, s1), 3: swap(near, s1)}
        for number in range(4):
            self.pieces[4 + number] = swap(self.pieces[number], core)
        return piece

    def place(self, numbers, tokens):
        sources = [self.pieces[number] for number in numbers]
        _, size, width = sources[0].shape
        args = [self.here] + sources
        aliases = {}
        if self.placed is not None:
            aliases = {len(args) + index: 1 + index for index in range(len(self.placed))}
            args += [Hbm(item) for item in self.placed]
        token, *self.placed = launch(
            functools.partial(place_kernel, numbers, self.target, self.stages), self.name, args,
            [TOKEN], out_hbm=[(shape, F32) for shape in self.out_shapes], tokens=tokens,
            aliases=aliases,
            scratch=[pltpu.VMEM((2, 4 * size, width), F32), pltpu.SemaphoreType.DMA((2,))],
        )
        return token

    def p0(self, tokens):
        return self.place((0, 4), tokens)

    def p1(self, tokens):
        return self.place((1, 2, 5, 6), tokens)

    def p2(self, tokens):
        return self.place((3, 7), tokens)


def add_rows_kernel(a_ref, b_ref, out_ref):
    out_ref[...] = a_ref[...] + b_ref[...]


def add_rows_call(rows, got, tokens):
    return launch(
        add_rows_kernel, "add_rows", (rows, got), [(rows.shape, F32)], tokens=tokens
    )[0]


def unpack_kernel(vec_ref, *out_refs):
    for start, out_ref in zip((V_BQ, V_BV, V_BO, V_BU, V_BD, V_GA, V_SA, V_GF, V_SF), out_refs):
        count = out_ref.shape[0] // vec_ref.shape[1]
        rows = [vec_ref[start + index : start + index + 1, :] for index in range(count)]
        out_ref[...] = jnp.concatenate(rows, axis=1).reshape(out_ref.shape[0])


def unpack_call(vec, ff):
    width = vec.shape[1]
    outs = shapes(*[((ff if index == 3 else width,), F32) for index in range(9)])
    return pl.pallas_call(
        unpack_kernel,
        in_specs=[VMEM],
        out_specs=[VMEM] * 9,
        out_shape=outs,
        compiler_params=pltpu.CompilerParams(vmem_limit_bytes=4 * 2**20),
        name="unpack",
    )(pltpu.with_memory_space_constraint(vec, pltpu.VMEM))


def from_peers(rows):
    size = lax.axis_size("seq")
    got = [
        lax.ppermute(rows, "seq", [(i, (i + shift) % size) for i in range(size)])
        for shift in range(1, size)
    ]
    return jnp.stack(got)


def shards(
    inputs, cluster_ids, masked, cotangent,
    w_query, w_key, w_value, w_out, w_up, w_down,
    bias_query, bias_value, bias_out, bias_up, bias_down,
    gain_attn, shift_attn, gain_ffn, shift_ffn,
):
    Estimate.now = 5.0
    seqs, tokens, width = inputs.shape
    every = range(seqs)
    ff = w_up.shape[1]
    core, x, y = ("dp", 1), ("dp", 2), ("seq", 1)
    z = ("dp", lax.axis_size("dp") // 4)
    stages_a = stage_list([core, x, y])
    stages_b = stage_list([core, z, y, x])
    stages_c = stage_list([core, y, z, x])
    stages_d = stage_list([core, x, y])
    here = Scalar(jnp.stack([lax.axis_index("dp"), lax.axis_index("seq")]).astype(jnp.int32))
    ids = cluster_ids.transpose(1, 0, 2)

    fetched = [
        Hbm(item)
        for item in (
            inputs, ids, w_query, w_key, w_value, bias_query, bias_value, gain_attn, shift_attn,
            masked,
        )
    ]
    more = [cotangent, w_out, w_up, w_down, bias_out, bias_down, gain_ffn, shift_ffn, bias_up]
    projected, sel = [], None
    for s in every:
        results, fetched, brought, found = project_call(
            s, here, fetched, more if s == seqs - 1 else []
        )
        projected.append(results)
        sel = found if s == 0 else sel
    normed, keys, values, own, message = zip(*projected)
    x_v, ids_v, wq_v, wk_v, wv_v, _, _, gain_v, _, _ = fetched
    cot_v, wo_v, wu_v, wd_v, bo_v, bd_v, gf_v, sf_v, _, up_rows = brought
    got = [from_peers(item) for item in message]
    attended, tokens_in = [], ()
    for s in every:
        attended.append(
            attend_call(own[s], message[s], got[s], keys[s], values[s], tokens=tokens_in)
        )
        tokens_in = (attended[s][1],)
    cent, count, out, lse, send = zip(*attended)
    got = [from_peers(item) for item in send]
    merges = []
    for s in every:
        merges.append(
            merge_call(s, out[s], lse[s], got[s], x_v, cot_v, sel, ids_v, tokens=tokens_in)
        )
        tokens_in = (merges[s][2],)
    ctx, merged, lse_all, ctx_m, x_m, cot_m, ids_m = zip(*merges)
    keep, away, ctx_m, attn_m, mid_m, vec, own, message = masked_call(
        here, ids_m, ctx_m, x_m, cot_m, wo_v, wu_v, wd_v, bo_v, up_rows, gf_v, sf_v
    )
    got_grad = from_peers(message)
    other = swap(away, core)
    weights = (wo_v, wu_v, wd_v, bo_v, up_rows, bd_v, gf_v, sf_v)
    blocks = [(s, start) for s in every for start in range(0, tokens, 256)]
    block_out = None

    def forward(*earlier):
        nonlocal block_out
        if blocks:
            s, start = blocks.pop(0)
            token, block_out = forward_call(s, start, x_v, ctx[s], weights, block_out, earlier)
            return token
        return earlier[0]

    a = Stream(here, stages_a, DownTarget(), [(ff, width)], "place_down")
    b = Stream(here, stages_b, UpTarget(), [(width, ff)], "place_up")
    c = Stream(here, stages_c, PairTarget(), [(width, width)] * 2, "place_out_value")
    d = Stream(here, stages_d, PairTarget(), [(width, width)] * 2, "place_key_query")
    back = {}
    waiting = {}
    grad_input = None

    def ffn_grads(stream, down, half):
        def act(tokens):
            waiting[stream, half] = ffn_grad_call(
                here, stream.stages, keep, other, ff, width, down, half, tokens
            )
            if half == 0:
                stream.begin(waiting[stream, 1], waiting[stream, 0])
            return waiting[stream, half][0]

        return act

    def pair_grads(stream, name, half):
        def act(tokens):
            if stream is c:
                first = [(ctx_m, attn_m)]
                second = [(normed[s], back[s][1]) for s in every]
            else:
                first = [(normed[s], back[s][0]) for s in every]
                second = [(normed[s], waiting["query", s]) for s in every]
            result = pair_grad_call(here, stream.stages, first, second, half, name, tokens)
            waiting[stream, half] = result
            if half == 0:
                stream.begin_core(waiting[stream, 1], result)
            return result

        return act

    def attend_back(s):
        def act(tokens):
            back[s] = attend_back_call(
                s, cent[s], lse_all[s], merged[s], own, got_grad, keys[s], values[s],
                tokens=tokens,
            )
            waiting["part", s] = from_peers(back[s][3])
            return back[s][3]

        return act

    def query(s):
        def act(tokens):
            waiting["query", s] = query_call(
                s, back[s][2], waiting["part", s], count[s], ids_v, width, tokens
            )
            return waiting["query", s]

        return act

    def back_input(s):
        def act(tokens):
            nonlocal grad_input, vec
            grad_input, vec = back_input_call(
                s, waiting["query", s], back[s][0], back[s][1], x_v, wq_v, wk_v, wv_v, gain_v, mid_m,
                sel, vec, former=grad_input, tokens=tokens,
            )
            return vec

        return act

    def forward_step(tokens):
        return forward(*tokens)

    def vector_step(stage):
        def act(tokens):
            nonlocal vec
            vec = add_rows_call(vec, waiting["vec"], tokens)
            place = stages_a.index(stage) + 1
            waiting["vec"] = swap(vec, stages_a[place]) if place < len(stages_a) else None
            return vec

        return act

    def vector_first(tokens):
        waiting["vec"] = swap(vec, stages_a[0])
        return tokens[0]

    def all_seqs(make):
        return [make(s) for s in every]

    def streams(*steps):
        return [getattr(stream, step) for stream, step in steps]

    order = [
        (forward_step, 0.1), (ffn_grads(a, True, 1), 5.0), (ffn_grads(a, True, 0), 5.0),
        (ffn_grads(b, False, 1), 5.0), (ffn_grads(b, False, 0), 5.0), (attend_back(0), 5.0),
        *[(step, 0.1) for step in all_seqs(attend_back)[1:]], (a.a1, 1.0),
        (pair_grads(c, "grad_out_value", 1), 5.0), (query(0), 5.0),
        *[(step, 5.0) for step in all_seqs(query)[1:]], (pair_grads(d, "grad_key_query", 1), 17.0),
        (pair_grads(c, "grad_out_value", 0), 5.0), (pair_grads(d, "grad_key_query", 0), 17.0),
        (b.a1, 1.0), (c.a0, 1.0), (a.a2, 1.0), (d.a0, 1.0), (back_input(0), 10.0),
        *[(step, 10.0) for step in all_seqs(back_input)[1:]], (vector_first, 1.0), (b.a2, 1.0),
        (a.a3, 1.0), (d.a1, 1.0), (vector_step(stages_a[0]), 1.0), (c.a1, 2.0), (forward_step, 5.0),
        (b.a3, 1.0), (a.a4, 0.1), (vector_step(stages_a[1]), 1.0), (d.a2, 1.0), (c.a2, 1.0),
        (vector_step(stages_a[2]), 1.0), (forward_step, 5.0), (c.a3, 1.0), (b.a4, 1.0), (a.j4, 1.0),
        (d.a3, 1.0), (vector_step(stages_a[3]), 1.0), (b.j4, 1.0), (c.a4, 5.0), (a.j3, 1.0),
        (d.a4, 1.0), (b.j3, 1.0), *[(forward_step, 5.0)] * (len(blocks) - 3), (c.j4, 1.0), (a.p0, 5.0),
        (d.j4, 1.0), (b.p0, 5.0), (c.j3, 1.0), (a.p1, 5.0), (d.j3, 1.0), (b.p1, 5.0), (c.p0, 8.0),
        (a.p2, 5.0), *[(step, 1.0) for step in [vector_step(stage) for stage in stages_a[4:]]],
        (d.p0, 16.0), (c.p1, 8.0), (b.p2, 5.0), (c.p2, 8.0), (d.p1, 16.0), (d.p2, 8.0),
    ]
    last = vec
    for step, Estimate.now in order:
        last = step((last,))
    (grad_w_down,), (grad_w_up,) = a.placed, b.placed
    grad_w_out, grad_w_value = c.placed
    grad_w_key, grad_w_query = d.placed
    return (
        block_out, grad_input,
        grad_w_query, grad_w_key, grad_w_value, grad_w_out, grad_w_up, grad_w_down,
        *unpack_call(vec, ff),
    )


def solution(mesh):
    rows = P("dp", "seq", None)
    return jax.shard_map(
        shards,
        mesh=mesh,
        in_specs=(rows, P("dp", None, "seq"), P("dp", "seq"), rows) + (P(),) * 15,
        out_specs=(rows, rows) + (P(),) * 15,
        check_vma=False,
    )
```

```python
import functools

import jax
import jax.numpy as jnp
from jax import lax
from jax.experimental import pallas as pl
from jax.experimental.pallas import tpu as pltpu
from jax.sharding import PartitionSpec as P

HEADS = 12
HDIM = 64
CLUSTERS = 100
MASK_MOST = 128
PAIRS = HEADS // 2
LANES = 2 * HDIM
ROWS = 112
SCALE = HDIM**-0.5
EPS = 1e-05
BF = jnp.bfloat16
F32 = jnp.float32

V_BQ, V_BV, V_BO, V_BU, V_BD, V_GA, V_SA, V_GF, V_SF = 0, 1, 2, 3, 7, 8, 9, 10, 11
VEC_ROWS = 16


def dot(a, b):
    return lax.dot_general(a, b, (((1,), (0,)), ((), ())), preferred_element_type=F32)


def dot_nt(a, b):
    return lax.dot_general(a, b, (((1,), (1,)), ((), ())), preferred_element_type=F32)


def dot_tn(a, b):
    return lax.dot_general(a, b, (((0,), (0,)), ((), ())), preferred_element_type=F32)


def norm_parts(rows):
    center = rows - jnp.mean(rows, axis=-1, keepdims=True)
    inverse = lax.rsqrt(jnp.mean(center * center, axis=-1, keepdims=True) + EPS)
    return center * inverse, inverse


def norm_back(incoming, unit, inverse, gain):
    scaled = incoming * gain
    return inverse * (
        scaled
        - jnp.mean(scaled, axis=-1, keepdims=True)
        - unit * jnp.mean(scaled * unit, axis=-1, keepdims=True)
    )


def normal_cdf(upper):
    return 0.5 * (1.0 + lax.erf(upper * (0.5**0.5)))


def lane_of(rows):
    return lax.broadcasted_iota(jnp.int32, (rows, LANES), 1)


def column(slab, index):
    picked = jnp.where(lane_of(slab.shape[0]) == index, slab, 0.0)
    return jnp.sum(picked, axis=1, keepdims=True)


def member_pair(ids, seq, pair):
    tokens = ids.shape[-1]
    rows = lax.broadcasted_iota(jnp.int32, (ROWS, tokens), 0)
    one = [
        jnp.where(rows == ids[2 * pair + side, seq : seq + 1, :], 1.0, 0.0).astype(BF)
        for side in range(2)
    ]
    return jnp.concatenate(one, axis=0)


def row_blocks(rows, act, block=256):
    def step(index, carry):
        act(pl.ds(pl.multiple_of(index * block, block), block))
        return carry

    lax.fori_loop(0, rows // block, step, 0)


def vector(ref):
    return ref[...].astype(F32).reshape(1, -1)


def pick_rows(sel):
    slots = lax.broadcasted_iota(jnp.int32, (MASK_MOST, sel.shape[-1]), 0)
    return jnp.where(slots == sel, 1.0, 0.0).astype(BF)


def stack_pair(both):
    left = lane_of(both.shape[0]) < HDIM
    return jnp.concatenate(
        [jnp.where(left, both, 0.0).astype(BF), jnp.where(left, 0.0, both).astype(BF)], axis=0
    )


def unstack_pair(stacked):
    left = lane_of(ROWS) < HDIM
    return jnp.where(left, stacked[:ROWS], stacked[ROWS:])


def pair_lanes(pair):
    return pl.ds(pl.multiple_of(pair * LANES, LANES), LANES)


class Hbm:
    def __init__(self, array):
        self.array = array


class Scalar:
    def __init__(self, array):
        self.array = array


def rank_from(here_ref, stages):
    rank = 0
    for place, (axis, bit) in enumerate(stages[:5]):
        index = here_ref[0 if axis == "dp" else 1]
        rank = rank + ((index >> (bit.bit_length() - 1)) & 1) * (16 >> place)
    return rank


def shapes(*items):
    return [jax.ShapeDtypeStruct(shape, dtype) for shape, dtype in items]


class Estimate:
    now = 5.0


TOKEN = ((8, LANES), F32)
VMEM = pl.BlockSpec(memory_space=pltpu.VMEM)
HBM = pl.BlockSpec(memory_space=pltpu.HBM)
ANY = pl.BlockSpec(memory_space=pl.ANY)


def launch(kernel, name, args, outs, out_hbm=(), tokens=(), scratch=(), mib=16, aliases=None):
    count = len(tokens)
    operands, in_specs = list(tokens), [ANY] * count
    for arg in args:
        if isinstance(arg, Hbm):
            operands.append(pltpu.with_memory_space_constraint(arg.array, pltpu.HBM))
            in_specs.append(HBM)
        elif isinstance(arg, Scalar):
            operands.append(arg.array)
            in_specs.append(pl.BlockSpec(memory_space=pltpu.SMEM))
        else:
            operands.append(pltpu.with_memory_space_constraint(arg, pltpu.VMEM))
            in_specs.append(VMEM)
    out_shape = [pltpu.VMEM(shape, dtype) for shape, dtype in outs] + shapes(*out_hbm)
    return pl.pallas_call(
        lambda *refs: kernel(*refs[count:]),
        in_specs=in_specs,
        out_specs=[VMEM] * len(outs) + [HBM] * len(out_hbm),
        out_shape=out_shape,
        scratch_shapes=list(scratch),
        input_output_aliases={count + a: b for a, b in (aliases or {}).items()},
        compiler_params=pltpu.CompilerParams(vmem_limit_bytes=mib * 2**20),
        cost_estimate=pl.CostEstimate(
            flops=int(Estimate.now * 1e9), bytes_accessed=0, transcendentals=0
        ),
        name=name,
    )(*operands)


def load(pairs, sems):
    copies = [
        pltpu.make_async_copy(source, target, sems.at[index])
        for index, (source, target) in enumerate(pairs)
    ]
    for copy in copies:
        copy.start()
    return copies


def project_rows(
    seq, x, ids_ref, wq_ref, wk_ref, wv_ref, bq_ref, bv_ref, gain_ref, shift_ref,
    masked_ref, normed_ref, key_ref, value_ref, own_ref, message_ref, sel_ref, query_s, ready,
):
    ready("x")
    if sel_ref is not None:
        tokens = masked_ref.shape[1]
        before = jnp.where(
            lax.broadcasted_iota(jnp.int32, (tokens, tokens), 0)
            <= lax.broadcasted_iota(jnp.int32, (tokens, tokens), 1),
            1.0,
            0.0,
        ).astype(BF)
        for s in range(masked_ref.shape[0]):
            row = masked_ref[s : s + 1, :]
            spread = jnp.broadcast_to(row.astype(F32), (16, tokens)).astype(BF)
            slot = dot(spread, before)[:1].astype(jnp.int32) - 1
            sel_ref[s : s + 1, :] = jnp.where(row == 1, slot, -1)
    length = normed_ref.shape[0]

    def norm(rows):
        unit, _ = norm_parts(x[seq, rows, :].astype(F32))
        normed_ref[rows, :] = (unit * vector(gain_ref) + vector(shift_ref)).astype(BF)

    def query(rows):
        query_s[rows, :] = (dot(normed_ref[rows, :], wq_ref[...]) + vector(bq_ref)).astype(BF)

    def key_value(rows):
        normed = normed_ref[rows, :]
        key_ref[rows, :] = dot(normed, wk_ref[...]).astype(BF)
        value_ref[rows, :] = (dot(normed, wv_ref[...]) + vector(bv_ref)).astype(BF)

    row_blocks(length, norm)
    ready("q")
    row_blocks(length, query)
    lane = lane_of(ROWS)
    ones = jnp.ones((length, LANES), BF)

    def step(pair, slab):
        right = jnp.concatenate([query_s[:, pair_lanes(pair)], ones], axis=1)
        sums = dot(member_pair(ids_ref, seq, pair), right)
        own = unstack_pair(sums[:, :LANES])
        own_ref[pair] = own
        message_ref[pair] = own.astype(BF)
        for side in range(2):
            count = sums[side * ROWS : (side + 1) * ROWS, LANES:]
            low = jnp.minimum(count, 256.0)
            slab = slab + jnp.where(lane == 2 * pair + side, low, 0.0)
            slab = slab + jnp.where(lane == 16 + 2 * pair + side, count - low, 0.0)
        return slab

    slab = lax.fori_loop(0, PAIRS, step, jnp.zeros((ROWS, LANES), F32), unroll=2)
    message_ref[PAIRS] = slab.astype(BF)
    ready("kv")
    row_blocks(length, key_value)


SLAB = (PAIRS, ROWS, LANES)
SLAB_MORE = (PAIRS + 1, ROWS, LANES)


def project_outs(x):
    _, tokens, width = x.shape
    rows = ((tokens, width), BF)
    return [rows, rows, rows, (SLAB, F32), (SLAB_MORE, BF)], [pltpu.VMEM((tokens, width), BF)]


def project_call(seq, here, fetched, more):
    first = isinstance(fetched[0], Hbm)
    brought = [item.array for item in fetched] if first else []
    x = brought[0] if first else fetched[0]
    outs, scratch = project_outs(x)
    seqs = x.shape[0]
    count, extra = len(fetched), len(more)
    loads = count + seqs - 1 if first else 0
    own_outs = 6 if first else 5
    if first:
        outs = outs + [((seqs, x.shape[1]), jnp.int32)]

    def kernel(here_ref, *refs):
        sources, refs = refs[:count], refs[count:]
        more_in, refs = refs[:extra], refs[extra:]
        results, refs = refs[:own_outs], refs[own_outs:]
        targets, refs = (refs[:count], refs[count:]) if first else (sources, refs)
        more_out, refs = refs[:extra], refs[extra:]
        row_ref, refs = (refs[0], refs[1:]) if extra else (None, refs)
        query_s, sems = refs
        results = tuple(results) + (() if first else (None,))
        pairs = []
        if first:
            order = [seq] + [s for s in range(seqs) if s != seq]
            rows = [(sources[0].at[s], targets[0].at[s]) for s in order]
            pairs = [rows[0]] + list(zip(sources[1:], targets[1:])) + rows[1:]
        pairs = pairs + list(zip(more_in, more_out))
        copies = load(pairs, sems)
        groups = {"x": [], "q": [], "kv": []}
        if first:
            groups = {"x": [0, 7, 8, 9], "q": [1, 2, 5], "kv": [3, 4, 6]}
        waited = set()

        def ready(name):
            for index in groups[name]:
                copies[index].wait()
                waited.add(index)

        project_rows(seq, *targets, *results, query_s, ready)
        for index, copy in enumerate(copies):
            if index not in waited:
                copy.wait()
        if extra:
            row_ref[...] = vector(more_out[-1])

    brings = [(item.shape, item.dtype) for item in brought] + [
        (item.shape, item.dtype) for item in more
    ]
    if extra:
        brings.append(((1, more[-1].shape[0]), F32))
    results = launch(
        kernel, "project", [here] + list(fetched) + [Hbm(item) for item in more], outs + brings,
        scratch=scratch + [pltpu.SemaphoreType.DMA((loads + extra,))],
    )
    if first:
        return results[:5], results[6 : 6 + count], results[6 + count :], results[5]
    return results[:5], fetched, results[5:], None


def attend_kernel(
    own_ref, message_ref, got_ref, key_ref, value_ref,
    cent_ref, count_ref, out_ref, lse_ref, send_ref,
):
    peers = got_ref.shape[0]
    lane = lane_of(ROWS)
    slab = message_ref[PAIRS].astype(F32)
    for peer in range(peers):
        slab = slab + got_ref[peer, PAIRS].astype(F32)
    count = jnp.maximum(slab + pltpu.roll(slab, LANES - 16, 1), 1.0)
    count_ref[...] = count

    def step(pair, lses):
        total = own_ref[pair]
        for peer in range(peers):
            total = total + got_ref[peer, pair].astype(F32)
        divisor = jnp.where(lane < HDIM, column(count, 2 * pair), column(count, 2 * pair + 1))
        cent = (total / divisor).astype(BF)
        cent_ref[pair] = cent
        scores = dot_nt(stack_pair(cent.astype(F32)), key_ref[:, pair_lanes(pair)]) * SCALE
        peak = jnp.max(scores, axis=1, keepdims=True)
        raised = jnp.exp(scores - peak)
        mass = jnp.sum(raised, axis=1, keepdims=True)
        mixed = unstack_pair(dot(raised.astype(BF), value_ref[:, pair_lanes(pair)]) / mass)
        out_ref[pair] = mixed
        send_ref[pair] = mixed.astype(BF)
        lse = peak + jnp.log(mass)
        lses = lses + jnp.where(lane == 2 * pair, lse[:ROWS], 0.0)
        return lses + jnp.where(lane == 2 * pair + 1, lse[ROWS:], 0.0)

    lses = lax.fori_loop(0, PAIRS, step, jnp.zeros((ROWS, LANES), F32), unroll=2)
    lse_ref[...] = lses
    high = lses.astype(BF).astype(F32)
    rest = lses - high
    middle = rest.astype(BF).astype(F32)
    low = (rest - middle).astype(BF).astype(F32)
    send_ref[PAIRS] = (high + pltpu.roll(middle, 16, 1) + pltpu.roll(low, 32, 1)).astype(BF)


def attend_call(*args, tokens=()):
    one = ((ROWS, LANES), F32)
    return launch(
        attend_kernel, "attend", args, [(SLAB, BF), one, (SLAB, F32), one, (SLAB_MORE, BF)],
        tokens=tokens,
    )


def merge_kernel(
    seq, out_ref, lse_ref, got_ref, x_ref, cot_ref, sel_ref, ids_ref,
    ctx_ref, merged_ref, lse_all_ref, ctx_m_ref, x_m_ref, cot_m_ref, ids_m_ref,
):
    peers = got_ref.shape[0]
    lane = lane_of(ROWS)
    lses = [lse_ref[...]]
    for peer in range(peers):
        slab = got_ref[peer, PAIRS].astype(F32)
        lses.append(slab + pltpu.roll(slab, LANES - 16, 1) + pltpu.roll(slab, LANES - 32, 1))
    peak = functools.reduce(jnp.maximum, lses)
    merged = peak + jnp.log(sum(jnp.exp(item - peak) for item in lses))
    lse_all_ref[...] = merged
    portions = [jnp.exp(item - merged) for item in lses]

    def gather(pair, carry):
        total = jnp.zeros((ROWS, LANES), F32)
        for index, portion in enumerate(portions):
            part = out_ref[pair] if index == 0 else got_ref[index - 1, pair].astype(F32)
            weight = jnp.where(
                lane < HDIM, column(portion, 2 * pair), column(portion, 2 * pair + 1)
            )
            total = total + weight * part
        merged_ref[pair] = total
        member = member_pair(ids_ref, seq, pair)
        ctx_ref[:, pair_lanes(pair)] = dot_tn(member, stack_pair(total)).astype(BF)
        return carry

    lax.fori_loop(0, PAIRS, gather, 0, unroll=2)
    pick = pick_rows(sel_ref[seq : seq + 1, :])
    ctx_m_ref[...] = dot(pick, ctx_ref[...]).astype(BF)
    x_m_ref[...] = dot(pick, x_ref[seq]).astype(BF)
    cot_m_ref[...] = dot(pick, cot_ref[seq]).astype(BF)
    heads = [ids_ref[head, seq : seq + 1, :].astype(F32) for head in range(HEADS)]
    heads = jnp.concatenate(heads + [jnp.zeros_like(heads[0])] * (16 - HEADS), axis=0)
    ids_m_ref[...] = dot_nt(heads.astype(BF), pick).astype(jnp.int32)


def merge_call(seq, out, lse, got, x, cot, sel, ids, tokens=()):
    _, length, width = x.shape
    picked = ((MASK_MOST, width), BF)
    return launch(
        functools.partial(merge_kernel, seq), "merge", (out, lse, got, x, cot, sel, ids),
        [((length, width), BF), (SLAB, F32), ((ROWS, LANES), F32), picked, picked, picked,
            ((16, MASK_MOST), jnp.int32)],
        tokens=tokens,
    )


def masked_kernel(seqs, *refs):
    here_ref, ids_refs = refs[0], refs[1 : 1 + seqs]
    rest = refs[1 + seqs :]
    ctx_refs, x_refs, cot_refs = rest[:seqs], rest[seqs : 2 * seqs], rest[2 * seqs : 3 * seqs]
    (
        wo_ref, wu_ref, wd_ref, bo_ref, bu_ref, gain_ref, shift_ref,
        keep_a, send_a, keep_b, send_b, ctx_m_ref, attn_m_ref, mid_m_ref, vec_ref,
    ) = rest[3 * seqs : 3 * seqs + 15]
    own_ref, message_ref, middle_s, back_s = rest[3 * seqs + 15 :]
    width = wo_ref.shape[0]
    ff_block = width
    ff_blocks = wu_ref.shape[1] // ff_block
    half_blocks = ff_blocks // 2
    tail = half_blocks * ff_block
    core = here_ref[0] & 1
    vec_ref[...] = jnp.zeros_like(vec_ref)
    for s in range(seqs):
        rows = pl.ds(s * MASK_MOST, MASK_MOST)
        ctx_m_ref[rows, :] = ctx_refs[s][...]
        middle_s[rows, :] = x_refs[s][...].astype(F32)
        keep_a[rows, tail:] = cot_refs[s][...]
        send_a[rows, tail:] = cot_refs[s][...]
    middle = middle_s[...] + (dot(ctx_m_ref[...], wo_ref[...]) + vector(bo_ref))
    middle_s[...] = middle
    unit, _ = norm_parts(middle)
    low = (unit * vector(gain_ref) + vector(shift_ref)).astype(BF)
    keep_b[:, tail:] = low
    send_b[:, tail:] = low
    back_s[...] = jnp.zeros_like(back_s)

    def feed(block, carry):
        lanes = pl.ds(pl.multiple_of(block * ff_block, ff_block), ff_block)
        upper = dot(keep_b[:, tail:], wu_ref[:, lanes]) + bu_ref[:, lanes]
        cdf = normal_cdf(upper)
        hidden = (upper * cdf).astype(BF)
        slope = cdf + upper * (jnp.exp(-0.5 * upper * upper) * 0.3989422804014327)
        grad_y = keep_a[:, tail:]
        grad_upper = (dot_nt(grad_y, wd_ref[lanes, :]) * slope).astype(BF)
        back_s[...] += dot_nt(grad_upper, wu_ref[:, lanes])
        vec_ref[pl.ds(V_BU + block, 1), :] = jnp.sum(
            grad_upper.astype(F32), axis=0, keepdims=True
        )
        half = block // half_blocks
        inner = block - half * half_blocks
        place = pl.ds(pl.multiple_of(inner * ff_block, ff_block), ff_block)

        @pl.when(half == core)
        def _():
            keep_a[:, place] = hidden
            keep_b[:, place] = grad_upper

        @pl.when(half != core)
        def _():
            send_a[:, place] = hidden
            send_b[:, place] = grad_upper

        return carry

    lax.fori_loop(0, ff_blocks, feed, 0, unroll=1)
    unit, inverse = norm_parts(middle_s[...])
    incoming = back_s[...]
    grad_y = keep_a[:, tail:].astype(F32)
    grad_middle = grad_y + norm_back(incoming, unit, inverse, vector(gain_ref))
    mid_m_ref[...] = grad_middle
    grad_attn = grad_middle.astype(BF)
    attn_m_ref[...] = grad_attn
    vec_ref[V_BD : V_BD + 1, :] = jnp.sum(grad_y, axis=0, keepdims=True)
    vec_ref[V_BO : V_BO + 1, :] = jnp.sum(grad_attn.astype(F32), axis=0, keepdims=True)
    vec_ref[V_GF : V_GF + 1, :] = jnp.sum(incoming * unit, axis=0, keepdims=True)
    vec_ref[V_SF : V_SF + 1, :] = jnp.sum(incoming, axis=0, keepdims=True)
    back_s[...] = dot_nt(grad_attn, wo_ref[...])
    for s in range(seqs):
        clusters = lax.broadcasted_iota(jnp.int32, (ROWS, MASK_MOST), 0)

        def scatter(pair, carry, s=s, clusters=clusters):
            sides = [
                jnp.where(clusters == ids_refs[s][pl.ds(2 * pair + side, 1), :], 1.0, 0.0)
                for side in range(2)
            ]
            member = jnp.concatenate(sides, axis=0).astype(BF)
            rows = back_s[s * MASK_MOST : (s + 1) * MASK_MOST, pair_lanes(pair)]
            high = rows.astype(BF)
            low = (rows - high.astype(F32)).astype(BF)
            own = unstack_pair(dot(member, high) + dot(member, low))
            own_ref[s, pair] = own
            message_ref[s, pair] = own.astype(BF)
            return carry

        lax.fori_loop(0, PAIRS, scatter, 0, unroll=2)


def masked_call(here, ids, ctx, x, cot, *weights):
    seqs = len(ctx)
    width, ff = weights[1].shape
    picked = seqs * MASK_MOST
    wide = ((picked, ff // 2 + width), BF)
    out = launch(
        functools.partial(masked_kernel, seqs), "masked_rows",
        (here, *ids, *ctx, *x, *cot, *weights),
        [
            wide, wide, wide, wide, ((picked, width), BF), ((picked, width), BF), ((picked, width), F32),
            ((VEC_ROWS, width), F32), ((seqs,) + SLAB, F32), ((seqs,) + SLAB, BF),
        ],
        scratch=[pltpu.VMEM((picked, width), F32), pltpu.VMEM((picked, width), F32)],
    )
    return out


def forward_kernel(
    seq, start, x_ref, ctx_ref, wo_ref, wu_ref, wd_ref, bo_ref, bu_ref, bd_ref, gain_ref, shift_ref,
    *rest,
):
    token_ref, y_ref, low_s, total_s, out_s, sem = rest[-6:]
    token_ref[...] = jnp.zeros_like(token_ref)
    rows = pl.ds(start, low_s.shape[0])
    middle = x_ref[seq, rows, :].astype(F32) + (dot(ctx_ref[rows, :], wo_ref[...]) + vector(bo_ref))
    unit, _ = norm_parts(middle)
    low_s[...] = (unit * vector(gain_ref) + vector(shift_ref)).astype(BF)
    total_s[...] = middle + vector(bd_ref)
    block = x_ref.shape[2]

    def feed(index, carry):
        lanes = pl.ds(pl.multiple_of(index * block, block), block)
        upper = dot(low_s[...], wu_ref[:, lanes]) + bu_ref[:, lanes]
        hidden = (upper * normal_cdf(upper)).astype(BF)
        total_s[...] += dot(hidden, wd_ref[lanes, :])
        return carry

    lax.fori_loop(0, wu_ref.shape[1] // block, feed, 0, unroll=1)
    out_s[...] = total_s[...].astype(BF)
    copy = pltpu.make_async_copy(out_s, y_ref.at[seq, rows], sem)
    copy.start()
    copy.wait()


def forward_call(seq, start, x, ctx, weights, former, tokens, block=256):
    width = x.shape[2]
    args = [x, ctx, *weights]
    aliases = {}
    if former is not None:
        aliases = {len(args): 1}
        args.append(Hbm(former))
    return launch(
        functools.partial(forward_kernel, seq, start), "forward_rows", args, [TOKEN],
        out_hbm=[(x.shape, BF)], tokens=tokens, aliases=aliases,
        scratch=[
            pltpu.VMEM((block, width), BF), pltpu.VMEM((block, width), F32),
            pltpu.VMEM((block, width), BF), pltpu.SemaphoreType.DMA,
        ],
    )


def attend_back_kernel(
    seq, cent_ref, lse_ref, merged_ref, own_ref, got_ref, key_ref, value_ref,
    grad_key_ref, grad_value_ref, part_ref, send_ref,
):
    peers = got_ref.shape[0]
    lane = lane_of(ROWS)
    lses = lse_ref[...]

    def step(pair, carry):
        total = own_ref[seq, pair]
        for peer in range(peers):
            total = total + got_ref[peer, seq, pair].astype(F32)
        grad_cent = total.astype(BF).astype(F32)
        product = grad_cent * merged_ref[pair]
        delta = jnp.concatenate(
            [
                jnp.sum(jnp.where(lane < HDIM, product, 0.0), axis=1, keepdims=True),
                jnp.sum(jnp.where(lane < HDIM, 0.0, product), axis=1, keepdims=True),
            ],
            axis=0,
        )
        lse = jnp.concatenate([column(lses, 2 * pair), column(lses, 2 * pair + 1)], axis=0)
        cents = stack_pair(cent_ref[pair].astype(F32))
        grads = stack_pair(grad_cent)
        keys = key_ref[:, pair_lanes(pair)]
        weights = jnp.exp(dot_nt(cents, keys) * SCALE - lse)
        grad_weights = dot_nt(grads, value_ref[:, pair_lanes(pair)])
        grad_scores = (weights * (grad_weights - delta)).astype(BF)
        part = unstack_pair(dot(grad_scores, keys))
        part_ref[pair] = part
        send_ref[pair] = part.astype(BF)
        grad_key_ref[:, pair_lanes(pair)] = (dot_tn(grad_scores, cents) * SCALE).astype(BF)
        grad_value_ref[:, pair_lanes(pair)] = dot_tn(weights.astype(BF), grads).astype(BF)
        return carry

    lax.fori_loop(0, PAIRS, step, 0, unroll=2)


def attend_back_call(seq, *args, tokens=()):
    rows = (args[5].shape, BF)
    return launch(
        functools.partial(attend_back_kernel, seq), "attend_back", args, [rows, rows, (SLAB, F32), (SLAB, BF)],
        tokens=tokens,
    )


def query_kernel(seq, part_ref, got_ref, count_ref, ids_ref, gq_ref):
    peers = got_ref.shape[0]
    lane = lane_of(ROWS)
    count = count_ref[...]

    def step(pair, carry):
        total = part_ref[pair]
        for peer in range(peers):
            total = total + got_ref[peer, pair].astype(F32)
        grad_cent = (total * SCALE).astype(BF).astype(F32)
        divisor = jnp.where(lane < HDIM, column(count, 2 * pair), column(count, 2 * pair + 1))
        spread = stack_pair(grad_cent / divisor)
        member = member_pair(ids_ref, seq, pair)
        gq_ref[:, pair_lanes(pair)] = dot_tn(member, spread).astype(BF)
        return carry

    lax.fori_loop(0, PAIRS, step, 0, unroll=2)


def query_call(seq, part, got, count, ids, width, tokens=()):
    return launch(
        functools.partial(query_kernel, seq), "query_grad", (part, got, count, ids),
        [((ids.shape[-1], width), BF)], tokens=tokens,
    )[0]


def back_input_kernel(
    seq, gq_ref, gk_ref, gv_ref, x_ref, wq_ref, wk_ref, wv_ref, gain_ref, mid_ref, sel_ref,
    vec_in_ref, *rest,
):
    vec_ref, gx_ref, out_s, sem = rest[-4:]
    vec_ref[...] = vec_in_ref[...]
    middle = mid_ref[seq * MASK_MOST : (seq + 1) * MASK_MOST, :]
    high = middle.astype(BF)
    low = (middle - high.astype(F32)).astype(BF)

    def act(rows):
        grad_query, grad_value = gq_ref[rows, :], gv_ref[rows, :]
        incoming = (
            dot_nt(grad_query, wq_ref[...])
            + dot_nt(gk_ref[rows, :], wk_ref[...])
            + dot_nt(grad_value, wv_ref[...])
        )
        unit, inverse = norm_parts(x_ref[seq, rows, :].astype(F32))
        grad = norm_back(incoming, unit, inverse, vector(gain_ref))
        pick = pick_rows(sel_ref[seq : seq + 1, rows])
        out_s[rows, :] = (grad + (dot_tn(pick, high) + dot_tn(pick, low))).astype(BF)
        vec_ref[V_BQ : V_BQ + 1, :] += jnp.sum(grad_query.astype(F32), axis=0, keepdims=True)
        vec_ref[V_BV : V_BV + 1, :] += jnp.sum(grad_value.astype(F32), axis=0, keepdims=True)
        vec_ref[V_GA : V_GA + 1, :] += jnp.sum(incoming * unit, axis=0, keepdims=True)
        vec_ref[V_SA : V_SA + 1, :] += jnp.sum(incoming, axis=0, keepdims=True)

    row_blocks(gq_ref.shape[0], act)
    copy = pltpu.make_async_copy(out_s, gx_ref.at[seq], sem)
    copy.start()
    copy.wait()


def back_input_call(seq, *args, former, tokens=()):
    args = list(args)
    x, vec = args[3], args[10]
    aliases = {}
    if former is not None:
        aliases = {len(args): 1}
        args.append(Hbm(former))
    vec, grad = launch(
        functools.partial(back_input_kernel, seq), "back_input", args, [(vec.shape, F32)],
        out_hbm=[(x.shape, BF)], tokens=tokens, aliases=aliases,
        scratch=[pltpu.VMEM(x.shape[1:], BF), pltpu.SemaphoreType.DMA],
    )
    return grad, vec


def store_chunks(out_ref, base, product, rank, per_group):
    size = product.shape[0] // per_group
    for index in range(per_group):
        out_ref[base + (index ^ (rank & (per_group - 1)))] = product[
            index * size : (index + 1) * size
        ].astype(BF)


def lanes_at(start, size):
    return pl.ds(pl.multiple_of(start * size, size), size)


def ffn_grad_kernel(ff, width, down, half, stages, here_ref, keep_ref, got_ref, *out_refs):
    rank = rank_from(here_ref, stages) & 15
    rows = ff // 8
    for index, out_ref in enumerate(out_refs):
        group = (2 * half + 1 - index) ^ (rank // 4)
        if down:
            left, right = lanes_at(group, rows), pl.ds(ff // 2, width)
        else:
            left = lanes_at(ff // 2 // rows + (group & 1), rows)
            right = lanes_at(group // 2, width)
        product = dot_tn(keep_ref[:, left], keep_ref[:, right]) + dot_tn(
            got_ref[:, left], got_ref[:, right]
        )
        store_chunks(out_ref, 0, product, rank, 4)


def ffn_grad_call(here, stages, keep, got, ff, width, down, half, tokens=()):
    return launch(
        functools.partial(ffn_grad_kernel, ff, width, down, half, stages),
        "grad_down" if down else "grad_up", (here, keep, got),
        [((4, ff // 32, width), BF)] * 2, tokens=tokens,
    )


def pair_grad_kernel(splits, half, stages, here_ref, *refs):
    out_ref = refs[-1]
    rank = rank_from(here_ref, stages)
    rows = refs[0].shape[1] // 2
    pairs = [(refs[2 * k], refs[2 * k + 1]) for k in range(len(refs) // 2)]

    def step(index, carry):
        group = (2 * half + index) ^ (rank // 8)
        lanes = lanes_at(group & 1, rows)

        def fill(some):
            product = sum(dot_tn(left[:, lanes], right[...]) for left, right in some)
            store_chunks(out_ref, 8 * index, product, rank, 8)

        @pl.when(group < 2)
        def _():
            fill(pairs[:splits])

        @pl.when(group >= 2)
        def _():
            fill(pairs[splits:])

        return carry

    lax.fori_loop(0, 2, step, 0)


def pair_grad_call(here, stages, first, second, half, name, tokens=()):
    args = [array for pair in first + second for array in pair]
    width = args[0].shape[1]
    return launch(
        functools.partial(pair_grad_kernel, len(first), half, stages), name, (here, *args),
        [((16, width // 16, width), BF)], tokens=tokens,
    )[0]


def add_kernel(terms, *refs):
    inputs, outs = refs[:terms], refs[terms:]
    count = outs[0].shape[0]

    def step(index, carry):
        for place, out_ref in enumerate(reversed(outs)):
            total = inputs[0][place * count + index].astype(F32)
            for more in inputs[1:]:
                total = total + more[place * count + index].astype(F32)
            out_ref[index] = total.astype(BF)
        return carry

    lax.fori_loop(0, count, step, 0)


def add_call(args, parts, tokens=()):
    count, size, width = args[0].shape
    return launch(
        functools.partial(add_kernel, len(args)), "add", args,
        [((count // parts, size, width), BF)] * parts, tokens=tokens,
    )


def join_kernel(keep_ref, got_ref, out_ref):
    count = keep_ref.shape[0]
    out_ref[:count] = keep_ref[...]
    out_ref[count:] = got_ref[...]


def join_call(keep, got, tokens=()):
    count, size, width = keep.shape
    return launch(
        join_kernel, "join", (keep, got), [((2 * count, size, width), BF)], tokens=tokens,
    )[0]


def place_kernel(pieces, target, stages, here_ref, *refs):
    sources, refs = refs[: len(pieces)], refs[-target.outputs - 3 :]
    token_ref, outs, stage_s, sems = refs[0], refs[1:-2], refs[-2], refs[-1]
    token_ref[...] = jnp.zeros_like(token_ref)
    rank = rank_from(here_ref, stages)
    size = sources[0].shape[1]
    copies = []
    for index, (piece, source) in enumerate(zip(pieces, sources)):
        slot = index % 2
        if index >= 2:
            copies[index - 2].wait()

        def step(inner, carry, source=source, slot=slot):
            rows = pl.ds(pl.multiple_of(inner * size, size), size)
            stage_s[slot, rows, :] = source[inner ^ (rank & 3)].astype(F32)
            return carry

        lax.fori_loop(0, 4, step, 0)
        copies.append(target(outs, piece ^ (rank // 4), stage_s.at[slot], sems.at[slot]))
    for copy in copies[-2:]:
        copy.wait()


class Copy:
    def __init__(self, choices):
        self.choices = choices
        for chosen, copy in choices:
            if chosen is None:
                copy.start()
            else:
                pl.when(chosen)(copy.start)

    def wait(self):
        self.choices[0][1].wait()


class DownTarget:
    outputs = 1

    def __call__(self, outs, piece, source, sem):
        place = outs[0].at[lanes_at(piece, source.shape[0])]
        return Copy([(None, pltpu.make_async_copy(source, place, sem))])


class UpTarget:
    outputs = 1

    def __call__(self, outs, piece, source, sem):
        rows, width = source.shape
        place = outs[0].at[lanes_at(piece & 1, rows), lanes_at(piece // 2, width)]
        return Copy([(None, pltpu.make_async_copy(source, place, sem))])


class PairTarget:
    outputs = 2

    def __call__(self, outs, piece, source, sem):
        rows = source.shape[0]
        return Copy([
            (
                piece // 4 == matrix,
                pltpu.make_async_copy(source, outs[matrix].at[lanes_at(piece & 3, rows)], sem),
            )
            for matrix in range(2)
        ])


def swap(rows, stage):
    axis, bit = stage
    return lax.ppermute(rows, axis, [(i, i ^ bit) for i in range(lax.axis_size(axis))])


def stage_list(first):
    every = []
    for axis in ("dp", "seq"):
        every += [(axis, 1 << k) for k in range(lax.axis_size(axis).bit_length() - 1)]
    return first + [stage for stage in every if stage not in first]


class Stream:
    def __init__(self, here, stages, target, out_shapes, name):
        self.here, self.stages, self.target = here, stages, target
        self.out_shapes, self.name, self.placed = out_shapes, name, None
        self.pieces = {}

    def begin(self, sent, kept):
        self.kept = kept
        self.got = [swap(piece, self.stages[1]) for piece in sent]

    def begin_core(self, sent, kept):
        self.kept, self.got = kept, swap(sent, self.stages[0])

    def a0(self, tokens):
        first, second, third, fourth = add_call((self.kept, self.got), 4, tokens)
        self.begin((first, second), (third, fourth))
        return first

    def a1(self, tokens):
        total = add_call((self.kept[0], self.got[0]), 1, tokens)[0]
        self.more = swap(total, self.stages[2])
        return total

    def a2(self, tokens):
        send, self.kept = add_call((self.kept[1], self.got[1], self.more), 2, tokens)
        self.got = swap(send, self.stages[3])
        return send

    def a3(self, tokens):
        send, self.kept = add_call((self.kept, self.got), 2, tokens)
        self.got = swap(send, self.stages[4])
        return send

    def a4(self, tokens):
        total = add_call((self.kept, self.got), 1, tokens)[0]
        for stage in self.stages[5:]:
            total = add_call((total, swap(total, stage)), 1)[0]
        self.kept, self.got = total, swap(total, self.stages[4])
        return total

    def j4(self, tokens):
        self.kept = join_call(self.kept, self.got, tokens)
        self.got = swap(self.kept, self.stages[3])
        return self.kept

    def j3(self, tokens):
        piece = join_call(self.kept, self.got, tokens)
        core, s1, s2 = self.stages[:3]
        near = swap(piece, s2)
        self.pieces = {0: piece, 1: near, 2: swap(piece, s1), 3: swap(near, s1)}
        for number in range(4):
            self.pieces[4 + number] = swap(self.pieces[number], core)
        return piece

    def place(self, numbers, tokens):
        sources = [self.pieces[number] for number in numbers]
        _, size, width = sources[0].shape
        args = [self.here] + sources
        aliases = {}
        if self.placed is not None:
            aliases = {len(args) + index: 1 + index for index in range(len(self.placed))}
            args += [Hbm(item) for item in self.placed]
        token, *self.placed = launch(
            functools.partial(place_kernel, numbers, self.target, self.stages), self.name, args,
            [TOKEN], out_hbm=[(shape, F32) for shape in self.out_shapes], tokens=tokens,
            aliases=aliases,
            scratch=[pltpu.VMEM((2, 4 * size, width), F32), pltpu.SemaphoreType.DMA((2,))],
        )
        return token

    def p0(self, tokens):
        return self.place((0, 4), tokens)

    def p1(self, tokens):
        return self.place((1, 2, 5, 6), tokens)

    def p2(self, tokens):
        return self.place((3, 7), tokens)


def add_rows_kernel(a_ref, b_ref, out_ref):
    out_ref[...] = a_ref[...] + b_ref[...]


def add_rows_call(rows, got, tokens):
    return launch(
        add_rows_kernel, "add_rows", (rows, got), [(rows.shape, F32)], tokens=tokens
    )[0]


def unpack_kernel(vec_ref, *out_refs):
    for start, out_ref in zip((V_BQ, V_BV, V_BO, V_BU, V_BD, V_GA, V_SA, V_GF, V_SF), out_refs):
        count = out_ref.shape[0] // vec_ref.shape[1]
        rows = [vec_ref[start + index : start + index + 1, :] for index in range(count)]
        out_ref[...] = jnp.concatenate(rows, axis=1).reshape(out_ref.shape[0])


def unpack_call(vec, ff):
    width = vec.shape[1]
    outs = shapes(*[((ff if index == 3 else width,), F32) for index in range(9)])
    return pl.pallas_call(
        unpack_kernel,
        in_specs=[VMEM],
        out_specs=[VMEM] * 9,
        out_shape=outs,
        compiler_params=pltpu.CompilerParams(vmem_limit_bytes=4 * 2**20),
        name="unpack",
    )(pltpu.with_memory_space_constraint(vec, pltpu.VMEM))


def from_peers(rows):
    size = lax.axis_size("seq")
    got = [
        lax.ppermute(rows, "seq", [(i, (i + shift) % size) for i in range(size)])
        for shift in range(1, size)
    ]
    return jnp.stack(got)


def shards(
    inputs, cluster_ids, masked, cotangent,
    w_query, w_key, w_value, w_out, w_up, w_down,
    bias_query, bias_value, bias_out, bias_up, bias_down,
    gain_attn, shift_attn, gain_ffn, shift_ffn,
):
    Estimate.now = 5.0
    seqs, tokens, width = inputs.shape
    every = range(seqs)
    ff = w_up.shape[1]
    core, x, y = ("dp", 1), ("dp", 2), ("seq", 1)
    z = ("dp", lax.axis_size("dp") // 4)
    stages_a = stage_list([core, x, y])
    stages_b = stage_list([core, z, y, x])
    stages_c = stage_list([core, y, z, x])
    stages_d = stage_list([core, x, y])
    here = Scalar(jnp.stack([lax.axis_index("dp"), lax.axis_index("seq")]).astype(jnp.int32))
    ids = cluster_ids.transpose(1, 0, 2)

    fetched = [
        Hbm(item)
        for item in (
            inputs, ids, w_query, w_key, w_value, bias_query, bias_value, gain_attn, shift_attn,
            masked,
        )
    ]
    more = [cotangent, w_out, w_up, w_down, bias_out, bias_down, gain_ffn, shift_ffn, bias_up]
    projected, sel = [], None
    for s in every:
        results, fetched, brought, found = project_call(
            s, here, fetched, more if s == seqs - 1 else []
        )
        projected.append(results)
        sel = found if s == 0 else sel
    normed, keys, values, own, message = zip(*projected)
    x_v, ids_v, wq_v, wk_v, wv_v, _, _, gain_v, _, _ = fetched
    cot_v, wo_v, wu_v, wd_v, bo_v, bd_v, gf_v, sf_v, _, up_rows = brought
    got = [from_peers(item) for item in message]
    attended, tokens_in = [], ()
    for s in every:
        attended.append(
            attend_call(own[s], message[s], got[s], keys[s], values[s], tokens=tokens_in)
        )
        tokens_in = (attended[s][1],)
    cent, count, out, lse, send = zip(*attended)
    got = [from_peers(item) for item in send]
    merges = []
    for s in every:
        merges.append(
            merge_call(s, out[s], lse[s], got[s], x_v, cot_v, sel, ids_v, tokens=tokens_in)
        )
        tokens_in = (merges[s][2],)
    ctx, merged, lse_all, ctx_m, x_m, cot_m, ids_m = zip(*merges)
    keep_a, away_a, keep_b, away_b, ctx_m, attn_m, mid_m, vec, own, message = masked_call(
        here, ids_m, ctx_m, x_m, cot_m, wo_v, wu_v, wd_v, bo_v, up_rows, gf_v, sf_v
    )
    got_grad = from_peers(message)
    other_a, other_b = swap(away_a, core), swap(away_b, core)
    weights = (wo_v, wu_v, wd_v, bo_v, up_rows, bd_v, gf_v, sf_v)
    blocks = [(s, start) for s in every for start in range(0, tokens, 256)]
    block_out = None

    def forward(*earlier):
        nonlocal block_out
        if blocks:
            s, start = blocks.pop(0)
            token, block_out = forward_call(s, start, x_v, ctx[s], weights, block_out, earlier)
            return token
        return earlier[0]

    a = Stream(here, stages_a, DownTarget(), [(ff, width)], "place_down")
    b = Stream(here, stages_b, UpTarget(), [(width, ff)], "place_up")
    c = Stream(here, stages_c, PairTarget(), [(width, width)] * 2, "place_out_value")
    d = Stream(here, stages_d, PairTarget(), [(width, width)] * 2, "place_key_query")
    back = {}
    waiting = {}
    grad_input = None

    def ffn_grads(stream, down, half):
        def act(tokens):
            waiting[stream, half] = ffn_grad_call(
                here, stream.stages, keep_a if down else keep_b, other_a if down else other_b,
                ff, width, down, half, tokens,
            )
            if half == 0:
                stream.begin(waiting[stream, 1], waiting[stream, 0])
            return waiting[stream, half][0]

        return act

    def pair_grads(stream, name, half):
        def act(tokens):
            if stream is c:
                first = [(ctx_m, attn_m)]
                second = [(normed[s], back[s][1]) for s in every]
            else:
                first = [(normed[s], back[s][0]) for s in every]
                second = [(normed[s], waiting["query", s]) for s in every]
            result = pair_grad_call(here, stream.stages, first, second, half, name, tokens)
            waiting[stream, half] = result
            if half == 0:
                stream.begin_core(waiting[stream, 1], result)
            return result

        return act

    def attend_back(s):
        def act(tokens):
            back[s] = attend_back_call(
                s, cent[s], lse_all[s], merged[s], own, got_grad, keys[s], values[s],
                tokens=tokens,
            )
            waiting["part", s] = from_peers(back[s][3])
            return back[s][3]

        return act

    def query(s):
        def act(tokens):
            waiting["query", s] = query_call(
                s, back[s][2], waiting["part", s], count[s], ids_v, width, tokens
            )
            return waiting["query", s]

        return act

    def back_input(s):
        def act(tokens):
            nonlocal grad_input, vec
            grad_input, vec = back_input_call(
                s, waiting["query", s], back[s][0], back[s][1], x_v, wq_v, wk_v, wv_v, gain_v, mid_m,
                sel, vec, former=grad_input, tokens=tokens,
            )
            return vec

        return act

    def forward_step(tokens):
        return forward(*tokens)

    def vector_step(stage):
        def act(tokens):
            nonlocal vec
            vec = add_rows_call(vec, waiting["vec"], tokens)
            place = stages_a.index(stage) + 1
            waiting["vec"] = swap(vec, stages_a[place]) if place < len(stages_a) else None
            return vec

        return act

    def vector_first(tokens):
        waiting["vec"] = swap(vec, stages_a[0])
        return tokens[0]

    def all_seqs(make):
        return [make(s) for s in every]

    def streams(*steps):
        return [getattr(stream, step) for stream, step in steps]

    order = [
        (ffn_grads(a, True, 1), 5.0), (ffn_grads(a, True, 0), 5.0), (ffn_grads(b, False, 1), 5.0),
        (ffn_grads(b, False, 0), 5.0), (forward_step, 0.1), (attend_back(0), 5.0),
        *[(step, 0.1) for step in all_seqs(attend_back)[1:]], (a.a1, 1.0),
        (pair_grads(c, "grad_out_value", 1), 5.0), (query(0), 5.0),
        *[(step, 5.0) for step in all_seqs(query)[1:]], (pair_grads(d, "grad_key_query", 1), 17.0),
        (pair_grads(c, "grad_out_value", 0), 5.0), (pair_grads(d, "grad_key_query", 0), 17.0),
        (b.a1, 1.0), (c.a0, 1.0), (a.a2, 1.0), (d.a0, 1.0), (back_input(0), 10.0),
        *[(step, 10.0) for step in all_seqs(back_input)[1:]], (vector_first, 1.0), (b.a2, 1.0),
        (a.a3, 1.0), (vector_step(stages_a[0]), 1.0), (d.a1, 1.0), (c.a1, 2.0), (forward_step, 5.0),
        (b.a3, 1.0), (a.a4, 0.1), (vector_step(stages_a[1]), 1.0), (d.a2, 1.0), (c.a2, 1.0),
        (vector_step(stages_a[2]), 1.0), (forward_step, 5.0), (b.a4, 1.0), (c.a3, 1.0), (a.j4, 1.0),
        (d.a3, 1.0), (vector_step(stages_a[3]), 1.0), (b.j4, 0.1), (c.a4, 5.0), (a.j3, 1.0),
        (d.a4, 1.0), (b.j3, 1.0), *[(forward_step, 5.0)] * (len(blocks) - 3), (c.j4, 1.0), (d.j4, 1.0),
        (b.p0, 5.0), (a.p0, 5.0), (c.j3, 1.0), (a.p1, 5.0), (d.j3, 1.0), (b.p1, 5.0), (c.p0, 8.0),
        (a.p2, 5.0), (c.p1, 8.0),
        *[(step, 1.0) for step in [vector_step(stage) for stage in stages_a[4:]]], (d.p0, 16.0),
        (b.p2, 5.0), (c.p2, 8.0), (d.p1, 16.0), (d.p2, 8.0),
    ]
    last = vec
    for step, Estimate.now in order:
        last = step((last,))
    (grad_w_down,), (grad_w_up,) = a.placed, b.placed
    grad_w_out, grad_w_value = c.placed
    grad_w_key, grad_w_query = d.placed
    return (
        block_out, grad_input,
        grad_w_query, grad_w_key, grad_w_value, grad_w_out, grad_w_up, grad_w_down,
        *unpack_call(vec, ff),
    )


def solution(mesh):
    rows = P("dp", "seq", None)
    return jax.shard_map(
        shards,
        mesh=mesh,
        in_specs=(rows, P("dp", None, "seq"), P("dp", "seq"), rows) + (P(),) * 15,
        out_specs=(rows, rows) + (P(),) * 15,
        check_vma=False,
    )
```

```python
import functools

import jax
import jax.numpy as jnp
from jax import lax
from jax.experimental import pallas as pl
from jax.experimental.pallas import tpu as pltpu
from jax.sharding import PartitionSpec as P

HEADS = 12
HDIM = 64
CLUSTERS = 100
MASK_MOST = 128
PAIRS = HEADS // 2
LANES = 2 * HDIM
ROWS = 112
SCALE = HDIM**-0.5
EPS = 1e-05
BF = jnp.bfloat16
F32 = jnp.float32

V_BQ, V_BV, V_BO, V_BU, V_BD, V_GA, V_SA, V_GF, V_SF = 0, 1, 2, 3, 7, 8, 9, 10, 11
VEC_ROWS = 16


def dot(a, b):
    return lax.dot_general(a, b, (((1,), (0,)), ((), ())), preferred_element_type=F32)


def dot_nt(a, b):
    return lax.dot_general(a, b, (((1,), (1,)), ((), ())), preferred_element_type=F32)


def dot_tn(a, b):
    return lax.dot_general(a, b, (((0,), (0,)), ((), ())), preferred_element_type=F32)


def norm_parts(rows):
    center = rows - jnp.mean(rows, axis=-1, keepdims=True)
    inverse = lax.rsqrt(jnp.mean(center * center, axis=-1, keepdims=True) + EPS)
    return center * inverse, inverse


def norm_back(incoming, unit, inverse, gain):
    scaled = incoming * gain
    return inverse * (
        scaled
        - jnp.mean(scaled, axis=-1, keepdims=True)
        - unit * jnp.mean(scaled * unit, axis=-1, keepdims=True)
    )


def normal_cdf(upper):
    return 0.5 * (1.0 + lax.erf(upper * (0.5**0.5)))


def lane_of(rows):
    return lax.broadcasted_iota(jnp.int32, (rows, LANES), 1)


def column(slab, index):
    picked = jnp.where(lane_of(slab.shape[0]) == index, slab, 0.0)
    return jnp.sum(picked, axis=1, keepdims=True)


def member_pair(ids, seq, pair):
    tokens = ids.shape[-1]
    rows = lax.broadcasted_iota(jnp.int32, (ROWS, tokens), 0)
    one = [
        jnp.where(rows == ids[2 * pair + side, seq : seq + 1, :], 1.0, 0.0).astype(BF)
        for side in range(2)
    ]
    return jnp.concatenate(one, axis=0)


def row_blocks(rows, act, block=256):
    def step(index, carry):
        act(pl.ds(pl.multiple_of(index * block, block), block))
        return carry

    lax.fori_loop(0, rows // block, step, 0)


def vector(ref):
    return ref[...].astype(F32).reshape(1, -1)


def pick_rows(sel):
    slots = lax.broadcasted_iota(jnp.int32, (MASK_MOST, sel.shape[-1]), 0)
    return jnp.where(slots == sel, 1.0, 0.0).astype(BF)


def stack_pair(both):
    left = lane_of(both.shape[0]) < HDIM
    return jnp.concatenate(
        [jnp.where(left, both, 0.0).astype(BF), jnp.where(left, 0.0, both).astype(BF)], axis=0
    )


def unstack_pair(stacked):
    left = lane_of(ROWS) < HDIM
    return jnp.where(left, stacked[:ROWS], stacked[ROWS:])


def pair_lanes(pair):
    return pl.ds(pl.multiple_of(pair * LANES, LANES), LANES)


class Hbm:
    def __init__(self, array):
        self.array = array


class Scalar:
    def __init__(self, array):
        self.array = array


def rank_from(here_ref, stages):
    rank = 0
    for place, (axis, bit) in enumerate(stages[:5]):
        index = here_ref[0 if axis == "dp" else 1]
        rank = rank + ((index >> (bit.bit_length() - 1)) & 1) * (16 >> place)
    return rank


def shapes(*items):
    return [jax.ShapeDtypeStruct(shape, dtype) for shape, dtype in items]


class Estimate:
    now = 5.0


TOKEN = ((8, LANES), F32)
VMEM = pl.BlockSpec(memory_space=pltpu.VMEM)
HBM = pl.BlockSpec(memory_space=pltpu.HBM)
ANY = pl.BlockSpec(memory_space=pl.ANY)


def launch(kernel, name, args, outs, out_hbm=(), tokens=(), scratch=(), mib=16, aliases=None):
    count = len(tokens)
    operands, in_specs = list(tokens), [ANY] * count
    for arg in args:
        if isinstance(arg, Hbm):
            operands.append(pltpu.with_memory_space_constraint(arg.array, pltpu.HBM))
            in_specs.append(HBM)
        elif isinstance(arg, Scalar):
            operands.append(arg.array)
            in_specs.append(pl.BlockSpec(memory_space=pltpu.SMEM))
        else:
            operands.append(pltpu.with_memory_space_constraint(arg, pltpu.VMEM))
            in_specs.append(VMEM)
    out_shape = [pltpu.VMEM(shape, dtype) for shape, dtype in outs] + shapes(*out_hbm)
    return pl.pallas_call(
        lambda *refs: kernel(*refs[count:]),
        in_specs=in_specs,
        out_specs=[VMEM] * len(outs) + [HBM] * len(out_hbm),
        out_shape=out_shape,
        scratch_shapes=list(scratch),
        input_output_aliases={count + a: b for a, b in (aliases or {}).items()},
        compiler_params=pltpu.CompilerParams(vmem_limit_bytes=mib * 2**20),
        cost_estimate=pl.CostEstimate(
            flops=int(Estimate.now * 1e9), bytes_accessed=0, transcendentals=0
        ),
        name=name,
    )(*operands)


def load(pairs, sems):
    copies = [
        pltpu.make_async_copy(source, target, sems.at[index])
        for index, (source, target) in enumerate(pairs)
    ]
    for copy in copies:
        copy.start()
    return copies


def project_rows(
    seq, x, ids_ref, wq_ref, wk_ref, wv_ref, bq_ref, bv_ref, gain_ref, shift_ref,
    masked_ref, normed_ref, key_ref, value_ref, own_ref, message_ref, sel_ref, query_s, ready,
):
    ready("x")
    if sel_ref is not None:
        tokens = masked_ref.shape[1]
        before = jnp.where(
            lax.broadcasted_iota(jnp.int32, (tokens, tokens), 0)
            <= lax.broadcasted_iota(jnp.int32, (tokens, tokens), 1),
            1.0,
            0.0,
        ).astype(BF)
        for s in range(masked_ref.shape[0]):
            row = masked_ref[s : s + 1, :]
            spread = jnp.broadcast_to(row.astype(F32), (16, tokens)).astype(BF)
            slot = dot(spread, before)[:1].astype(jnp.int32) - 1
            sel_ref[s : s + 1, :] = jnp.where(row == 1, slot, -1)
    length = normed_ref.shape[0]

    def norm(rows):
        unit, _ = norm_parts(x[seq, rows, :].astype(F32))
        normed_ref[rows, :] = (unit * vector(gain_ref) + vector(shift_ref)).astype(BF)

    def query(rows):
        query_s[rows, :] = (dot(normed_ref[rows, :], wq_ref[...]) + vector(bq_ref)).astype(BF)

    def key_value(rows):
        normed = normed_ref[rows, :]
        key_ref[rows, :] = dot(normed, wk_ref[...]).astype(BF)
        value_ref[rows, :] = (dot(normed, wv_ref[...]) + vector(bv_ref)).astype(BF)

    row_blocks(length, norm)
    ready("q")
    row_blocks(length, query)
    lane = lane_of(ROWS)
    ones = jnp.ones((length, LANES), BF)

    def step(pair, slab):
        right = jnp.concatenate([query_s[:, pair_lanes(pair)], ones], axis=1)
        sums = dot(member_pair(ids_ref, seq, pair), right)
        own = unstack_pair(sums[:, :LANES])
        own_ref[pair] = own
        message_ref[pair] = own.astype(BF)
        for side in range(2):
            count = sums[side * ROWS : (side + 1) * ROWS, LANES:]
            low = jnp.minimum(count, 256.0)
            slab = slab + jnp.where(lane == 2 * pair + side, low, 0.0)
            slab = slab + jnp.where(lane == 16 + 2 * pair + side, count - low, 0.0)
        return slab

    slab = lax.fori_loop(0, PAIRS, step, jnp.zeros((ROWS, LANES), F32), unroll=2)
    message_ref[PAIRS] = slab.astype(BF)
    ready("kv")
    row_blocks(length, key_value)


SLAB = (PAIRS, ROWS, LANES)
SLAB_MORE = (PAIRS + 1, ROWS, LANES)


def project_outs(x):
    _, tokens, width = x.shape
    rows = ((tokens, width), BF)
    return [rows, rows, rows, (SLAB, F32), (SLAB_MORE, BF)], [pltpu.VMEM((tokens, width), BF)]


def project_call(seq, here, fetched, more):
    first = isinstance(fetched[0], Hbm)
    brought = [item.array for item in fetched] if first else []
    x = brought[0] if first else fetched[0]
    outs, scratch = project_outs(x)
    seqs = x.shape[0]
    count, extra = len(fetched), len(more)
    loads = count + seqs - 1 if first else 0
    own_outs = 6 if first else 5
    if first:
        outs = outs + [((seqs, x.shape[1]), jnp.int32)]

    def kernel(here_ref, *refs):
        sources, refs = refs[:count], refs[count:]
        more_in, refs = refs[:extra], refs[extra:]
        results, refs = refs[:own_outs], refs[own_outs:]
        targets, refs = (refs[:count], refs[count:]) if first else (sources, refs)
        more_out, refs = refs[:extra], refs[extra:]
        row_ref, refs = (refs[0], refs[1:]) if extra else (None, refs)
        query_s, sems = refs
        results = tuple(results) + (() if first else (None,))
        pairs = []
        if first:
            order = [seq] + [s for s in range(seqs) if s != seq]
            rows = [(sources[0].at[s], targets[0].at[s]) for s in order]
            pairs = [rows[0]] + list(zip(sources[1:], targets[1:])) + rows[1:]
        pairs = pairs + list(zip(more_in, more_out))
        copies = load(pairs, sems)
        groups = {"x": [], "q": [], "kv": []}
        if first:
            groups = {"x": [0, 7, 8, 9], "q": [1, 2, 5], "kv": [3, 4, 6]}
        waited = set()

        def ready(name):
            for index in groups[name]:
                copies[index].wait()
                waited.add(index)

        project_rows(seq, *targets, *results, query_s, ready)
        for index, copy in enumerate(copies):
            if index not in waited:
                copy.wait()
        if extra:
            row_ref[...] = vector(more_out[-1])

    brings = [(item.shape, item.dtype) for item in brought] + [
        (item.shape, item.dtype) for item in more
    ]
    if extra:
        brings.append(((1, more[-1].shape[0]), F32))
    results = launch(
        kernel, "project", [here] + list(fetched) + [Hbm(item) for item in more], outs + brings,
        scratch=scratch + [pltpu.SemaphoreType.DMA((loads + extra,))],
    )
    if first:
        return results[:5], results[6 : 6 + count], results[6 + count :], results[5]
    return results[:5], fetched, results[5:], None


def attend_kernel(
    own_ref, message_ref, got_ref, key_ref, value_ref,
    cent_ref, count_ref, out_ref, lse_ref, send_ref,
):
    peers = got_ref.shape[0]
    lane = lane_of(ROWS)
    slab = message_ref[PAIRS].astype(F32)
    for peer in range(peers):
        slab = slab + got_ref[peer, PAIRS].astype(F32)
    count = jnp.maximum(slab + pltpu.roll(slab, LANES - 16, 1), 1.0)
    count_ref[...] = count

    def step(pair, lses):
        total = own_ref[pair]
        for peer in range(peers):
            total = total + got_ref[peer, pair].astype(F32)
        divisor = jnp.where(lane < HDIM, column(count, 2 * pair), column(count, 2 * pair + 1))
        cent = (total / divisor).astype(BF)
        cent_ref[pair] = cent
        scores = dot_nt(stack_pair(cent.astype(F32)), key_ref[:, pair_lanes(pair)]) * SCALE
        peak = jnp.max(scores, axis=1, keepdims=True)
        raised = jnp.exp(scores - peak)
        mass = jnp.sum(raised, axis=1, keepdims=True)
        mixed = unstack_pair(dot(raised.astype(BF), value_ref[:, pair_lanes(pair)]) / mass)
        out_ref[pair] = mixed
        send_ref[pair] = mixed.astype(BF)
        lse = peak + jnp.log(mass)
        lses = lses + jnp.where(lane == 2 * pair, lse[:ROWS], 0.0)
        return lses + jnp.where(lane == 2 * pair + 1, lse[ROWS:], 0.0)

    lses = lax.fori_loop(0, PAIRS, step, jnp.zeros((ROWS, LANES), F32), unroll=2)
    lse_ref[...] = lses
    high = lses.astype(BF).astype(F32)
    rest = lses - high
    middle = rest.astype(BF).astype(F32)
    low = (rest - middle).astype(BF).astype(F32)
    send_ref[PAIRS] = (high + pltpu.roll(middle, 16, 1) + pltpu.roll(low, 32, 1)).astype(BF)


def attend_call(*args, tokens=()):
    one = ((ROWS, LANES), F32)
    return launch(
        attend_kernel, "attend", args, [(SLAB, BF), one, (SLAB, F32), one, (SLAB_MORE, BF)],
        tokens=tokens,
    )


def merge_kernel(
    seq, out_ref, lse_ref, got_ref, x_ref, cot_ref, sel_ref, ids_ref,
    ctx_ref, merged_ref, lse_all_ref, ctx_m_ref, x_m_ref, cot_m_ref, ids_m_ref,
):
    peers = got_ref.shape[0]
    lane = lane_of(ROWS)
    lses = [lse_ref[...]]
    for peer in range(peers):
        slab = got_ref[peer, PAIRS].astype(F32)
        lses.append(slab + pltpu.roll(slab, LANES - 16, 1) + pltpu.roll(slab, LANES - 32, 1))
    peak = functools.reduce(jnp.maximum, lses)
    merged = peak + jnp.log(sum(jnp.exp(item - peak) for item in lses))
    lse_all_ref[...] = merged
    portions = [jnp.exp(item - merged) for item in lses]

    def gather(pair, carry):
        total = jnp.zeros((ROWS, LANES), F32)
        for index, portion in enumerate(portions):
            part = out_ref[pair] if index == 0 else got_ref[index - 1, pair].astype(F32)
            weight = jnp.where(
                lane < HDIM, column(portion, 2 * pair), column(portion, 2 * pair + 1)
            )
            total = total + weight * part
        merged_ref[pair] = total
        member = member_pair(ids_ref, seq, pair)
        ctx_ref[:, pair_lanes(pair)] = dot_tn(member, stack_pair(total)).astype(BF)
        return carry

    lax.fori_loop(0, PAIRS, gather, 0, unroll=2)
    pick = pick_rows(sel_ref[seq : seq + 1, :])
    ctx_m_ref[...] = dot(pick, ctx_ref[...]).astype(BF)
    x_m_ref[...] = dot(pick, x_ref[seq]).astype(BF)
    cot_m_ref[...] = dot(pick, cot_ref[seq]).astype(BF)
    heads = [ids_ref[head, seq : seq + 1, :].astype(F32) for head in range(HEADS)]
    heads = jnp.concatenate(heads + [jnp.zeros_like(heads[0])] * (16 - HEADS), axis=0)
    ids_m_ref[...] = dot_nt(heads.astype(BF), pick).astype(jnp.int32)


def merge_call(seq, out, lse, got, x, cot, sel, ids, tokens=()):
    _, length, width = x.shape
    picked = ((MASK_MOST, width), BF)
    return launch(
        functools.partial(merge_kernel, seq), "merge", (out, lse, got, x, cot, sel, ids),
        [((length, width), BF), (SLAB, F32), ((ROWS, LANES), F32), picked, picked, picked,
            ((16, MASK_MOST), jnp.int32)],
        tokens=tokens,
    )


def masked_kernel(seqs, *refs):
    here_ref, ids_refs = refs[0], refs[1 : 1 + seqs]
    rest = refs[1 + seqs :]
    ctx_refs, x_refs, cot_refs = rest[:seqs], rest[seqs : 2 * seqs], rest[2 * seqs : 3 * seqs]
    (
        wo_ref, wu_ref, wd_ref, bo_ref, bu_ref, gain_ref, shift_ref,
        keep_a, send_a, keep_b, send_b, ctx_m_ref, attn_m_ref, mid_m_ref, vec_ref,
    ) = rest[3 * seqs : 3 * seqs + 15]
    own_ref, message_ref, middle_s, back_s = rest[3 * seqs + 15 :]
    width = wo_ref.shape[0]
    ff_block = width
    ff_blocks = wu_ref.shape[1] // ff_block
    half_blocks = ff_blocks // 2
    tail = half_blocks * ff_block
    core = here_ref[0] & 1
    vec_ref[...] = jnp.zeros_like(vec_ref)
    for s in range(seqs):
        rows = pl.ds(s * MASK_MOST, MASK_MOST)
        ctx_m_ref[rows, :] = ctx_refs[s][...]
        middle_s[rows, :] = x_refs[s][...].astype(F32)
        keep_a[rows, tail:] = cot_refs[s][...]
        send_a[rows, tail:] = cot_refs[s][...]
    middle = middle_s[...] + (dot(ctx_m_ref[...], wo_ref[...]) + vector(bo_ref))
    middle_s[...] = middle
    unit, _ = norm_parts(middle)
    low = (unit * vector(gain_ref) + vector(shift_ref)).astype(BF)
    keep_b[:, tail:] = low
    send_b[:, tail:] = low
    back_s[...] = jnp.zeros_like(back_s)

    def feed(block, carry):
        lanes = pl.ds(pl.multiple_of(block * ff_block, ff_block), ff_block)
        upper = dot(keep_b[:, tail:], wu_ref[:, lanes]) + bu_ref[:, lanes]
        cdf = normal_cdf(upper)
        hidden = (upper * cdf).astype(BF)
        slope = cdf + upper * (jnp.exp(-0.5 * upper * upper) * 0.3989422804014327)
        grad_y = keep_a[:, tail:]
        grad_upper = (dot_nt(grad_y, wd_ref[lanes, :]) * slope).astype(BF)
        back_s[...] += dot_nt(grad_upper, wu_ref[:, lanes])
        vec_ref[pl.ds(V_BU + block, 1), :] = jnp.sum(
            grad_upper.astype(F32), axis=0, keepdims=True
        )
        half = block // half_blocks
        inner = block - half * half_blocks
        place = pl.ds(pl.multiple_of(inner * ff_block, ff_block), ff_block)

        @pl.when(half == core)
        def _():
            keep_a[:, place] = hidden
            keep_b[:, place] = grad_upper

        @pl.when(half != core)
        def _():
            send_a[:, place] = hidden
            send_b[:, place] = grad_upper

        return carry

    lax.fori_loop(0, ff_blocks, feed, 0, unroll=1)
    unit, inverse = norm_parts(middle_s[...])
    incoming = back_s[...]
    grad_y = keep_a[:, tail:].astype(F32)
    grad_middle = grad_y + norm_back(incoming, unit, inverse, vector(gain_ref))
    mid_m_ref[...] = grad_middle
    grad_attn = grad_middle.astype(BF)
    attn_m_ref[...] = grad_attn
    vec_ref[V_BD : V_BD + 1, :] = jnp.sum(grad_y, axis=0, keepdims=True)
    vec_ref[V_BO : V_BO + 1, :] = jnp.sum(grad_attn.astype(F32), axis=0, keepdims=True)
    vec_ref[V_GF : V_GF + 1, :] = jnp.sum(incoming * unit, axis=0, keepdims=True)
    vec_ref[V_SF : V_SF + 1, :] = jnp.sum(incoming, axis=0, keepdims=True)
    back_s[...] = dot_nt(grad_attn, wo_ref[...])
    for s in range(seqs):
        clusters = lax.broadcasted_iota(jnp.int32, (ROWS, MASK_MOST), 0)

        def scatter(pair, carry, s=s, clusters=clusters):
            sides = [
                jnp.where(clusters == ids_refs[s][pl.ds(2 * pair + side, 1), :], 1.0, 0.0)
                for side in range(2)
            ]
            member = jnp.concatenate(sides, axis=0).astype(BF)
            rows = back_s[s * MASK_MOST : (s + 1) * MASK_MOST, pair_lanes(pair)]
            high = rows.astype(BF)
            low = (rows - high.astype(F32)).astype(BF)
            own = unstack_pair(dot(member, high) + dot(member, low))
            own_ref[s, pair] = own
            message_ref[s, pair] = own.astype(BF)
            return carry

        lax.fori_loop(0, PAIRS, scatter, 0, unroll=2)


def masked_call(here, ids, ctx, x, cot, *weights):
    seqs = len(ctx)
    width, ff = weights[1].shape
    picked = seqs * MASK_MOST
    wide = ((picked, ff // 2 + width), BF)
    out = launch(
        functools.partial(masked_kernel, seqs), "masked_rows",
        (here, *ids, *ctx, *x, *cot, *weights),
        [
            wide, wide, wide, wide, ((picked, width), BF), ((picked, width), BF), ((picked, width), F32),
            ((VEC_ROWS, width), F32), ((seqs,) + SLAB, F32), ((seqs,) + SLAB, BF),
        ],
        scratch=[pltpu.VMEM((picked, width), F32), pltpu.VMEM((picked, width), F32)],
    )
    return out


def forward_kernel(
    seq, start, x_ref, ctx_ref, wo_ref, wu_ref, wd_ref, bo_ref, bu_ref, bd_ref, gain_ref, shift_ref,
    *rest,
):
    token_ref, y_ref, low_s, total_s, out_s, sem = rest[-6:]
    token_ref[...] = jnp.zeros_like(token_ref)
    rows = pl.ds(start, low_s.shape[0])
    middle = x_ref[seq, rows, :].astype(F32) + (dot(ctx_ref[rows, :], wo_ref[...]) + vector(bo_ref))
    unit, _ = norm_parts(middle)
    low_s[...] = (unit * vector(gain_ref) + vector(shift_ref)).astype(BF)
    total_s[...] = middle + vector(bd_ref)
    block = x_ref.shape[2]

    def feed(index, carry):
        lanes = pl.ds(pl.multiple_of(index * block, block), block)
        upper = dot(low_s[...], wu_ref[:, lanes]) + bu_ref[:, lanes]
        hidden = (upper * normal_cdf(upper)).astype(BF)
        total_s[...] += dot(hidden, wd_ref[lanes, :])
        return carry

    lax.fori_loop(0, wu_ref.shape[1] // block, feed, 0, unroll=1)
    out_s[...] = total_s[...].astype(BF)
    copy = pltpu.make_async_copy(out_s, y_ref.at[seq, rows], sem)
    copy.start()
    copy.wait()


def forward_call(seq, start, x, ctx, weights, former, tokens, block=256):
    width = x.shape[2]
    args = [x, ctx, *weights]
    aliases = {}
    if former is not None:
        aliases = {len(args): 1}
        args.append(Hbm(former))
    return launch(
        functools.partial(forward_kernel, seq, start), "forward_rows", args, [TOKEN],
        out_hbm=[(x.shape, BF)], tokens=tokens, aliases=aliases,
        scratch=[
            pltpu.VMEM((block, width), BF), pltpu.VMEM((block, width), F32),
            pltpu.VMEM((block, width), BF), pltpu.SemaphoreType.DMA,
        ],
    )


def attend_back_kernel(
    seq, cent_ref, lse_ref, merged_ref, own_ref, got_ref, key_ref, value_ref,
    grad_key_ref, grad_value_ref, part_ref, send_ref,
):
    peers = got_ref.shape[0]
    lane = lane_of(ROWS)
    lses = lse_ref[...]

    def step(pair, carry):
        total = own_ref[seq, pair]
        for peer in range(peers):
            total = total + got_ref[peer, seq, pair].astype(F32)
        grad_cent = total.astype(BF).astype(F32)
        product = grad_cent * merged_ref[pair]
        delta = jnp.concatenate(
            [
                jnp.sum(jnp.where(lane < HDIM, product, 0.0), axis=1, keepdims=True),
                jnp.sum(jnp.where(lane < HDIM, 0.0, product), axis=1, keepdims=True),
            ],
            axis=0,
        )
        lse = jnp.concatenate([column(lses, 2 * pair), column(lses, 2 * pair + 1)], axis=0)
        cents = stack_pair(cent_ref[pair].astype(F32))
        grads = stack_pair(grad_cent)
        keys = key_ref[:, pair_lanes(pair)]
        weights = jnp.exp(dot_nt(cents, keys) * SCALE - lse)
        grad_weights = dot_nt(grads, value_ref[:, pair_lanes(pair)])
        grad_scores = (weights * (grad_weights - delta)).astype(BF)
        part = unstack_pair(dot(grad_scores, keys))
        part_ref[pair] = part
        send_ref[pair] = part.astype(BF)
        grad_key_ref[:, pair_lanes(pair)] = (dot_tn(grad_scores, cents) * SCALE).astype(BF)
        grad_value_ref[:, pair_lanes(pair)] = dot_tn(weights.astype(BF), grads).astype(BF)
        return carry

    lax.fori_loop(0, PAIRS, step, 0, unroll=2)


def attend_back_call(seq, *args, tokens=()):
    rows = (args[5].shape, BF)
    return launch(
        functools.partial(attend_back_kernel, seq), "attend_back", args, [rows, rows, (SLAB, F32), (SLAB, BF)],
        tokens=tokens,
    )


def query_kernel(seq, part_ref, got_ref, count_ref, ids_ref, gq_ref):
    peers = got_ref.shape[0]
    lane = lane_of(ROWS)
    count = count_ref[...]

    def step(pair, carry):
        total = part_ref[pair]
        for peer in range(peers):
            total = total + got_ref[peer, pair].astype(F32)
        grad_cent = (total * SCALE).astype(BF).astype(F32)
        divisor = jnp.where(lane < HDIM, column(count, 2 * pair), column(count, 2 * pair + 1))
        spread = stack_pair(grad_cent / divisor)
        member = member_pair(ids_ref, seq, pair)
        gq_ref[:, pair_lanes(pair)] = dot_tn(member, spread).astype(BF)
        return carry

    lax.fori_loop(0, PAIRS, step, 0, unroll=2)


def query_call(seq, part, got, count, ids, width, tokens=()):
    return launch(
        functools.partial(query_kernel, seq), "query_grad", (part, got, count, ids),
        [((ids.shape[-1], width), BF)], tokens=tokens,
    )[0]


def back_input_kernel(
    seq, gq_ref, gk_ref, gv_ref, x_ref, wq_ref, wk_ref, wv_ref, gain_ref, mid_ref, sel_ref,
    vec_in_ref, *rest,
):
    vec_ref, gx_ref, out_s, sem = rest[-4:]
    vec_ref[...] = vec_in_ref[...]
    middle = mid_ref[seq * MASK_MOST : (seq + 1) * MASK_MOST, :]
    high = middle.astype(BF)
    low = (middle - high.astype(F32)).astype(BF)

    def act(rows):
        grad_query, grad_value = gq_ref[rows, :], gv_ref[rows, :]
        incoming = (
            dot_nt(grad_query, wq_ref[...])
            + dot_nt(gk_ref[rows, :], wk_ref[...])
            + dot_nt(grad_value, wv_ref[...])
        )
        unit, inverse = norm_parts(x_ref[seq, rows, :].astype(F32))
        grad = norm_back(incoming, unit, inverse, vector(gain_ref))
        pick = pick_rows(sel_ref[seq : seq + 1, rows])
        out_s[rows, :] = (grad + (dot_tn(pick, high) + dot_tn(pick, low))).astype(BF)
        vec_ref[V_BQ : V_BQ + 1, :] += jnp.sum(grad_query.astype(F32), axis=0, keepdims=True)
        vec_ref[V_BV : V_BV + 1, :] += jnp.sum(grad_value.astype(F32), axis=0, keepdims=True)
        vec_ref[V_GA : V_GA + 1, :] += jnp.sum(incoming * unit, axis=0, keepdims=True)
        vec_ref[V_SA : V_SA + 1, :] += jnp.sum(incoming, axis=0, keepdims=True)

    row_blocks(gq_ref.shape[0], act)
    copy = pltpu.make_async_copy(out_s, gx_ref.at[seq], sem)
    copy.start()
    copy.wait()


def back_input_call(seq, *args, former, tokens=()):
    args = list(args)
    x, vec = args[3], args[10]
    aliases = {}
    if former is not None:
        aliases = {len(args): 1}
        args.append(Hbm(former))
    vec, grad = launch(
        functools.partial(back_input_kernel, seq), "back_input", args, [(vec.shape, F32)],
        out_hbm=[(x.shape, BF)], tokens=tokens, aliases=aliases,
        scratch=[pltpu.VMEM(x.shape[1:], BF), pltpu.SemaphoreType.DMA],
    )
    return grad, vec


def store_chunks(out_ref, base, product, rank, per_group):
    size = product.shape[0] // per_group
    for index in range(per_group):
        out_ref[base + (index ^ (rank & (per_group - 1)))] = product[
            index * size : (index + 1) * size
        ].astype(BF)


def lanes_at(start, size):
    return pl.ds(pl.multiple_of(start * size, size), size)


def ffn_grad_kernel(ff, width, down, half, stages, here_ref, keep_ref, got_ref, *out_refs):
    rank = rank_from(here_ref, stages) & 15
    rows = ff // 8
    for index, out_ref in enumerate(out_refs):
        group = (2 * half + 1 - index) ^ (rank // 4)
        if down:
            left, right = lanes_at(group, rows), pl.ds(ff // 2, width)
        else:
            left = lanes_at(ff // 2 // rows + (group & 1), rows)
            right = lanes_at(group // 2, width)
        product = dot_tn(keep_ref[:, left], keep_ref[:, right]) + dot_tn(
            got_ref[:, left], got_ref[:, right]
        )
        store_chunks(out_ref, 0, product, rank, 4)


def ffn_grad_call(here, stages, keep, got, ff, width, down, half, tokens=()):
    return launch(
        functools.partial(ffn_grad_kernel, ff, width, down, half, stages),
        "grad_down" if down else "grad_up", (here, keep, got),
        [((4, ff // 32, width), BF)] * 2, tokens=tokens,
    )


def pair_grad_kernel(splits, half, stages, here_ref, *refs):
    out_ref = refs[-1]
    rank = rank_from(here_ref, stages)
    rows = refs[0].shape[1] // 2
    pairs = [(refs[2 * k], refs[2 * k + 1]) for k in range(len(refs) // 2)]

    def step(index, carry):
        group = (2 * half + index) ^ (rank // 8)
        lanes = lanes_at(group & 1, rows)

        def fill(some):
            product = sum(dot_tn(left[:, lanes], right[...]) for left, right in some)
            store_chunks(out_ref, 8 * index, product, rank, 8)

        @pl.when(group < 2)
        def _():
            fill(pairs[:splits])

        @pl.when(group >= 2)
        def _():
            fill(pairs[splits:])

        return carry

    lax.fori_loop(0, 2, step, 0)


def pair_grad_call(here, stages, first, second, half, name, tokens=()):
    args = [array for pair in first + second for array in pair]
    width = args[0].shape[1]
    return launch(
        functools.partial(pair_grad_kernel, len(first), half, stages), name, (here, *args),
        [((16, width // 16, width), BF)], tokens=tokens,
    )[0]


def add_kernel(terms, *refs):
    inputs, outs = refs[:terms], refs[terms:]
    count = outs[0].shape[0]

    def step(index, carry):
        for place, out_ref in enumerate(reversed(outs)):
            total = inputs[0][place * count + index].astype(F32)
            for more in inputs[1:]:
                total = total + more[place * count + index].astype(F32)
            out_ref[index] = total.astype(BF)
        return carry

    lax.fori_loop(0, count, step, 0)


def add_call(args, parts, tokens=()):
    count, size, width = args[0].shape
    return launch(
        functools.partial(add_kernel, len(args)), "add", args,
        [((count // parts, size, width), BF)] * parts, tokens=tokens,
    )


def join_kernel(keep_ref, got_ref, out_ref):
    count = keep_ref.shape[0]
    out_ref[:count] = keep_ref[...]
    out_ref[count:] = got_ref[...]


def join_call(keep, got, tokens=()):
    count, size, width = keep.shape
    return launch(
        join_kernel, "join", (keep, got), [((2 * count, size, width), BF)], tokens=tokens,
    )[0]


def place_kernel(pieces, target, stages, here_ref, *refs):
    sources, refs = refs[: len(pieces)], refs[-target.outputs - 3 :]
    token_ref, outs, stage_s, sems = refs[0], refs[1:-2], refs[-2], refs[-1]
    token_ref[...] = jnp.zeros_like(token_ref)
    rank = rank_from(here_ref, stages)
    size = sources[0].shape[1]
    copies = []
    for index, (piece, source) in enumerate(zip(pieces, sources)):

        def step(inner, carry, source=source, slot=index):
            rows = pl.ds(pl.multiple_of(inner * size, size), size)
            stage_s[slot, rows, :] = source[inner ^ (rank & 3)].astype(F32)
            return carry

        lax.fori_loop(0, 4, step, 0)
        copies.append(target(outs, piece ^ (rank // 4), stage_s.at[index], sems.at[index]))
    for copy in copies:
        copy.wait()


class Copy:
    def __init__(self, choices):
        self.choices = choices
        for chosen, copy in choices:
            if chosen is None:
                copy.start()
            else:
                pl.when(chosen)(copy.start)

    def wait(self):
        self.choices[0][1].wait()


class DownTarget:
    outputs = 1

    def __call__(self, outs, piece, source, sem):
        place = outs[0].at[lanes_at(piece, source.shape[0])]
        return Copy([(None, pltpu.make_async_copy(source, place, sem))])


class UpTarget:
    outputs = 1

    def __call__(self, outs, piece, source, sem):
        rows, width = source.shape
        place = outs[0].at[lanes_at(piece & 1, rows), lanes_at(piece // 2, width)]
        return Copy([(None, pltpu.make_async_copy(source, place, sem))])


class PairTarget:
    outputs = 2

    def __call__(self, outs, piece, source, sem):
        rows = source.shape[0]
        return Copy([
            (
                piece // 4 == matrix,
                pltpu.make_async_copy(source, outs[matrix].at[lanes_at(piece & 3, rows)], sem),
            )
            for matrix in range(2)
        ])


def swap(rows, stage):
    axis, bit = stage
    return lax.ppermute(rows, axis, [(i, i ^ bit) for i in range(lax.axis_size(axis))])


def stage_list(first):
    every = []
    for axis in ("dp", "seq"):
        every += [(axis, 1 << k) for k in range(lax.axis_size(axis).bit_length() - 1)]
    return first + [stage for stage in every if stage not in first]


class Stream:
    def __init__(self, here, stages, target, out_shapes, name):
        self.here, self.stages, self.target = here, stages, target
        self.out_shapes, self.name, self.placed = out_shapes, name, None
        self.pieces = {}

    def begin(self, sent, kept):
        self.kept = kept
        self.got = [swap(piece, self.stages[1]) for piece in sent]

    def begin_core(self, sent, kept):
        self.kept, self.got = kept, swap(sent, self.stages[0])

    def a0(self, tokens):
        first, second, third, fourth = add_call((self.kept, self.got), 4, tokens)
        self.begin((first, second), (third, fourth))
        return first

    def a1(self, tokens):
        total = add_call((self.kept[0], self.got[0]), 1, tokens)[0]
        self.more = swap(total, self.stages[2])
        return total

    def a2(self, tokens):
        send, self.kept = add_call((self.kept[1], self.got[1], self.more), 2, tokens)
        self.got = swap(send, self.stages[3])
        return send

    def a3(self, tokens):
        send, self.kept = add_call((self.kept, self.got), 2, tokens)
        self.got = swap(send, self.stages[4])
        return send

    def a4(self, tokens):
        total = add_call((self.kept, self.got), 1, tokens)[0]
        for stage in self.stages[5:]:
            total = add_call((total, swap(total, stage)), 1)[0]
        self.kept, self.got = total, swap(total, self.stages[4])
        return total

    def j4(self, tokens):
        self.kept = join_call(self.kept, self.got, tokens)
        self.got = swap(self.kept, self.stages[3])
        return self.kept

    def j3(self, tokens):
        piece = join_call(self.kept, self.got, tokens)
        core, s1, s2 = self.stages[:3]
        near = swap(piece, s2)
        self.pieces = {0: piece, 1: near, 2: swap(piece, s1), 3: swap(near, s1)}
        for number in range(4):
            self.pieces[4 + number] = swap(self.pieces[number], core)
        return piece

    def place(self, numbers, tokens):
        sources = [self.pieces[number] for number in numbers]
        _, size, width = sources[0].shape
        args = [self.here] + sources
        aliases = {}
        if self.placed is not None:
            aliases = {len(args) + index: 1 + index for index in range(len(self.placed))}
            args += [Hbm(item) for item in self.placed]
        token, *self.placed = launch(
            functools.partial(place_kernel, numbers, self.target, self.stages), self.name, args,
            [TOKEN], out_hbm=[(shape, F32) for shape in self.out_shapes], tokens=tokens,
            aliases=aliases,
            scratch=[
                pltpu.VMEM((len(numbers), 4 * size, width), F32),
                pltpu.SemaphoreType.DMA((len(numbers),)),
            ],
        )
        return token

    def p0(self, tokens):
        return self.place((0, 4), tokens)

    def p1(self, tokens):
        return self.place((1, 2, 5, 6), tokens)

    def p2(self, tokens):
        return self.place((3, 7), tokens)


def add_rows_kernel(a_ref, b_ref, out_ref):
    out_ref[...] = a_ref[...] + b_ref[...]


def add_rows_call(rows, got, tokens):
    return launch(
        add_rows_kernel, "add_rows", (rows, got), [(rows.shape, F32)], tokens=tokens
    )[0]


def unpack_kernel(vec_ref, *out_refs):
    for start, out_ref in zip((V_BQ, V_BV, V_BO, V_BU, V_BD, V_GA, V_SA, V_GF, V_SF), out_refs):
        count = out_ref.shape[0] // vec_ref.shape[1]
        rows = [vec_ref[start + index : start + index + 1, :] for index in range(count)]
        out_ref[...] = jnp.concatenate(rows, axis=1).reshape(out_ref.shape[0])


def unpack_call(vec, ff):
    width = vec.shape[1]
    outs = shapes(*[((ff if index == 3 else width,), F32) for index in range(9)])
    return pl.pallas_call(
        unpack_kernel,
        in_specs=[VMEM],
        out_specs=[VMEM] * 9,
        out_shape=outs,
        compiler_params=pltpu.CompilerParams(vmem_limit_bytes=4 * 2**20),
        name="unpack",
    )(pltpu.with_memory_space_constraint(vec, pltpu.VMEM))


def from_peers(rows):
    size = lax.axis_size("seq")
    got = [
        lax.ppermute(rows, "seq", [(i, (i + shift) % size) for i in range(size)])
        for shift in range(1, size)
    ]
    return jnp.stack(got)


def shards(
    inputs, cluster_ids, masked, cotangent,
    w_query, w_key, w_value, w_out, w_up, w_down,
    bias_query, bias_value, bias_out, bias_up, bias_down,
    gain_attn, shift_attn, gain_ffn, shift_ffn,
):
    Estimate.now = 5.0
    seqs, tokens, width = inputs.shape
    every = range(seqs)
    ff = w_up.shape[1]
    core, x, y = ("dp", 1), ("dp", 2), ("seq", 1)
    z = ("dp", lax.axis_size("dp") // 4)
    stages_a = stage_list([core, x, y])
    stages_b = stage_list([core, z, y, x])
    stages_c = stage_list([core, y, z, x])
    stages_d = stage_list([core, x, y])
    here = Scalar(jnp.stack([lax.axis_index("dp"), lax.axis_index("seq")]).astype(jnp.int32))
    ids = cluster_ids.transpose(1, 0, 2)

    fetched = [
        Hbm(item)
        for item in (
            inputs, ids, w_query, w_key, w_value, bias_query, bias_value, gain_attn, shift_attn,
            masked,
        )
    ]
    more = [cotangent, w_out, w_up, w_down, bias_out, bias_down, gain_ffn, shift_ffn, bias_up]
    projected, sel = [], None
    for s in every:
        results, fetched, brought, found = project_call(
            s, here, fetched, more if s == seqs - 1 else []
        )
        projected.append(results)
        sel = found if s == 0 else sel
    normed, keys, values, own, message = zip(*projected)
    x_v, ids_v, wq_v, wk_v, wv_v, _, _, gain_v, _, _ = fetched
    cot_v, wo_v, wu_v, wd_v, bo_v, bd_v, gf_v, sf_v, _, up_rows = brought
    got = [from_peers(item) for item in message]
    attended, tokens_in = [], ()
    for s in every:
        attended.append(
            attend_call(own[s], message[s], got[s], keys[s], values[s], tokens=tokens_in)
        )
        tokens_in = (attended[s][1],)
    cent, count, out, lse, send = zip(*attended)
    got = [from_peers(item) for item in send]
    merges = []
    for s in every:
        merges.append(
            merge_call(s, out[s], lse[s], got[s], x_v, cot_v, sel, ids_v, tokens=tokens_in)
        )
        tokens_in = (merges[s][2],)
    ctx, merged, lse_all, ctx_m, x_m, cot_m, ids_m = zip(*merges)
    keep_a, away_a, keep_b, away_b, ctx_m, attn_m, mid_m, vec, own, message = masked_call(
        here, ids_m, ctx_m, x_m, cot_m, wo_v, wu_v, wd_v, bo_v, up_rows, gf_v, sf_v
    )
    got_grad = from_peers(message)
    other_a, other_b = swap(away_a, core), swap(away_b, core)
    weights = (wo_v, wu_v, wd_v, bo_v, up_rows, bd_v, gf_v, sf_v)
    blocks = [(s, start) for s in every for start in range(0, tokens, 256)]
    block_out = None

    def forward(*earlier):
        nonlocal block_out
        if blocks:
            s, start = blocks.pop(0)
            token, block_out = forward_call(s, start, x_v, ctx[s], weights, block_out, earlier)
            return token
        return earlier[0]

    a = Stream(here, stages_a, DownTarget(), [(ff, width)], "place_down")
    b = Stream(here, stages_b, UpTarget(), [(width, ff)], "place_up")
    c = Stream(here, stages_c, PairTarget(), [(width, width)] * 2, "place_out_value")
    d = Stream(here, stages_d, PairTarget(), [(width, width)] * 2, "place_key_query")
    back = {}
    waiting = {}
    grad_input = None

    def ffn_grads(stream, down, half):
        def act(tokens):
            waiting[stream, half] = ffn_grad_call(
                here, stream.stages, keep_a if down else keep_b, other_a if down else other_b,
                ff, width, down, half, tokens,
            )
            if half == 0:
                stream.begin(waiting[stream, 1], waiting[stream, 0])
            return waiting[stream, half][0]

        return act

    def pair_grads(stream, name, half):
        def act(tokens):
            if stream is c:
                first = [(ctx_m, attn_m)]
                second = [(normed[s], back[s][1]) for s in every]
            else:
                first = [(normed[s], back[s][0]) for s in every]
                second = [(normed[s], waiting["query", s]) for s in every]
            result = pair_grad_call(here, stream.stages, first, second, half, name, tokens)
            waiting[stream, half] = result
            if half == 0:
                stream.begin_core(waiting[stream, 1], result)
            return result

        return act

    def attend_back(s):
        def act(tokens):
            back[s] = attend_back_call(
                s, cent[s], lse_all[s], merged[s], own, got_grad, keys[s], values[s],
                tokens=tokens,
            )
            waiting["part", s] = from_peers(back[s][3])
            return back[s][3]

        return act

    def query(s):
        def act(tokens):
            waiting["query", s] = query_call(
                s, back[s][2], waiting["part", s], count[s], ids_v, width, tokens
            )
            return waiting["query", s]

        return act

    def back_input(s):
        def act(tokens):
            nonlocal grad_input, vec
            grad_input, vec = back_input_call(
                s, waiting["query", s], back[s][0], back[s][1], x_v, wq_v, wk_v, wv_v, gain_v, mid_m,
                sel, vec, former=grad_input, tokens=tokens,
            )
            return vec

        return act

    def forward_step(tokens):
        return forward(*tokens)

    def vector_step(stage):
        def act(tokens):
            nonlocal vec
            vec = add_rows_call(vec, waiting["vec"], tokens)
            place = stages_a.index(stage) + 1
            waiting["vec"] = swap(vec, stages_a[place]) if place < len(stages_a) else None
            return vec

        return act

    def vector_first(tokens):
        waiting["vec"] = swap(vec, stages_a[0])
        return tokens[0]

    def all_seqs(make):
        return [make(s) for s in every]

    def streams(*steps):
        return [getattr(stream, step) for stream, step in steps]

    order = [
        (ffn_grads(a, True, 1), 5.0), (ffn_grads(a, True, 0), 5.0), (ffn_grads(b, False, 1), 5.0),
        (ffn_grads(b, False, 0), 5.0), (forward_step, 0.1), (attend_back(0), 5.0),
        *[(step, 0.1) for step in all_seqs(attend_back)[1:]], (a.a1, 1.0),
        (pair_grads(c, "grad_out_value", 1), 5.0), (query(0), 5.0),
        *[(step, 5.0) for step in all_seqs(query)[1:]], (pair_grads(d, "grad_key_query", 1), 17.0),
        (pair_grads(c, "grad_out_value", 0), 5.0), (pair_grads(d, "grad_key_query", 0), 17.0),
        (b.a1, 1.0), (c.a0, 1.0), (a.a2, 1.0), (d.a0, 1.0), (back_input(0), 10.0),
        *[(step, 10.0) for step in all_seqs(back_input)[1:]], (vector_first, 1.0), (b.a2, 1.0),
        (a.a3, 1.0), (vector_step(stages_a[0]), 1.0), (d.a1, 1.0), (c.a1, 2.0), (forward_step, 5.0),
        (b.a3, 1.0), (a.a4, 0.1), (vector_step(stages_a[1]), 1.0), (d.a2, 1.0), (c.a2, 1.0),
        (vector_step(stages_a[2]), 1.0), (forward_step, 5.0), (b.a4, 1.0), (c.a3, 1.0), (a.j4, 1.0),
        (d.a3, 1.0), (vector_step(stages_a[3]), 1.0), (b.j4, 0.1), (c.a4, 5.0), (a.j3, 1.0),
        (d.a4, 1.0), (b.j3, 1.0), *[(forward_step, 5.0)] * (len(blocks) - 3), (c.j4, 1.0), (d.j4, 1.0),
        (b.p0, 5.0), (a.p0, 5.0), (c.j3, 1.0), (a.p1, 5.0), (d.j3, 1.0), (b.p1, 5.0), (c.p0, 8.0),
        (a.p2, 5.0), (c.p1, 8.0),
        *[(step, 1.0) for step in [vector_step(stage) for stage in stages_a[4:]]], (d.p0, 16.0),
        (b.p2, 5.0), (c.p2, 8.0), (d.p1, 16.0), (d.p2, 8.0),
    ]
    last = vec
    for step, Estimate.now in order:
        last = step((last,))
    (grad_w_down,), (grad_w_up,) = a.placed, b.placed
    grad_w_out, grad_w_value = c.placed
    grad_w_key, grad_w_query = d.placed
    return (
        block_out, grad_input,
        grad_w_query, grad_w_key, grad_w_value, grad_w_out, grad_w_up, grad_w_down,
        *unpack_call(vec, ff),
    )


def solution(mesh):
    rows = P("dp", "seq", None)
    return jax.shard_map(
        shards,
        mesh=mesh,
        in_specs=(rows, P("dp", None, "seq"), P("dp", "seq"), rows) + (P(),) * 15,
        out_specs=(rows, rows) + (P(),) * 15,
        check_vma=False,
    )
```
